32 devices in a mesh: dom: 32 (over z, y, x, core).
Axes of the slice: x: 2, y: 2, z: 4, core: 2. Of those that a mesh axis runs over, the one named last changes fastest.
Arguments:
- right_side: float32 [3, 8, 24576], P(None, None, 'dom')
- mass_diag: float32 [24576], P('dom'), may hold values from 0.3 to 3
- precond_blocks: float32 [3, 3, 24576], P(None, None, 'dom'), as said below
- connectivity: int32 [10, 16384], P(None, 'dom'), may hold values from 0 to 1023, as said below
- shape_grads: bfloat16 [4, 3, 10, 16384], P(None, None, None, 'dom'), may hold values from -3 to 3
- quad_weight: float32 [4, 16384], P(None, 'dom'), may hold values from 0.05 to 0.15
- lame_moduli: float32 [2, 16384], P(None, 'dom'), may hold values from 0.2 to 5
- elem_count: int32 [32], P('dom'), may hold values from 64 to 512, as said below
- boundary_ids: int32 [8192], P('dom'), may hold values from 0 to 767, as said below
Outputs:
- solution: float32 [3, 8, 24576], P(None, None, 'dom')
- residual: float32 [3, 8, 24576], P(None, None, 'dom')
The draws below stay inside these ranges and needn't reach their ends.
Inputs may be any that keep to these rules, and one draw needn't show every extreme that they name: `connectivity`: slots below 768 name the partition's own nodes; slot 768 + j names the partition's j-th ghost node. The ten slots of a live element are distinct. Slots of elements beyond the partition's live count are 0. The first elem_count[p] of partition p's 512 element slots are live; some partition is full. `boundary_ids`: each partition's 256 entries are distinct own-node numbers; entry j of ghost block k lists the node that partition p - o_k holds in its ghost slot j. `precond_blocks`: each node's 3x3 block is symmetric positive definite.
All inputs are finite; a program needn't handle non-finite values.
Results may differ from the reference program's by a relative error of at most 0.00055.
Values sent between devices are 32-bit elements; how exact they have to be, the bound alone decides.
No kernel may reach another device: no remote copies, remote signals or barrier semaphores. Data moves between devices by JAX's collectives and lax.ppermute only.
A program may use at most 64 MiB of HBM per device.

```python
import math
import jax
import jax.numpy as jnp
import numpy as np
from jax import lax

NODE_DEV = 768
CASES = 8
ITERS = 2
ELEM_DEV = 512
BND = 256
NODES = 24576
ELEMS = 16384
N_DOM = 32


def element_counts(key):
    sub_key = jax.random.fold_in(key, 11)
    low_count = ELEM_DEV // 8
    high_count = ELEM_DEV // 2 + 1
    counts = jax.random.randint(jax.random.fold_in(sub_key, 1), (N_DOM,), low_count, high_count, dtype=jnp.int32)
    shuffled = jax.random.permutation(jax.random.fold_in(sub_key, 2), N_DOM)
    counts = counts.at[shuffled[0]].set(ELEM_DEV)
    counts = counts.at[shuffled[1]].set(low_count)
    return counts


def draw_elem_count(key, part):
    return element_counts(key)


def draw_connectivity(key, part):
    counts = element_counts(key)
    slot_total = NODE_DEV + BND
    slot_index = jnp.arange(ELEM_DEV, dtype=jnp.int32)[None, :]
    live_limit = counts[:, None]
    base_node = slot_index * (slot_total - 30) // jnp.maximum(live_limit - 1, 1)
    jitter = jax.random.randint(jax.random.fold_in(key, 12), (10, N_DOM, ELEM_DEV), 0, 3, dtype=jnp.int32)
    node_index = jnp.arange(10, dtype=jnp.int32)[:, None, None]
    jitter = jnp.where((node_index == 9) & (slot_index[None] == live_limit[None] - 1), 2, jitter)
    jitter = jnp.where((node_index == 0) & (slot_index[None] == 0), 0, jitter)
    node_links = base_node[None] + 3 * node_index + jitter
    node_links = jnp.where(slot_index[None] < live_limit[None], node_links, 0)
    return node_links.reshape(10, N_DOM * ELEM_DEV).astype(jnp.int32)


def draw_boundary_ids(key, part):

    def one_part(part_index):
        sub_key = jax.random.fold_in(key, part_index)
        inner_ids = jax.random.permutation(jax.random.fold_in(sub_key, 1), NODE_DEV - 2)[:BND - 2] + 1
        chosen_ids = jnp.concatenate([jnp.array([0, NODE_DEV - 1], dtype=jnp.int32), inner_ids.astype(jnp.int32)])
        return chosen_ids[jax.random.permutation(jax.random.fold_in(sub_key, 2), BND)]
    return jax.vmap(one_part)(jnp.arange(N_DOM, dtype=jnp.int32)).reshape(N_DOM * BND)


def draw_precond_blocks(key, part):
    diagonal = jnp.exp(jnp.log(0.3) + jnp.log(10.0) * jax.random.uniform(jax.random.fold_in(key, 1), (3, NODES), dtype=jnp.float32))
    coupling = 0.3 * jax.random.uniform(jax.random.fold_in(key, 2), (3, NODES), dtype=jnp.float32, minval=-1.0, maxval=1.0)
    root_diag = jnp.sqrt(diagonal)
    pair_xy = coupling[0] * root_diag[0] * root_diag[1]
    pair_xz = coupling[1] * root_diag[0] * root_diag[2]
    pair_yz = coupling[2] * root_diag[1] * root_diag[2]
    first_row = jnp.stack([diagonal[0], pair_xy, pair_xz])
    second_row = jnp.stack([pair_xy, diagonal[1], pair_yz])
    third_row = jnp.stack([pair_xz, pair_yz, diagonal[2]])
    return jnp.stack([first_row, second_row, third_row])


def draw_right_side(key, part):
    node_index = jnp.arange(NODES, dtype=jnp.int32)
    ramp_frac = (node_index // NODE_DEV).astype(jnp.float32) / max(N_DOM - 1, 1)
    node_scale = jnp.exp(jnp.log(10.0) * jax.random.uniform(jax.random.fold_in(key, 1), (NODES,), dtype=jnp.float32))
    case_scale = jnp.exp(jnp.log(10.0) * jax.random.uniform(jax.random.fold_in(key, 2), (CASES,), dtype=jnp.float32))
    ramp_scale = jnp.exp(jnp.log(3.0) * ramp_frac)
    fluctuation = jnp.clip(jax.random.normal(jax.random.fold_in(key, 3), (3, CASES, NODES), dtype=jnp.float32), -4.0, 4.0)
    return 0.05 * fluctuation * (node_scale * ramp_scale)[None, None, :] * case_scale[None, :, None]


def shard_levels(rng, extent, cuts, low, largest):
    loudness, own = 1.0, jax.random.fold_in(rng, 6)
    for position, shards_of in cuts:
        heights = jnp.exp(jax.random.uniform(jax.random.fold_in(own, position), (shards_of,), jnp.float32, low / len(cuts), largest / len(cuts)))
        loudness = loudness * jnp.repeat(heights, extent[position] // shards_of).reshape([-1 if axis == position else 1 for axis in range(len(extent))])
    return loudness


def centred(rng, shape, spread, limit, shards=(), kind=jnp.bfloat16):
    level = shard_levels(rng, shape, shards, -0.22, 0.18) if shards else 1.0
    values = jax.random.normal(rng, shape, jnp.float32) * spread * level
    return jnp.minimum(jnp.maximum(values, -limit), limit).astype(kind)


def setup_inputs(seed: int = 0) -> dict:
    key_list = jax.random.split(jax.random.key(seed), 10)
    return {
        "right_side": draw_right_side(jax.random.fold_in(key_list[9], 71), 0),
        "mass_diag": jnp.clip(jnp.exp(math.log(3.0) - 2.3025851 * jax.random.uniform(key_list[1], (NODES,), jnp.float32) ** shard_levels(key_list[1], (NODES,), ((0, 32),), -0.2, 0.2)), 0.3, 3.0),
        "precond_blocks": draw_precond_blocks(jax.random.fold_in(key_list[9], 71), 0),
        "connectivity": draw_connectivity(jax.random.fold_in(key_list[9], 71), 0),
        "shape_grads": centred(key_list[4], (4, 3, 10, ELEMS), 0.5, 3.0, ((3, 32),)),
        "quad_weight": jnp.clip(0.05 + 0.10000001 * jax.random.uniform(key_list[5], (4, ELEMS), jnp.float32) ** shard_levels(key_list[5], (4, ELEMS), ((1, 32),), -0.2, 0.2), 0.05, 0.15),
        "lame_moduli": jnp.clip(jnp.exp(math.log(5.0) - 3.218876 * jax.random.uniform(key_list[6], (2, ELEMS), jnp.float32) ** shard_levels(key_list[6], (2, ELEMS), ((1, 32),), -0.2, 0.2)), 0.2, 5.0),
        "elem_count": draw_elem_count(jax.random.fold_in(key_list[9], 71), 0),
        "boundary_ids": draw_boundary_ids(jax.random.fold_in(key_list[9], 71), 0),
    }


NEIGHBOUR_SHIFTS = (1, -1, 4, -4, 16, -16)
NEIGHBOUR_SHARES = (4, 4, 3, 3, 1, 1)


def ghost_offsets(ghost_count):
    share_unit = ghost_count // 16
    pieces = [np.full(share * share_unit, offset, np.int32) for offset, share in zip(NEIGHBOUR_SHIFTS, NEIGHBOUR_SHARES)]
    return np.concatenate(pieces)


def element_forces(nodal_values, shape_grads, quad_weight, lame_moduli):
    shape_float = shape_grads.astype(jnp.float32)
    gradient = nodal_values[None, :, None, :, 0, :] * shape_float[:, None, :, None, 0, :]
    for node_index in range(1, 10):
        gradient = gradient + nodal_values[None, :, None, :, node_index, :] * shape_float[:, None, :, None, node_index, :]
    dilation = gradient[:, 0, 0] + gradient[:, 1, 1] + gradient[:, 2, 2]
    identity = jnp.eye(3, dtype=jnp.float32)
    stress = lame_moduli[1] * (gradient + jnp.swapaxes(gradient, 1, 2))
    stress = stress + identity[None, :, :, None, None] * (lame_moduli[0] * dilation)[:, None, None, :, :]
    stress = stress * quad_weight[:, None, None, None, :]
    forces = shape_float[0, 0][None, None, :, :] * stress[0, :, 0][:, :, None, :]
    for quad_point in range(4):
        for deriv_index in range(3):
            if quad_point + deriv_index > 0:
                forces = forces + shape_float[quad_point, deriv_index][None, None, :, :] * stress[quad_point, :, deriv_index][:, :, None, :]
    return forces


def precondition(blocks, vector):
    case_count = vector.shape[0] // 3
    components = vector.reshape(3, case_count, vector.shape[1])
    result = blocks[:, 0][:, None, :] * components[0][None] + blocks[:, 1][:, None, :] * components[1][None] + blocks[:, 2][:, None, :] * components[2][None]
    return result.reshape(vector.shape)


def per_row(values):
    return jnp.tile(values, 3)[:, None]


def reference(right_side, mass_diag, precond_blocks, connectivity, shape_grads, quad_weight, lame_moduli, elem_count, boundary_ids):
    case_count = right_side.shape[1]
    row_count = 3 * case_count
    total_nodes = right_side.shape[2]
    ghost_shift = jnp.asarray(ghost_offsets(BND), dtype=jnp.int32)
    ghost_index = jnp.arange(BND, dtype=jnp.int32)

    def inner_product(left, right):
        return jnp.sum((left * right).reshape(3, case_count, total_nodes), axis=(0, 2))

    def operate(vector):
        padded = jnp.concatenate([vector, jnp.zeros((row_count, 1), jnp.float32)], axis=1)

        def visit_part(accumulated, partition):
            first_slot = partition * ELEM_DEV
            node_links = lax.dynamic_slice_in_dim(connectivity, first_slot, ELEM_DEV, 1)
            owner = (partition + ghost_shift).astype(jnp.int32)
            valid = (owner >= 0) & (owner < N_DOM)
            safe_owner = jnp.clip(owner, 0, N_DOM - 1).astype(jnp.int32)
            far_ids = jnp.take(boundary_ids, (safe_owner * BND + ghost_index).astype(jnp.int32))
            far_global = jnp.where(valid, safe_owner * NODE_DEV + far_ids, total_nodes).astype(jnp.int32)
            ghost_slot = jnp.clip(node_links - NODE_DEV, 0, BND - 1).astype(jnp.int32)
            global_links = jnp.where(node_links < NODE_DEV, partition * NODE_DEV + node_links, far_global[ghost_slot]).astype(jnp.int32)
            nodal_values = jnp.take(padded, global_links, axis=1).reshape(3, case_count, 10, ELEM_DEV)
            grad_block = lax.dynamic_slice_in_dim(shape_grads, first_slot, ELEM_DEV, 3)
            weight_block = lax.dynamic_slice_in_dim(quad_weight, first_slot, ELEM_DEV, 1)
            moduli_block = lax.dynamic_slice_in_dim(lame_moduli, first_slot, ELEM_DEV, 1)
            forces = element_forces(nodal_values, grad_block, weight_block, moduli_block)
            is_live = lax.iota(jnp.int32, ELEM_DEV) < elem_count[partition]
            forces = jnp.where(is_live, forces, 0.0).reshape(row_count, 10, ELEM_DEV)
            return accumulated.at[:, global_links].add(forces), None

        accumulated, unused = lax.scan(visit_part, jnp.zeros((row_count, total_nodes + 1), jnp.float32), jnp.arange(N_DOM, dtype=jnp.int32))
        return accumulated[:, :total_nodes] + mass_diag[None, :] * vector

    residual = right_side.reshape(row_count, total_nodes)
    solution = jnp.zeros((row_count, total_nodes), jnp.float32)
    search = precondition(precond_blocks, residual)
    direction = search
    energy = inner_product(residual, search)
    for iteration in range(ITERS):
        applied = operate(direction)
        step_size = energy / inner_product(direction, applied)
        solution = solution + per_row(step_size) * direction
        residual = residual - per_row(step_size) * applied
        search = precondition(precond_blocks, residual)
        fresh_energy = inner_product(residual, search)
        direction = search + per_row(fresh_energy / energy) * direction
        energy = fresh_energy
    return (solution.reshape(3, case_count, total_nodes), residual.reshape(3, case_count, total_nodes))
```

```python
import functools

import jax
import jax.numpy as jnp
from jax import lax
from jax.experimental import pallas as pl
from jax.experimental.pallas import tpu as pltpu
from jax.sharding import PartitionSpec as P

F32 = jnp.float32
BF16 = jnp.bfloat16
AXIS = "dom"
CASES = 8
LANES = 128
DISTANCES = (1, 4, 16)
SHARES = {1: 4, 4: 3, 16: 1}


def matchings(devices):
    listed = []
    for distance in DISTANCES:
        for parity in (0, 1):
            pairs = []
            for i in range(devices - distance):
                if (i // distance) % 2 == parity:
                    pairs += [(i, i + distance), (i + distance, i)]
            if pairs:
                listed.append((distance, parity, pairs))
    return listed


def take_lanes(chunks, index):
    lane = index & (LANES - 1)
    which = index >> 7
    rows = len(chunks)
    picked = [None] * rows
    for c in range(len(chunks[0])):
        mask = which == c
        for r in range(rows):
            moved = jnp.take_along_axis(chunks[r][c], lane, axis=1)
            picked[r] = moved if c == 0 else jnp.where(mask, moved, picked[r])
    return picked


def row8(ref, row, start=0, width=LANES):
    return jnp.broadcast_to(ref[row : row + 1, start : start + width], (8, width))


def split_lanes(value):
    return [value[:, c * LANES : (c + 1) * LANES] for c in range(value.shape[1] // LANES)]


def in_two(value):
    head = value.astype(BF16)
    tail = (value - head.astype(F32)).astype(BF16)
    return head, tail


def pick_sides(p, distance, even, odd):
    first = lax.rem(lax.div(p, distance), 2) == 0
    zero = jnp.zeros_like(even)
    odd = zero if odd is None else odd
    return jnp.where(first, even, odd), jnp.where(first, odd, even)


def ghost_bounds(unit):
    return 4 * unit, 8 * unit, 11 * unit, 14 * unit, 15 * unit, 16 * unit


def joined(p, received, rows, lane, opposite):
    sides = {}
    for distance in DISTANCES:
        even = received.get((distance, 0))
        odd = received.get((distance, 1))
        even = even[rows, :]
        odd = None if odd is None else odd[rows, :]
        plus, minus = pick_sides(p, distance, even, odd)
        sides[distance] = (minus, plus) if opposite else (plus, minus)
    tile0 = jnp.where(lane < 64, sides[1][0], sides[1][1])
    tile1 = jnp.where(
        lane < 48,
        sides[4][0],
        jnp.where(lane < 96, sides[4][1], jnp.where(lane < 112, sides[16][0], sides[16][1])),
    )
    return [tile0, tile1]


def spread(tiles, bids_ref, own):
    width = bids_ref.shape[1]
    stacked = jnp.concatenate([jnp.concatenate(t, axis=1) for t in tiles], axis=0)
    head, tail = in_two(stacked)
    left = jnp.concatenate([head, tail], axis=0)
    nodes = lax.broadcasted_iota(jnp.int32, (own, width), 0)
    right = jnp.where(nodes == bids_ref[0:1, :], 1.0, 0.0).astype(BF16)
    out = lax.dot_general(left, right, (((1,), (1,)), ((), ())), preferred_element_type=F32)
    return out[:24] + out[24:]


def boundary_values(chunks, bids_ref):
    return [take_lanes(chunks, row8(bids_ref, 0, t * LANES)) for t in range(2)]


def operate(chunks, conn_ref, grads, qw_ref, lame_ref, live, left_ref, right_ref):
    elems = conn_ref.shape[1]
    lows = lax.broadcasted_iota(jnp.int32, (256, LANES), 0)
    lane = lax.broadcasted_iota(jnp.int32, (1, LANES), 1)

    def block(e):
        e0 = e * LANES
        is_live = (e0 + lane) < live
        nodal = []
        for a in range(10):
            index = conn_ref[a : a + 1, e0 : e0 + LANES]
            nodal.append(take_lanes(chunks, jnp.broadcast_to(index, (8, LANES))))
            hot = jnp.where(lows == (index & 255), 1.0, 0.0).astype(BF16)
            right_ref[:, a * elems + e0 : a * elems + e0 + LANES] = hot

        forces = [[None] * 10 for _ in range(3)]
        lam = lame_ref[0:1, e0 : e0 + LANES]
        mu = lame_ref[1:2, e0 : e0 + LANES]
        for q in range(4):
            grad = [[None] * 3 for _ in range(3)]
            for k in range(3):
                for a in range(10):
                    g = grads(q, k, a, e0)
                    for i in range(3):
                        term = nodal[a][i] * g
                        grad[i][k] = term if a == 0 else grad[i][k] + term
            w = qw_ref[q : q + 1, e0 : e0 + LANES]
            wmu = jnp.broadcast_to(w * mu, (8, LANES))
            wlam = jnp.broadcast_to(w * lam, (8, LANES))
            swell = wlam * (grad[0][0] + grad[1][1] + grad[2][2])
            stress = [[None] * 3 for _ in range(3)]
            for i in range(3):
                stress[i][i] = wmu * (grad[i][i] + grad[i][i]) + swell
                for k in range(i):
                    stress[i][k] = wmu * (grad[i][k] + grad[k][i])
                    stress[k][i] = stress[i][k]
            for k in range(3):
                for a in range(10):
                    g = grads(q, k, a, e0)
                    for i in range(3):
                        term = stress[i][k] * g
                        forces[i][a] = term if q + k == 0 else forces[i][a] + term
        for a in range(10):
            index = conn_ref[a : a + 1, e0 : e0 + LANES]
            high = jnp.broadcast_to(jnp.where(is_live, index >> 8, -1), (8, LANES))
            parts = [in_two(forces[i][a]) for i in range(3)]
            for h in range(4):
                mask = high == h
                kept = [jnp.where(mask, parts[i][s].astype(F32), 0.0) for s in range(2) for i in range(3)]
                left_ref[h * 48 : h * 48 + 48, a * elems + e0 : a * elems + e0 + LANES] = jnp.concatenate(
                    kept, axis=0
                ).astype(BF16)

    for e in range(elems // LANES):
        block(e)
    out = lax.dot_general(
        left_ref[...], right_ref[...], (((1,), (1,)), ((), ())), preferred_element_type=F32
    )
    return [
        [
            (out[h * 48 + i * 8 : h * 48 + i * 8 + 8] + out[h * 48 + 24 + i * 8 : h * 48 + 32 + i * 8])[
                :, c * LANES : (c + 1) * LANES
            ]
            for h in range(4)
            for c in range(2)
        ]
        for i in range(3)
    ]


def widen_grads(grads_ref, wide_ref):
    for q in range(4):
        for k in range(3):
            wide_ref[q * 3 + k, 0:10, :] = grads_ref[q, k].astype(F32)

    def grads(q, k, a, e0):
        return jnp.broadcast_to(wide_ref[q * 3 + k, a : a + 1, e0 : e0 + LANES], (8, LANES))

    return grads


def lane_sum(values):
    total = values[0]
    for value in values[1:]:
        total = total + value
    return jnp.sum(total, axis=1, keepdims=True)


def begin_kernel(rhs_ref, prec_ref, bids_ref, d_ref, t0_ref, t1_ref, blocks_ref):
    own = rhs_ref.shape[1]
    blocks_ref[...] = jnp.zeros_like(blocks_ref)
    for i in range(3):
        d_ref[8 * i : 8 * i + 8, :] = (
            prec_ref[i, 0:1, :] * rhs_ref[0:8, :]
            + prec_ref[i, 1:2, :] * rhs_ref[8:16, :]
            + prec_ref[i, 2:3, :] * rhs_ref[16:24, :]
        )
        for j in range(3):
            blocks_ref[3 * i + j : 3 * i + j + 1, :] = prec_ref[i, j : j + 1, :]
    rows = [split_lanes(d_ref[8 * i : 8 * i + 8, :]) for i in range(3)]
    rows += [split_lanes(blocks_ref[8 * i : 8 * i + 8, :]) for i in range(2)]
    picked = boundary_values(rows, bids_ref)
    for t, ref in enumerate((t0_ref, t1_ref)):
        for r in range(5):
            ref[8 * r : 8 * r + 8, :] = picked[t][r]


def first_kernel(
    keys,
    p_ref,
    count_ref,
    d_ref,
    bids_ref,
    conn_ref,
    grads_ref,
    qw_ref,
    lame_ref,
    mass_ref,
    *rest,
):
    received = dict(zip(keys, rest[: len(keys)]))
    q_ref, s0_ref, s1_ref, gprec_ref, dot_ref, wide_ref, left_ref, right_ref = rest[len(keys) :]
    p = p_ref[0]
    lane = lax.broadcasted_iota(jnp.int32, (8, LANES), 1)
    chunks = []
    for i in range(3):
        ghost = joined(p, received, slice(8 * i, 8 * i + 8), lane, False)
        chunks.append(split_lanes(d_ref[8 * i : 8 * i + 8, :]) + ghost)
    for r in range(2):
        tiles = joined(p, received, slice(24 + 8 * r, 32 + 8 * r), lane, False)
        for t in range(2):
            gprec_ref[8 * r : 8 * r + 8, t * LANES : (t + 1) * LANES] = tiles[t]
    grads = widen_grads(grads_ref, wide_ref)
    acc = operate(chunks, conn_ref, grads, qw_ref, lame_ref, count_ref[0], left_ref, right_ref)
    own_chunks = d_ref.shape[1] // LANES
    dots = []
    partial = []
    for i in range(3):
        partial.append([])
        for c in range(own_chunks):
            value = acc[i][c] + mass_ref[0:1, c * LANES : (c + 1) * LANES] * chunks[i][c]
            q_ref[8 * i : 8 * i + 8, c * LANES : (c + 1) * LANES] = value
            partial[i].append(value)
            dots.append(value * chunks[i][c])
        for c in range(2):
            dots.append(acc[i][own_chunks + c] * chunks[i][own_chunks + c])
    picked = boundary_values(partial, bids_ref)
    for t, ref in enumerate((s0_ref, s1_ref)):
        for i in range(3):
            ref[8 * i : 8 * i + 8, :] = acc[i][own_chunks + t]
            ref[24 + 8 * i : 32 + 8 * i, :] = picked[t][i]
    dot_ref[...] = jnp.broadcast_to(lane_sum(dots), (8, LANES))


def second_kernel(
    keys,
    p_ref,
    count_ref,
    rhs_ref,
    d_ref,
    qpart_ref,
    s0_ref,
    s1_ref,
    prec_ref,
    gprec_ref,
    dot_ref,
    bids_ref,
    conn_ref,
    grads_ref,
    qw_ref,
    lame_ref,
    mass_ref,
    *rest,
):
    received = dict(zip(keys, rest[: len(keys)]))
    q_ref, s_ref, w_ref, out_ref, wide_ref, left_ref, right_ref = rest[len(keys) :]
    p = p_ref[0]
    devices = out_ref.shape[0]
    own = d_ref.shape[1]
    own_chunks = own // LANES
    lane = lax.broadcasted_iota(jnp.int32, (8, LANES), 1)
    back = [joined(p, received, slice(8 * i, 8 * i + 8), lane, True) for i in range(3)]
    q_ref[...] = qpart_ref[...] + spread(back, bids_ref, own)
    largest = jnp.maximum(jnp.max(jnp.abs(prec_ref[...])), jnp.max(jnp.abs(gprec_ref[...])))
    inverse = 1.0 / largest
    ghost_q = []
    for i in range(3):
        tiles = joined(p, received, slice(24 + 8 * i, 32 + 8 * i), lane, False)
        ghost_q.append([s0_ref[8 * i : 8 * i + 8, :] + tiles[0], s1_ref[8 * i : 8 * i + 8, :] + tiles[1]])
    chunks = []
    for i in range(3):
        value = (
            (prec_ref[i, 0:1, :] * inverse) * q_ref[0:8, :]
            + (prec_ref[i, 1:2, :] * inverse) * q_ref[8:16, :]
            + (prec_ref[i, 2:3, :] * inverse) * q_ref[16:24, :]
        )
        s_ref[8 * i : 8 * i + 8, :] = value
        chunks.append(split_lanes(value))
        for t in range(2):
            total = None
            for j in range(3):
                term = (gprec_ref[3 * i + j : 3 * i + j + 1, t * LANES : (t + 1) * LANES] * inverse) * ghost_q[j][t]
                total = term if j == 0 else total + term
            chunks[i].append(total)
    grads = widen_grads(grads_ref, wide_ref)
    acc = operate(chunks, conn_ref, grads, qw_ref, lame_ref, count_ref[0], left_ref, right_ref)
    start = []
    cross = []
    square = []
    for i in range(3):
        for c in range(own_chunks):
            here = slice(8 * i, 8 * i + 8), slice(c * LANES, (c + 1) * LANES)
            value = acc[i][c] + mass_ref[0:1, here[1]] * chunks[i][c]
            w_ref[here] = value
            square.append(value * chunks[i][c])
            cross.append(q_ref[here] * chunks[i][c])
            start.append(rhs_ref[here] * d_ref[here])
        for t in range(2):
            square.append(acc[i][own_chunks + t] * chunks[i][own_chunks + t])
    scalars = [lane_sum(start), dot_ref[:, 0:1], lane_sum(cross), lane_sum(square)]
    scalars.append(jnp.broadcast_to(jnp.reshape(largest, (1, 1)), (8, 1)))
    tail = jnp.zeros((8, LANES), F32)
    for k, value in enumerate(scalars):
        tail = jnp.where(lane == 64 + k, value, tail)

    def clear(j, unused):
        out_ref[j, 0:8, :] = jnp.zeros((8, LANES), F32)
        out_ref[j, 8:16, :] = tail
        return unused

    lax.fori_loop(0, devices, clear, 0)
    for distance, shift_plus, shift_minus, tile in WINDOWS:
        for sign, shift in ((1, shift_plus), (-1, shift_minus)):
            moved = [acc[i][own_chunks + tile] for i in range(3)]
            if shift:
                moved = [pltpu.roll(m, LANES - shift, 1) for m in moved]
            target = p + sign * distance

            @pl.when((target >= 0) & (target < devices))
            def _():
                out_ref[target, 0:8, :] = jnp.where(lane < 64, moved[0], pltpu.roll(moved[1], 64, 1))
                out_ref[target, 8:16, :] = jnp.where(lane < 64, moved[2], tail)


WINDOWS = ((1, 0, 64, 0), (4, 0, 48, 1), (16, 96, 112, 1))
WIDTHS = {1: 64, 4: 48, 16: 16}


def final_kernel(p_ref, in_ref, rhs_ref, d_ref, q_ref, s_ref, wpart_ref, bids_ref, x_ref, r_ref):
    p = p_ref[0]
    devices = in_ref.shape[0]
    own = rhs_ref.shape[1]
    lane = lax.broadcasted_iota(jnp.int32, (8, LANES), 1)
    mine = in_ref[p, 8:16, 68:69]
    inv_mine = 1.0 / mine

    def add_up(j, sums):
        values = in_ref[j, 8:16, 64:68]
        ratio = in_ref[j, 8:16, 68:69] * inv_mine
        column = lax.broadcasted_iota(jnp.int32, (8, 4), 1)
        factor = jnp.where(column < 2, 1.0, jnp.where(column == 2, ratio, ratio * ratio))
        return sums + values * factor

    sums = lax.fori_loop(0, devices, add_up, jnp.zeros((8, 4), F32))
    e0, d0, cross, square = (sums[:, k : k + 1] for k in range(4))
    step = e0 / d0
    scaled = step * mine
    fresh = scaled * (step * cross) - e0
    beta = fresh / e0
    more = 1.0 + beta
    bend = more * more * d0 - 2.0 * more * (scaled * cross) + scaled * (scaled * square)
    step1 = fresh / bend

    zero = jnp.zeros((8, LANES), F32)
    back = [[zero, zero] for _ in range(3)]
    for distance, shift_plus, shift_minus, tile in WINDOWS:
        for sign, shift in ((1, shift_plus), (-1, shift_minus)):
            source = p - sign * distance
            valid = (source >= 0) & (source < devices)
            source = jnp.clip(source, 0, devices - 1)
            ratio = jnp.where(valid, in_ref[source, 8:16, 68:69] * inv_mine, 0.0)
            pair = in_ref[source, 0:8, :]
            last = in_ref[source, 8:16, :]
            blocks = [pair, pltpu.roll(pair, 64, 1), last]
            inside = (lane >= shift) & (lane < shift + WIDTHS[distance])
            for i in range(3):
                moved = blocks[i] if shift == 0 else pltpu.roll(blocks[i], shift, 1)
                back[i][tile] = jnp.where(inside & valid, moved * ratio, back[i][tile])
    w = wpart_ref[...] + spread(back, bids_ref, own)
    for i in range(3):
        here = slice(8 * i, 8 * i + 8)
        d = d_ref[here, :]
        q = q_ref[here, :]
        x_ref[here, :] = step * d + step1 * (more * d - scaled * s_ref[here, :])
        r_ref[here, :] = rhs_ref[here, :] - step * q - step1 * (more * q - scaled * w[here])


def local(
    devices,
    right_side,
    mass_diag,
    precond_blocks,
    connectivity,
    shape_grads,
    quad_weight,
    lame_moduli,
    elem_count,
    boundary_ids,
):
    own = right_side.shape[2]
    elems = connectivity.shape[1]
    p = lax.axis_index(AXIS).astype(jnp.int32).reshape(1)
    rhs = right_side.reshape(24, own)
    mass = mass_diag.reshape(1, own)
    bids = boundary_ids.reshape(1, boundary_ids.shape[0])
    vmem = pl.BlockSpec(memory_space=pltpu.VMEM)
    smem = pl.BlockSpec(memory_space=pltpu.SMEM)
    moves = matchings(devices)
    keys = [(distance, parity) for distance, parity, _ in moves]

    def shape(*dims):
        return jax.ShapeDtypeStruct(dims, F32)

    def call(kernel, out_shape, in_specs, scratch=()):
        return pl.pallas_call(
            kernel,
            out_shape=out_shape,
            in_specs=in_specs,
            out_specs=[vmem] * len(out_shape),
            scratch_shapes=list(scratch),
            compiler_params=pltpu.CompilerParams(vmem_limit_bytes=32 << 20),
        )

    def exchange(tile0, tile1):
        return [
            lax.ppermute(tile0 if distance == 1 else tile1, AXIS, pairs) for distance, _, pairs in moves
        ]

    work = (
        pltpu.VMEM((12, 16, elems), F32),
        pltpu.VMEM((192, 10 * elems), BF16),
        pltpu.VMEM((256, 10 * elems), BF16),
    )
    d, t0, t1 = call(
        begin_kernel,
        [shape(24, own), shape(40, LANES), shape(40, LANES)],
        [vmem] * 3,
        [pltpu.VMEM((16, own), F32)],
    )(rhs, precond_blocks, bids)
    got = exchange(t0, t1)
    mesh_args = (bids, connectivity, shape_grads, quad_weight, lame_moduli, mass)
    qpart, s0, s1, gprec, dot = call(
        functools.partial(first_kernel, keys),
        [shape(24, own), shape(48, LANES), shape(48, LANES), shape(16, 2 * LANES), shape(8, LANES)],
        [smem, smem] + [vmem] * (7 + len(keys)),
        work,
    )(p, elem_count, d, *mesh_args, *got)
    got = exchange(s0, s1)
    q, s, wpart, message = call(
        functools.partial(second_kernel, keys),
        [shape(24, own), shape(24, own), shape(24, own), shape(devices, 16, LANES)],
        [smem, smem] + [vmem] * (14 + len(keys)),
        work,
    )(p, elem_count, rhs, d, qpart, s0, s1, precond_blocks, gprec, dot, *mesh_args, *got)
    message = lax.all_to_all(message, AXIS, 0, 0, tiled=True)
    x, r = call(final_kernel, [shape(24, own), shape(24, own)], [smem] + [vmem] * 7)(
        p, message, rhs, d, q, s, wpart, bids
    )
    return x.reshape(3, CASES, own), r.reshape(3, CASES, own)


def solution(mesh):
    return jax.shard_map(
        functools.partial(local, mesh.shape[AXIS]),
        mesh=mesh,
        in_specs=(
            P(None, None, AXIS),
            P(AXIS),
            P(None, None, AXIS),
            P(None, AXIS),
            P(None, None, None, AXIS),
            P(None, AXIS),
            P(None, AXIS),
            P(AXIS),
            P(AXIS),
        ),
        out_specs=(P(None, None, AXIS), P(None, None, AXIS)),
        check_vma=False,
    )
```

```python
import functools

import jax
import jax.numpy as jnp
from jax import lax
from jax.experimental import pallas as pl
from jax.experimental.pallas import tpu as pltpu
from jax.sharding import PartitionSpec as P

F32 = jnp.float32
BF16 = jnp.bfloat16
AXIS = "dom"
CASES = 8
LANES = 128
DISTANCES = (1, 4, 16)


def routes(devices):
    listed = {}
    for distance in DISTANCES:
        for parity in (0, 1):
            route = {}
            for i in range(devices - distance):
                if (i // distance) % 2 == parity:
                    route[i], route[i + distance] = i + distance, i
            if route:
                for i in range(devices):
                    route.setdefault(i, i ^ 1)
                listed[distance, parity] = route
    last = devices - 1
    listed[1, 1].update({0: 1, 1: 2, 2: 0, last: last - 1, last - 1: last - 2, last - 2: last})
    listed[4, 1].update({2: 1, 1: 0, 0: 3, 3: 2})
    listed[4, 1].update({last - 2: last - 1, last - 1: last, last: last - 3, last - 3: last - 2})
    for route in listed.values():
        assert sorted(route.values()) == list(range(devices))
    return listed


def take_lanes(chunks, index):
    lane = index & (LANES - 1)
    which = index >> 7
    rows = len(chunks)
    picked = [None] * rows
    for c in range(len(chunks[0])):
        mask = which == c
        for r in range(rows):
            moved = jnp.take_along_axis(chunks[r][c], lane, axis=1)
            picked[r] = moved if c == 0 else jnp.where(mask, moved, picked[r])
    return picked


def row8(ref, row, start=0, width=LANES):
    return jnp.broadcast_to(ref[row : row + 1, start : start + width], (8, width))


def split_lanes(value):
    return [value[:, c * LANES : (c + 1) * LANES] for c in range(value.shape[1] // LANES)]


def in_two(value):
    head = value.astype(BF16)
    tail = (value - head.astype(F32)).astype(BF16)
    return head, tail


def joined(p, devices, received, rows, lane, opposite):
    sides = {}
    detour = (p == 1) | (p == devices - 2)
    for distance in DISTANCES:
        even = received[distance, 0][rows, :]
        first = lax.rem(lax.div(p, distance), 2) == 0
        if (distance, 1) in received:
            odd = received[distance, 1][rows, :]
            if distance == 1:
                odd = jnp.where(detour, received[4, 1][rows, :], odd)
        else:
            odd = jnp.zeros_like(even)
        plus = jnp.where(p + distance < devices, jnp.where(first, even, odd), 0.0)
        minus = jnp.where(p - distance >= 0, jnp.where(first, odd, even), 0.0)
        sides[distance] = (minus, plus) if opposite else (plus, minus)
    tile0 = jnp.where(lane < 64, sides[1][0], sides[1][1])
    tile1 = jnp.where(
        lane < 48,
        sides[4][0],
        jnp.where(lane < 96, sides[4][1], jnp.where(lane < 112, sides[16][0], sides[16][1])),
    )
    return [tile0, tile1]


def send_mixed(p, devices, tile0, tile1):
    return jnp.where((p == 2) | (p == devices - 3), tile0, tile1)


def spread(tiles, spot_ref):
    stacked = jnp.concatenate([jnp.concatenate(t, axis=1) for t in tiles], axis=0)
    head, tail = in_two(stacked)
    left = jnp.concatenate([head, tail], axis=0)
    out = lax.dot_general(left, spot_ref[...], (((1,), (1,)), ((), ())), preferred_element_type=F32)
    return out[:24] + out[24:]


def boundary_values(chunks, bids_ref):
    return [take_lanes(chunks, row8(bids_ref, 0, t * LANES)) for t in range(2)]


def operate(chunks, conn_ref, high_ref, wide_ref, qw_ref, lame_ref, hot_ref, left_ref):
    elems = conn_ref.shape[1]

    def wide(k, a, q, e0):
        return jnp.broadcast_to(wide_ref[k * 10 + a, q : q + 1, e0 : e0 + LANES], (8, LANES))

    for e0 in range(0, elems, LANES):
        nodal = [take_lanes(chunks, row8(conn_ref, a, e0)) for a in range(10)]
        forces = [[None] * 10 for _ in range(3)]
        lam = lame_ref[0:1, e0 : e0 + LANES]
        mu = lame_ref[1:2, e0 : e0 + LANES]
        for q in range(4):
            grad = [[None] * 3 for _ in range(3)]
            for k in range(3):
                for a in range(10):
                    g = wide(k, a, q, e0)
                    for i in range(3):
                        term = nodal[a][i] * g
                        grad[i][k] = term if a == 0 else grad[i][k] + term
            w = qw_ref[q : q + 1, e0 : e0 + LANES]
            wmu = jnp.broadcast_to(w * mu, (8, LANES))
            wlam = jnp.broadcast_to(w * lam, (8, LANES))
            swell = wlam * (grad[0][0] + grad[1][1] + grad[2][2])
            stress = [[None] * 3 for _ in range(3)]
            for i in range(3):
                stress[i][i] = wmu * (grad[i][i] + grad[i][i]) + swell
                for k in range(i):
                    stress[i][k] = wmu * (grad[i][k] + grad[k][i])
                    stress[k][i] = stress[i][k]
            for k in range(3):
                for a in range(10):
                    g = wide(k, a, q, e0)
                    for i in range(3):
                        term = stress[i][k] * g
                        forces[i][a] = term if q + k == 0 else forces[i][a] + term
        for a in range(10):
            high = row8(high_ref, a, e0)
            parts = [in_two(forces[i][a]) for i in range(3)]
            for h in range(4):
                mask = high == h
                kept = [jnp.where(mask, parts[i][s].astype(F32), 0.0) for s in range(2) for i in range(3)]
                left_ref[h * 48 : h * 48 + 48, a * elems + e0 : a * elems + e0 + LANES] = jnp.concatenate(
                    kept, axis=0
                ).astype(BF16)
    out = lax.dot_general(
        left_ref[...], hot_ref[...], (((1,), (1,)), ((), ())), preferred_element_type=F32
    )
    return [
        [
            (out[h * 48 + i * 8 : h * 48 + i * 8 + 8] + out[h * 48 + 24 + i * 8 : h * 48 + 32 + i * 8])[
                :, c * LANES : (c + 1) * LANES
            ]
            for h in range(4)
            for c in range(2)
        ]
        for i in range(3)
    ]


def lane_sum(values):
    total = values[0]
    for value in values[1:]:
        total = total + value
    return jnp.sum(total, axis=1, keepdims=True)


def setup_kernel(count_ref, conn_ref, bids_ref, grads_ref, hot_ref, high_ref, wide_ref, spot_ref):
    elems = conn_ref.shape[1]
    lows = lax.broadcasted_iota(jnp.int32, (256, LANES), 0)
    element = lax.broadcasted_iota(jnp.int32, (10, elems), 1)
    is_live = element < count_ref[0]
    high_ref[...] = jnp.where(is_live, conn_ref[...] >> 8, -1)
    for a in range(10):
        for e0 in range(0, elems, LANES):
            index = conn_ref[a : a + 1, e0 : e0 + LANES] & 255
            hot_ref[:, a * elems + e0 : a * elems + e0 + LANES] = jnp.where(lows == index, 1.0, 0.0).astype(BF16)
    for k in range(3):
        for a in range(10):
            wide_ref[k * 10 + a] = grads_ref[k, a].astype(F32)
    nodes = lax.broadcasted_iota(jnp.int32, spot_ref.shape, 0)
    spot_ref[...] = jnp.where(nodes == bids_ref[0:1, :], 1.0, 0.0).astype(BF16)


def begin_kernel(devices, inputs, p_ref, *rest):
    hbm = rest[:inputs]
    held = rest[inputs : 2 * inputs]
    d_ref, t0_ref, t1_ref, mixed_ref, blocks_ref, sems = rest[2 * inputs :]
    copies = [pltpu.make_async_copy(hbm[k], held[k], sems.at[k]) for k in range(inputs)]
    for copy in copies:
        copy.start()
    for copy in copies[:3]:
        copy.wait()
    rhs_ref, prec_ref, bids_ref = held[:3]
    p = p_ref[0]
    blocks_ref[...] = jnp.zeros_like(blocks_ref)
    for i in range(3):
        d_ref[8 * i : 8 * i + 8, :] = (
            prec_ref[i, 0:1, :] * rhs_ref[0:8, :]
            + prec_ref[i, 1:2, :] * rhs_ref[8:16, :]
            + prec_ref[i, 2:3, :] * rhs_ref[16:24, :]
        )
        for j in range(3):
            blocks_ref[3 * i + j : 3 * i + j + 1, :] = prec_ref[i, j : j + 1, :]
    rows = [split_lanes(d_ref[8 * i : 8 * i + 8, :]) for i in range(3)]
    rows += [split_lanes(blocks_ref[8 * i : 8 * i + 8, :]) for i in range(2)]
    tiles = boundary_values(rows, bids_ref)
    for r in range(5):
        here = slice(8 * r, 8 * r + 8)
        t0_ref[here, :] = tiles[0][r]
        t1_ref[here, :] = tiles[1][r]
        mixed_ref[here, :] = send_mixed(p, devices, tiles[0][r], tiles[1][r])
    for copy in copies[3:]:
        copy.wait()


def first_kernel(keys, devices, p_ref, d_ref, bids_ref, conn_ref, high_ref, wide_ref, qw_ref, lame_ref, hot_ref, mass_ref, *rest):
    received = dict(zip(keys, rest[: len(keys)]))
    q_ref, s0_ref, s1_ref, mixed_ref, gprec_ref, dot_ref, left_ref = rest[len(keys) :]
    p = p_ref[0]
    lane = lax.broadcasted_iota(jnp.int32, (8, LANES), 1)
    chunks = []
    for i in range(3):
        ghost = joined(p, devices, received, slice(8 * i, 8 * i + 8), lane, False)
        chunks.append(split_lanes(d_ref[8 * i : 8 * i + 8, :]) + ghost)
    for r in range(2):
        tiles = joined(p, devices, received, slice(24 + 8 * r, 32 + 8 * r), lane, False)
        for t in range(2):
            gprec_ref[8 * r : 8 * r + 8, t * LANES : (t + 1) * LANES] = tiles[t]
    acc = operate(chunks, conn_ref, high_ref, wide_ref, qw_ref, lame_ref, hot_ref, left_ref)
    own_chunks = d_ref.shape[1] // LANES
    mass = mass_rows(mass_ref)
    partial = [[acc[i][c] + mass[c] * chunks[i][c] for c in range(own_chunks)] for i in range(3)]
    tiles = boundary_values(partial, bids_ref)
    for i in range(3):
        send = [acc[i][own_chunks], acc[i][own_chunks + 1]], [tiles[0][i], tiles[1][i]]
        for part, (tile0, tile1) in enumerate(send):
            here = slice(24 * part + 8 * i, 24 * part + 8 * i + 8)
            s0_ref[here, :] = tile0
            s1_ref[here, :] = tile1
            mixed_ref[here, :] = send_mixed(p, devices, tile0, tile1)
    dots = []
    for i in range(3):
        for c in range(own_chunks):
            q_ref[8 * i : 8 * i + 8, c * LANES : (c + 1) * LANES] = partial[i][c]
            dots.append(partial[i][c] * chunks[i][c])
        for c in range(2):
            dots.append(acc[i][own_chunks + c] * chunks[i][own_chunks + c])
    dot_ref[...] = jnp.broadcast_to(lane_sum(dots), (8, LANES))


def mass_rows(mass_ref):
    count = mass_ref.shape[0] // LANES
    return [jnp.broadcast_to(mass_ref[c * LANES : (c + 1) * LANES].reshape(1, LANES), (8, LANES)) for c in range(count)]


WINDOWS = ((1, 0, 64, 0), (4, 0, 48, 1), (16, 96, 112, 1))
WIDTHS = {1: 64, 4: 48, 16: 16}


def second_kernel(
    keys,
    devices,
    p_ref,
    rhs_ref,
    d_ref,
    qpart_ref,
    s0_ref,
    s1_ref,
    prec_ref,
    gprec_ref,
    dot_ref,
    spot_ref,
    conn_ref,
    high_ref,
    wide_ref,
    qw_ref,
    lame_ref,
    hot_ref,
    mass_ref,
    *rest,
):
    received = dict(zip(keys, rest[: len(keys)]))
    q_ref, s_ref, w_ref, out_ref, left_ref = rest[len(keys) :]
    p = p_ref[0]
    own_chunks = d_ref.shape[1] // LANES
    lane = lax.broadcasted_iota(jnp.int32, (8, LANES), 1)
    back = [joined(p, devices, received, slice(8 * i, 8 * i + 8), lane, True) for i in range(3)]
    q_ref[...] = qpart_ref[...] + spread(back, spot_ref)
    largest = jnp.maximum(jnp.max(jnp.abs(prec_ref[...])), jnp.max(jnp.abs(gprec_ref[...])))
    inverse = 1.0 / largest
    ghost_q = []
    for i in range(3):
        tiles = joined(p, devices, received, slice(24 + 8 * i, 32 + 8 * i), lane, False)
        ghost_q.append([s0_ref[8 * i : 8 * i + 8, :] + tiles[0], s1_ref[8 * i : 8 * i + 8, :] + tiles[1]])
    chunks = []
    for i in range(3):
        value = (
            (prec_ref[i, 0:1, :] * inverse) * q_ref[0:8, :]
            + (prec_ref[i, 1:2, :] * inverse) * q_ref[8:16, :]
            + (prec_ref[i, 2:3, :] * inverse) * q_ref[16:24, :]
        )
        s_ref[8 * i : 8 * i + 8, :] = value
        chunks.append(split_lanes(value))
        for t in range(2):
            total = None
            for j in range(3):
                term = (gprec_ref[3 * i + j : 3 * i + j + 1, t * LANES : (t + 1) * LANES] * inverse) * ghost_q[j][t]
                total = term if j == 0 else total + term
            chunks[i].append(total)
    acc = operate(chunks, conn_ref, high_ref, wide_ref, qw_ref, lame_ref, hot_ref, left_ref)
    start = []
    cross = []
    square = []
    mass = mass_rows(mass_ref)
    for i in range(3):
        for c in range(own_chunks):
            here = slice(8 * i, 8 * i + 8), slice(c * LANES, (c + 1) * LANES)
            value = acc[i][c] + mass[c] * chunks[i][c]
            w_ref[here] = value
            square.append(value * chunks[i][c])
            cross.append(q_ref[here] * chunks[i][c])
            start.append(rhs_ref[here] * d_ref[here])
        for t in range(2):
            square.append(acc[i][own_chunks + t] * chunks[i][own_chunks + t])
    scalars = [lane_sum(start), dot_ref[:, 0:1], lane_sum(cross), lane_sum(square)]
    tail = jnp.broadcast_to(jnp.reshape(largest, (1, 1)), (8, LANES))
    for k, value in enumerate(scalars):
        tail = jnp.where(lane == 64 + k, value, tail)
    zero = jnp.zeros((8, LANES), F32)

    def clear(j, unused):
        for k in range(8):
            out_ref[8 * j + k, 0:8, :] = zero
            out_ref[8 * j + k, 8:16, :] = tail
        return unused

    lax.fori_loop(0, devices // 8, clear, 0)
    for distance, shift_plus, shift_minus, tile in WINDOWS:
        for sign, shift in ((1, shift_plus), (-1, shift_minus)):
            moved = [acc[i][own_chunks + tile] for i in range(3)]
            if shift:
                moved = [pltpu.roll(m, LANES - shift, 1) for m in moved]
            target = p + sign * distance

            @pl.when((target >= 0) & (target < devices))
            def _():
                out_ref[target, 0:8, :] = jnp.where(lane < 64, moved[0], pltpu.roll(moved[1], 64, 1))
                out_ref[target, 8:16, :] = jnp.where(lane < 64, moved[2], tail)


def final_kernel(p_ref, in_ref, rhs_ref, d_ref, q_ref, s_ref, wpart_ref, spot_ref, x_ref, r_ref):
    p = p_ref[0]
    devices = in_ref.shape[0]
    lane = lax.broadcasted_iota(jnp.int32, (8, LANES), 1)
    mine = jnp.broadcast_to(in_ref[p, 8:16, 68:69], (8, LANES))
    inv_mine = 1.0 / mine

    def term(j):
        tile = in_ref[j, 8:16, :]
        ratio = pltpu.roll(tile, LANES - 4, 1) * inv_mine
        return tile * jnp.where(lane == 66, ratio, jnp.where(lane == 67, ratio * ratio, 1.0))

    def add_up(j, sums):
        values = [term(8 * j + k) for k in range(8)]
        while len(values) > 1:
            values = [a + b for a, b in zip(values[::2], values[1::2])]
        return sums + values[0]

    sums = lax.fori_loop(0, devices // 8, add_up, jnp.zeros((8, LANES), F32), unroll=devices <= 64)
    e0, d0, cross, square = (jnp.broadcast_to(sums[:, k : k + 1], (8, LANES)) for k in range(64, 68))
    step = e0 / d0
    scaled = step * mine
    fresh = scaled * (step * cross) - e0
    beta = fresh / e0
    more = 1.0 + beta
    bend = more * more * d0 - 2.0 * more * (scaled * cross) + scaled * (scaled * square)
    step1 = fresh / bend
    for_d = step + step1 * more
    for_s = step1 * scaled

    zero = jnp.zeros((8, LANES), F32)
    back = [[zero, zero] for _ in range(3)]
    for distance, shift_plus, shift_minus, tile in WINDOWS:
        for sign, shift in ((1, shift_plus), (-1, shift_minus)):
            source = p - sign * distance
            valid = (source >= 0) & (source < devices)
            source = jnp.clip(source, 0, devices - 1)
            pair = in_ref[source, 0:8, :]
            last = in_ref[source, 8:16, :]
            ratio = jnp.broadcast_to(last[:, 68:69], (8, LANES)) * inv_mine
            blocks = [pair, pltpu.roll(pair, 64, 1), last]
            inside = (lane >= shift) & (lane < shift + WIDTHS[distance]) & valid
            for i in range(3):
                moved = blocks[i] if shift == 0 else pltpu.roll(blocks[i], shift, 1)
                back[i][tile] = jnp.where(inside, moved * ratio, back[i][tile])
    w = spread(back, spot_ref)
    for i in range(3):
        for c in range(rhs_ref.shape[1] // LANES):
            here = slice(8 * i, 8 * i + 8), slice(c * LANES, (c + 1) * LANES)
            x_ref[here] = for_d * d_ref[here] - for_s * s_ref[here]
            r_ref[here] = rhs_ref[here] - for_d * q_ref[here] + for_s * (wpart_ref[here] + w[here])


def local(
    devices,
    right_side,
    mass_diag,
    precond_blocks,
    connectivity,
    shape_grads,
    quad_weight,
    lame_moduli,
    elem_count,
    boundary_ids,
):
    own = right_side.shape[2]
    elems = connectivity.shape[1]
    ghosts = boundary_ids.shape[0]
    p = lax.axis_index(AXIS).astype(jnp.int32).reshape(1)
    rhs = right_side.reshape(24, own)
    bids = boundary_ids.reshape(1, ghosts)
    grads = jnp.transpose(shape_grads, (1, 2, 0, 3))
    vmem = pl.BlockSpec(memory_space=pltpu.VMEM)
    smem = pl.BlockSpec(memory_space=pltpu.SMEM)
    hbm = pl.BlockSpec(memory_space=pltpu.HBM)
    moves = routes(devices)
    keys = list(moves)

    def shape(*dims, dtype=F32):
        return jax.ShapeDtypeStruct(dims, dtype)

    def call(kernel, out_shape, in_specs, scratch=(), cost=None):
        return pl.pallas_call(
            kernel,
            out_shape=out_shape,
            in_specs=in_specs,
            out_specs=[vmem] * len(out_shape),
            scratch_shapes=list(scratch),
            cost_estimate=cost,
            compiler_params=pltpu.CompilerParams(vmem_limit_bytes=24 << 20),
        )

    def exchange(tile0, tile1, mixed):
        tiles = {1: tile0, 4: tile1, 16: tile1}
        return [
            lax.ppermute(mixed if key == (4, 1) else tiles[key[0]], AXIS, sorted(moves[key].items())) for key in keys
        ]

    tile = shape(40, LANES)
    inputs = [
        pltpu.with_memory_space_constraint(value, pltpu.HBM)
        for value in (rhs, precond_blocks, bids, connectivity, grads, quad_weight, lame_moduli, mass_diag)
    ]
    *held, d, t0, t1, mixed = call(
        functools.partial(begin_kernel, devices, len(inputs)),
        [shape(*value.shape, dtype=value.dtype) for value in inputs] + [shape(24, own), tile, tile, tile],
        [smem] + [hbm] * len(inputs),
        [pltpu.VMEM((16, own), F32), pltpu.SemaphoreType.DMA((len(inputs),))],
    )(pltpu.with_memory_space_constraint(p, pltpu.SMEM), *inputs)
    rhs, precond_blocks, bids, connectivity, grads, quad_weight, lame_moduli, mass_diag = held
    got = exchange(t0, t1, mixed)
    hot, high, wide, spot = call(
        setup_kernel,
        [
            shape(256, 10 * elems, dtype=BF16),
            shape(10, elems, dtype=jnp.int32),
            shape(30, 4, elems),
            shape(own, ghosts, dtype=BF16),
        ],
        [smem] + [vmem] * 3,
        cost=pl.CostEstimate(flops=20_000_000, bytes_accessed=4_000_000, transcendentals=0),
    )(elem_count, connectivity, bids, grads)
    mesh_args = (connectivity, high, wide, quad_weight, lame_moduli, hot, mass_diag)
    left = [pltpu.VMEM((192, 10 * elems), BF16)]
    tile = shape(48, LANES)
    qpart, s0, s1, mixed, gprec, dot = call(
        functools.partial(first_kernel, keys, devices),
        [shape(24, own), tile, tile, tile, shape(16, 2 * LANES), shape(8, LANES)],
        [smem] + [vmem] * (9 + len(keys)),
        left,
    )(p, d, bids, *mesh_args, *got)
    got = exchange(s0, s1, mixed)
    q, s, wpart, message = call(
        functools.partial(second_kernel, keys, devices),
        [shape(24, own), shape(24, own), shape(24, own), shape(devices, 16, LANES)],
        [smem] + [vmem] * (16 + len(keys)),
        left,
    )(p, rhs, d, qpart, s0, s1, precond_blocks, gprec, dot, spot, *mesh_args, *got)
    message = lax.all_to_all(message, AXIS, 0, 0, tiled=True)
    x, r = call(final_kernel, [shape(24, own), shape(24, own)], [smem] + [vmem] * 7)(
        p, message, rhs, d, q, s, wpart, spot
    )
    return x.reshape(3, CASES, own), r.reshape(3, CASES, own)


def solution(mesh):
    return jax.shard_map(
        functools.partial(local, mesh.shape[AXIS]),
        mesh=mesh,
        in_specs=(
            P(None, None, AXIS),
            P(AXIS),
            P(None, None, AXIS),
            P(None, AXIS),
            P(None, None, None, AXIS),
            P(None, AXIS),
            P(None, AXIS),
            P(AXIS),
            P(AXIS),
        ),
        out_specs=(P(None, None, AXIS), P(None, None, AXIS)),
        check_vma=False,
    )
```

```python
import functools

import jax
import jax.numpy as jnp
from jax import lax
from jax.experimental import pallas as pl
from jax.experimental.pallas import tpu as pltpu
from jax.sharding import PartitionSpec as P

F32 = jnp.float32
BF16 = jnp.bfloat16
AXIS = "dom"
CASES = 8
LANES = 128
DISTANCES = (1, 4, 16)


def routes(devices):
    listed = {}
    for distance in DISTANCES:
        for parity in (0, 1):
            route = {}
            for i in range(devices - distance):
                if (i // distance) % 2 == parity:
                    route[i], route[i + distance] = i + distance, i
            if route:
                for i in range(devices):
                    route.setdefault(i, i ^ 1)
                listed[distance, parity] = route
    last = devices - 1
    listed[1, 1].update({0: 1, 1: 2, 2: 0, last: last - 1, last - 1: last - 2, last - 2: last})
    listed[4, 1].update({2: 1, 1: 0, 0: 3, 3: 2})
    listed[4, 1].update({last - 2: last - 1, last - 1: last, last: last - 3, last - 3: last - 2})
    for route in listed.values():
        assert sorted(route.values()) == list(range(devices))
    return listed


def take_lanes(chunks, index):
    lane = index & (LANES - 1)
    which = index >> 7
    rows = len(chunks)
    picked = [None] * rows
    for c in range(len(chunks[0])):
        mask = which == c
        for r in range(rows):
            moved = jnp.take_along_axis(chunks[r][c], lane, axis=1)
            picked[r] = moved if c == 0 else jnp.where(mask, moved, picked[r])
    return picked


def row8(ref, row, start=0, width=LANES):
    return jnp.broadcast_to(ref[row : row + 1, start : start + width], (8, width))


def split_lanes(value):
    return [value[:, c * LANES : (c + 1) * LANES] for c in range(value.shape[1] // LANES)]


def in_two(value):
    head = value.astype(BF16)
    tail = (value - head.astype(F32)).astype(BF16)
    return head, tail


def joined(p, devices, received, rows, lane, opposite):
    sides = {}
    detour = (p == 1) | (p == devices - 2)
    for distance in DISTANCES:
        even = received[distance, 0][rows, :]
        first = lax.rem(lax.div(p, distance), 2) == 0
        if (distance, 1) in received:
            odd = received[distance, 1][rows, :]
            if distance == 1:
                odd = jnp.where(detour, received[4, 1][rows, :], odd)
        else:
            odd = jnp.zeros_like(even)
        plus = jnp.where(p + distance < devices, jnp.where(first, even, odd), 0.0)
        minus = jnp.where(p - distance >= 0, jnp.where(first, odd, even), 0.0)
        sides[distance] = (minus, plus) if opposite else (plus, minus)
    tile0 = jnp.where(lane < 64, sides[1][0], sides[1][1])
    tile1 = jnp.where(
        lane < 48,
        sides[4][0],
        jnp.where(lane < 96, sides[4][1], jnp.where(lane < 112, sides[16][0], sides[16][1])),
    )
    return [tile0, tile1]


def send_mixed(p, devices, tile0, tile1):
    return jnp.where((p == 2) | (p == devices - 3), tile0, tile1)


def spread(tiles, spot_ref):
    stacked = jnp.concatenate([jnp.concatenate(t, axis=1) for t in tiles], axis=0)
    head, tail = in_two(stacked)
    left = jnp.concatenate([head, tail], axis=0)
    out = lax.dot_general(left, spot_ref[...], (((1,), (1,)), ((), ())), preferred_element_type=F32)
    return out[:24] + out[24:]


def boundary_values(chunks, bids_ref):
    return [take_lanes(chunks, row8(bids_ref, 0, t * LANES)) for t in range(2)]


def elements(chunks, conn_ref, high_ref, wide_ref, qw_ref, lame_ref, left_ref):
    elems = conn_ref.shape[1]
    work = jnp.zeros((8, LANES), F32)

    def wide(k, a, q, e0):
        return jnp.broadcast_to(wide_ref[k * 10 + a, q : q + 1, e0 : e0 + LANES], (8, LANES))

    for e0 in range(0, elems, LANES):
        nodal = [take_lanes(chunks, row8(conn_ref, a, e0)) for a in range(10)]
        forces = [[None] * 10 for _ in range(3)]
        lam = lame_ref[0:1, e0 : e0 + LANES]
        mu = lame_ref[1:2, e0 : e0 + LANES]
        for q in range(4):
            grad = [[None] * 3 for _ in range(3)]
            for k in range(3):
                for a in range(10):
                    g = wide(k, a, q, e0)
                    for i in range(3):
                        term = nodal[a][i] * g
                        grad[i][k] = term if a == 0 else grad[i][k] + term
            w = qw_ref[q : q + 1, e0 : e0 + LANES]
            wmu = jnp.broadcast_to(w * mu, (8, LANES))
            wlam = jnp.broadcast_to(w * lam, (8, LANES))
            swell = wlam * (grad[0][0] + grad[1][1] + grad[2][2])
            stress = [[None] * 3 for _ in range(3)]
            for i in range(3):
                stress[i][i] = wmu * (grad[i][i] + grad[i][i]) + swell
                for k in range(i):
                    stress[i][k] = wmu * (grad[i][k] + grad[k][i])
                    stress[k][i] = stress[i][k]
            for k in range(3):
                for a in range(10):
                    g = wide(k, a, q, e0)
                    for i in range(3):
                        term = stress[i][k] * g
                        forces[i][a] = term if q + k == 0 else forces[i][a] + term
        done = forces[0][0] * nodal[0][0]
        for a in range(10):
            for i in range(3):
                if a + i > 0:
                    done = done + forces[i][a] * nodal[a][i]
        work = work + jnp.where(row8(high_ref, 0, e0) >= 0, done, 0.0)
        for a in range(10):
            high = row8(high_ref, a, e0)
            parts = [in_two(forces[i][a]) for i in range(3)]
            for h in range(4):
                mask = high == h
                kept = [jnp.where(mask, parts[i][s].astype(F32), 0.0) for s in range(2) for i in range(3)]
                at = e0 * 10 + a * LANES
                left_ref[h * 48 : h * 48 + 48, at : at + LANES] = jnp.concatenate(kept, axis=0).astype(BF16)
    return work


def scatter(left_ref, hot_ref, first, last):
    out = lax.dot_general(
        left_ref[48 * first : 48 * last, :], hot_ref[...], (((1,), (0,)), ((), ())), preferred_element_type=F32
    )
    blocks = []
    for i in range(3):
        blocks.append([])
        for h in range(last - first):
            at = h * 48 + i * 8
            blocks[i] += split_lanes(out[at : at + 8] + out[at + 24 : at + 32])
    return blocks


def splat(value):
    return jnp.broadcast_to(value, (8, LANES))


def lane_sum(values):
    total = values[0]
    for value in values[1:]:
        total = total + value
    return jnp.sum(total, axis=1, keepdims=True)


def setup_kernel(
    count_ref, conn_ref, bids_ref, grads_ref, rhs_ref, d_ref, prec_ref, hot_ref, high_ref, wide_ref, spot_ref, start_ref, size_ref
):
    elems = conn_ref.shape[1]
    element = lax.broadcasted_iota(jnp.int32, (10, elems), 1)
    is_live = element < count_ref[0]
    high_ref[...] = jnp.where(is_live, conn_ref[...] >> 8, -1)
    lows = lax.broadcasted_iota(jnp.int32, (LANES, 256), 1)
    padding = jnp.zeros((6, LANES), jnp.int32)
    for e0 in range(0, elems, LANES):
        index = jnp.concatenate([conn_ref[:, e0 : e0 + LANES] & 255, padding], axis=0).T
        for a in range(10):
            at = e0 * 10 + a * LANES
            hot_ref[at : at + LANES, :] = jnp.where(lows == index[:, a : a + 1], 1.0, 0.0).astype(BF16)
    for k in range(3):
        for a in range(10):
            wide_ref[k * 10 + a] = grads_ref[k, a].astype(F32)
    nodes = lax.broadcasted_iota(jnp.int32, spot_ref.shape, 0)
    spot_ref[...] = jnp.where(nodes == bids_ref[0:1, :], 1.0, 0.0).astype(BF16)
    blocks = [slice(8 * i, 8 * i + 8) for i in range(3)]
    start_ref[...] = splat(lane_sum([p for b in blocks for p in split_lanes(rhs_ref[b, :] * d_ref[b, :])]))
    largest = jnp.abs(prec_ref[0])
    for i in range(1, 3):
        largest = jnp.maximum(largest, jnp.abs(prec_ref[i]))
    size_ref[...] = splat(jnp.max(jnp.max(largest, axis=1, keepdims=True), axis=0, keepdims=True))


def begin_kernel(devices, inputs, p_ref, *rest):
    hbm = rest[:inputs]
    held = rest[inputs : 2 * inputs]
    d_ref, t0_ref, t1_ref, mixed_ref, blocks_ref, sems = rest[2 * inputs :]
    copies = [pltpu.make_async_copy(hbm[k], held[k], sems.at[k]) for k in range(inputs)]
    for copy in copies:
        copy.start()
    for copy in copies[:3]:
        copy.wait()
    rhs_ref, prec_ref, bids_ref = held[:3]
    p = p_ref[0]
    blocks_ref[...] = jnp.zeros_like(blocks_ref)
    for i in range(3):
        d_ref[8 * i : 8 * i + 8, :] = (
            prec_ref[i, 0:1, :] * rhs_ref[0:8, :]
            + prec_ref[i, 1:2, :] * rhs_ref[8:16, :]
            + prec_ref[i, 2:3, :] * rhs_ref[16:24, :]
        )
        for j in range(3):
            blocks_ref[3 * i + j : 3 * i + j + 1, :] = prec_ref[i, j : j + 1, :]
    rows = [split_lanes(d_ref[8 * i : 8 * i + 8, :]) for i in range(3)]
    rows += [split_lanes(blocks_ref[8 * i : 8 * i + 8, :]) for i in range(2)]
    tiles = boundary_values(rows, bids_ref)
    for r in range(5):
        here = slice(8 * r, 8 * r + 8)
        t0_ref[here, :] = tiles[0][r]
        t1_ref[here, :] = tiles[1][r]
        mixed_ref[here, :] = send_mixed(p, devices, tiles[0][r], tiles[1][r])
    for copy in copies[3:]:
        copy.wait()


def first_kernel(
    keys, devices, p_ref, d_ref, bids_ref, size_ref, conn_ref, high_ref, wide_ref, qw_ref, lame_ref, hot_ref, mass_ref, *rest
):
    received = dict(zip(keys, rest[: len(keys)]))
    q_ref, s0_ref, s1_ref, mixed_ref, gprec_ref, scale_ref, dot_ref, left_ref = rest[len(keys) :]
    p = p_ref[0]
    lane = lax.broadcasted_iota(jnp.int32, (8, LANES), 1)
    chunks = []
    for i in range(3):
        ghost = joined(p, devices, received, slice(8 * i, 8 * i + 8), lane, False)
        chunks.append(split_lanes(d_ref[8 * i : 8 * i + 8, :]) + ghost)
    largest = size_ref[...]
    for r in range(2):
        tiles = joined(p, devices, received, slice(24 + 8 * r, 32 + 8 * r), lane, False)
        for t in range(2):
            gprec_ref[8 * r : 8 * r + 8, t * LANES : (t + 1) * LANES] = tiles[t]
            largest = jnp.maximum(largest, jnp.abs(tiles[t]))
    scale_ref[...] = splat(jnp.max(jnp.max(largest, axis=1, keepdims=True), axis=0, keepdims=True))
    work = elements(chunks, conn_ref, high_ref, wide_ref, qw_ref, lame_ref, left_ref)
    acc = scatter(left_ref, hot_ref, 0, 4)
    own_chunks = d_ref.shape[1] // LANES
    mass = mass_rows(mass_ref)
    dots = [work]
    partial = []
    for i in range(3):
        partial.append([])
        for c in range(own_chunks):
            heavy = mass[c] * chunks[i][c]
            partial[i].append(acc[i][c] + heavy)
            dots.append(heavy * chunks[i][c])
    tiles = boundary_values(partial, bids_ref)
    for i in range(3):
        send = [acc[i][own_chunks], acc[i][own_chunks + 1]], [tiles[0][i], tiles[1][i]]
        for part, (tile0, tile1) in enumerate(send):
            here = slice(24 * part + 8 * i, 24 * part + 8 * i + 8)
            s0_ref[here, :] = tile0
            s1_ref[here, :] = tile1
            mixed_ref[here, :] = send_mixed(p, devices, tile0, tile1)
        for c in range(own_chunks):
            q_ref[8 * i : 8 * i + 8, c * LANES : (c + 1) * LANES] = partial[i][c]
    dot_ref[...] = splat(lane_sum(dots))


def mass_rows(mass_ref):
    count = mass_ref.shape[0] // LANES
    return [jnp.broadcast_to(mass_ref[c * LANES : (c + 1) * LANES].reshape(1, LANES), (8, LANES)) for c in range(count)]


WINDOWS = ((1, 0, 64, 0), (4, 0, 48, 1), (16, 96, 112, 1))
WIDTHS = {1: 64, 4: 48, 16: 16}


def second_kernel(
    keys,
    devices,
    p_ref,
    qpart_ref,
    s0_ref,
    s1_ref,
    prec_ref,
    gprec_ref,
    scale_ref,
    start_ref,
    dot_ref,
    spot_ref,
    conn_ref,
    high_ref,
    wide_ref,
    qw_ref,
    lame_ref,
    hot_ref,
    mass_ref,
    *rest,
):
    received = dict(zip(keys, rest[: len(keys)]))
    q_ref, s_ref, w_ref, out_ref, left_ref = rest[len(keys) :]
    p = p_ref[0]
    own_chunks = q_ref.shape[1] // LANES
    lane = lax.broadcasted_iota(jnp.int32, (8, LANES), 1)
    case = lax.broadcasted_iota(jnp.int32, (8, LANES), 0)
    back = [joined(p, devices, received, slice(8 * i, 8 * i + 8), lane, True) for i in range(3)]
    q_ref[...] = qpart_ref[...] + spread(back, spot_ref)
    scale = scale_ref[...]
    inverse = (1.0 / scale)[0:1, 0:1]
    ghost_q = []
    for i in range(3):
        tiles = joined(p, devices, received, slice(24 + 8 * i, 32 + 8 * i), lane, False)
        ghost_q.append([s0_ref[8 * i : 8 * i + 8, :] + tiles[0], s1_ref[8 * i : 8 * i + 8, :] + tiles[1]])
    chunks = []
    for i in range(3):
        value = (
            (prec_ref[i, 0:1, :] * inverse) * q_ref[0:8, :]
            + (prec_ref[i, 1:2, :] * inverse) * q_ref[8:16, :]
            + (prec_ref[i, 2:3, :] * inverse) * q_ref[16:24, :]
        )
        s_ref[8 * i : 8 * i + 8, :] = value
        chunks.append(split_lanes(value))
        for t in range(2):
            total = None
            for j in range(3):
                term = (gprec_ref[3 * i + j : 3 * i + j + 1, t * LANES : (t + 1) * LANES] * inverse) * ghost_q[j][t]
                total = term if j == 0 else total + term
            chunks[i].append(total)
    work = elements(chunks, conn_ref, high_ref, wide_ref, qw_ref, lame_ref, left_ref)
    acc = scatter(left_ref, hot_ref, 0, 4)
    ghost = [acc[i][own_chunks:] for i in range(3)]
    mass = mass_rows(mass_ref)
    cross = []
    square = [work]
    for i in range(3):
        for c in range(own_chunks):
            here = slice(8 * i, 8 * i + 8), slice(c * LANES, (c + 1) * LANES)
            heavy = mass[c] * chunks[i][c]
            w_ref[here] = acc[i][c] + heavy
            cross.append(q_ref[here] * chunks[i][c])
            square.append(heavy * chunks[i][c])
    tail = jnp.zeros((8, LANES), F32)
    for k, value in enumerate((start_ref[...], dot_ref[...], splat(lane_sum(cross)), splat(lane_sum(square)))):
        tail = jnp.where(lane == 8 * k + case, value, tail)
    tail = jnp.where(lane[0:1] < 32, jnp.sum(tail, axis=0, keepdims=True), scale[0:1])

    def fill(j, unused):
        for k in range(8):
            out_ref[8 * j + k, 12, :, :] = tail
        return unused

    lax.fori_loop(0, devices // 8, fill, 0)
    for distance, shift_plus, shift_minus, tile in WINDOWS:
        for sign, shift in ((1, shift_plus), (-1, shift_minus)):
            moved = [ghost[i][tile] for i in range(3)]
            if shift:
                moved = [pltpu.roll(m, LANES - shift, 1) for m in moved]
            pair = jnp.where(lane < 64, moved[0], pltpu.roll(moved[1], 64, 1))
            rest = jnp.where(lane < 64, moved[2], pltpu.roll(pltpu.roll(moved[2], 4, 0), 64, 1))
            target = p + sign * distance

            @pl.when((target >= 0) & (target < devices))
            def _():
                out_ref[target, 0:8, 0, :] = pair
                out_ref[target, 8:12, 0, :] = rest[0:4]


def final_kernel(p_ref, in_ref, scale_ref, rhs_ref, d_ref, q_ref, s_ref, wpart_ref, spot_ref, x_ref, r_ref):
    p = p_ref[0]
    devices = in_ref.shape[0]
    lane = lax.broadcasted_iota(jnp.int32, (8, LANES), 1)
    case = lax.broadcasted_iota(jnp.int32, (8, LANES), 0)
    mine = scale_ref[...]
    inv_mine = 1.0 / mine
    sums = None
    for j in range(0, devices, 8):
        rows = in_ref[j : j + 8, 12, 0, :]
        ratio = pltpu.roll(rows, LANES - 32, 1) * inv_mine
        rows = rows * jnp.where(lane < 16, 1.0, jnp.where(lane < 24, ratio, ratio * ratio))
        sums = rows if j == 0 else sums + rows
    sums = splat(jnp.sum(sums, axis=0, keepdims=True))
    e0, d0, cross, square = (
        splat(jnp.sum(jnp.where(lane == 8 * k + case, sums, 0.0), axis=1, keepdims=True)) for k in range(4)
    )
    step = e0 / d0
    scaled = step * mine
    fresh = scaled * (step * cross) - e0
    beta = fresh / e0
    more = 1.0 + beta
    bend = more * more * d0 - 2.0 * more * (scaled * cross) + scaled * (scaled * square)
    step1 = fresh / bend
    for_d = step + step1 * more
    for_s = step1 * scaled

    zero = jnp.zeros((8, LANES), F32)
    back = [[zero, zero] for _ in range(3)]
    for distance, shift_plus, shift_minus, tile in WINDOWS:
        for sign, shift in ((1, shift_plus), (-1, shift_minus)):
            source = p - sign * distance
            valid = (source >= 0) & (source < devices)
            source = jnp.clip(source, 0, devices - 1)
            pair = in_ref[source, 0:8, 0, :]
            rest = in_ref[source, 8:12, 0, :]
            rest = jnp.concatenate([rest, pltpu.roll(rest, 64, 1)], axis=0)
            ratio = splat(in_ref[source, 12, :, 32:33]) * inv_mine
            blocks = [pair, pltpu.roll(pair, 64, 1), rest]
            inside = (lane >= shift) & (lane < shift + WIDTHS[distance]) & valid
            for i in range(3):
                moved = blocks[i] if shift == 0 else pltpu.roll(blocks[i], shift, 1)
                back[i][tile] = jnp.where(inside, moved * ratio, back[i][tile])
    w = spread(back, spot_ref)
    for i in range(3):
        for c in range(rhs_ref.shape[1] // LANES):
            here = slice(8 * i, 8 * i + 8), slice(c * LANES, (c + 1) * LANES)
            x_ref[here] = for_d * d_ref[here] - for_s * s_ref[here]
            r_ref[here] = rhs_ref[here] - for_d * q_ref[here] + for_s * (wpart_ref[here] + w[here])


def local(
    devices,
    right_side,
    mass_diag,
    precond_blocks,
    connectivity,
    shape_grads,
    quad_weight,
    lame_moduli,
    elem_count,
    boundary_ids,
):
    own = right_side.shape[2]
    elems = connectivity.shape[1]
    ghosts = boundary_ids.shape[0]
    p = lax.axis_index(AXIS).astype(jnp.int32).reshape(1)
    rhs = right_side.reshape(24, own)
    bids = boundary_ids.reshape(1, ghosts)
    grads = jnp.transpose(shape_grads, (1, 2, 0, 3))
    vmem = pl.BlockSpec(memory_space=pltpu.VMEM)
    smem = pl.BlockSpec(memory_space=pltpu.SMEM)
    hbm = pl.BlockSpec(memory_space=pltpu.HBM)
    moves = routes(devices)
    keys = list(moves)

    def shape(*dims, dtype=F32):
        return jax.ShapeDtypeStruct(dims, dtype)

    def call(kernel, out_shape, in_specs, scratch=(), cost=None):
        return pl.pallas_call(
            kernel,
            out_shape=out_shape,
            in_specs=in_specs,
            out_specs=[vmem] * len(out_shape),
            scratch_shapes=list(scratch),
            cost_estimate=cost,
            compiler_params=pltpu.CompilerParams(vmem_limit_bytes=24 << 20),
        )

    def exchange(tile0, tile1, mixed):
        tiles = {1: tile0, 4: tile1, 16: tile1}
        return [
            lax.ppermute(mixed if key == (4, 1) else tiles[key[0]], AXIS, sorted(moves[key].items())) for key in keys
        ]

    tile = shape(40, LANES)
    inputs = [
        pltpu.with_memory_space_constraint(value, pltpu.HBM)
        for value in (rhs, precond_blocks, bids, connectivity, grads, quad_weight, lame_moduli, mass_diag)
    ]
    *held, d, t0, t1, mixed = call(
        functools.partial(begin_kernel, devices, len(inputs)),
        [shape(*value.shape, dtype=value.dtype) for value in inputs] + [shape(24, own), tile, tile, tile],
        [smem] + [hbm] * len(inputs),
        [pltpu.VMEM((16, own), F32), pltpu.SemaphoreType.DMA((len(inputs),))],
    )(pltpu.with_memory_space_constraint(p, pltpu.SMEM), *inputs)
    rhs, precond_blocks, bids, connectivity, grads, quad_weight, lame_moduli, mass_diag = held
    got = exchange(t0, t1, mixed)
    row = shape(8, LANES)
    hot, high, wide, spot, start, size = call(
        setup_kernel,
        [
            shape(10 * elems, 256, dtype=BF16),
            shape(10, elems, dtype=jnp.int32),
            shape(30, 4, elems),
            shape(own, ghosts, dtype=BF16),
            row,
            row,
        ],
        [smem] + [vmem] * 6,
        cost=pl.CostEstimate(flops=20_000_000, bytes_accessed=4_000_000, transcendentals=0),
    )(elem_count, connectivity, bids, grads, rhs, d, precond_blocks)
    mesh_args = (connectivity, high, wide, quad_weight, lame_moduli, hot, mass_diag)
    left = [pltpu.VMEM((192, 10 * elems), BF16)]
    tile = shape(48, LANES)
    qpart, s0, s1, mixed, gprec, scale, dot = call(
        functools.partial(first_kernel, keys, devices),
        [shape(24, own), tile, tile, tile, shape(16, 2 * LANES), row, row],
        [smem] + [vmem] * (10 + len(keys)),
        left,
    )(p, d, bids, size, *mesh_args, *got)
    got = exchange(s0, s1, mixed)
    q, s, wpart, message = call(
        functools.partial(second_kernel, keys, devices),
        [shape(24, own), shape(24, own), shape(24, own), shape(devices, 13, 1, LANES)],
        [smem] + [vmem] * (16 + len(keys)),
        left,
    )(p, qpart, s0, s1, precond_blocks, gprec, scale, start, dot, spot, *mesh_args, *got)
    message = lax.all_to_all(message, AXIS, 0, 0, tiled=True)
    x, r = call(final_kernel, [shape(24, own), shape(24, own)], [smem] + [vmem] * 8)(
        p, message, scale, rhs, d, q, s, wpart, spot
    )
    return x.reshape(3, CASES, own), r.reshape(3, CASES, own)


def solution(mesh):
    return jax.shard_map(
        functools.partial(local, mesh.shape[AXIS]),
        mesh=mesh,
        in_specs=(
            P(None, None, AXIS),
            P(AXIS),
            P(None, None, AXIS),
            P(None, AXIS),
            P(None, None, None, AXIS),
            P(None, AXIS),
            P(None, AXIS),
            P(AXIS),
            P(AXIS),
        ),
        out_specs=(P(None, None, AXIS), P(None, None, AXIS)),
        check_vma=False,
    )
```

```python
import functools

import jax
import jax.numpy as jnp
from jax import lax
from jax.experimental import pallas as pl
from jax.experimental.pallas import tpu as pltpu
from jax.sharding import PartitionSpec as P

F32 = jnp.float32
BF16 = jnp.bfloat16
AXIS = "dom"
CASES = 8
LANES = 128
DISTANCES = (1, 4, 16)


def routes(devices):
    listed = {}
    for distance in DISTANCES:
        for parity in (0, 1):
            route = {}
            for i in range(devices - distance):
                if (i // distance) % 2 == parity:
                    route[i], route[i + distance] = i + distance, i
            if route:
                for i in range(devices):
                    route.setdefault(i, i ^ 1)
                listed[distance, parity] = route
    last = devices - 1
    listed[1, 1].update({0: 1, 1: 2, 2: 0, last: last - 1, last - 1: last - 2, last - 2: last})
    listed[4, 1].update({2: 1, 1: 0, 0: 3, 3: 2})
    listed[4, 1].update({last - 2: last - 1, last - 1: last, last: last - 3, last - 3: last - 2})
    for route in listed.values():
        assert sorted(route.values()) == list(range(devices))
    return listed


def take_lanes(chunks, index):
    lane = index & (LANES - 1)
    which = index >> 7
    rows = len(chunks)
    picked = [None] * rows
    for c in range(len(chunks[0])):
        mask = which == c
        for r in range(rows):
            moved = jnp.take_along_axis(chunks[r][c], lane, axis=1)
            picked[r] = moved if c == 0 else jnp.where(mask, moved, picked[r])
    return picked


def row8(ref, row, start=0, width=LANES):
    return jnp.broadcast_to(ref[row : row + 1, start : start + width], (8, width))


def split_lanes(value):
    return [value[:, c * LANES : (c + 1) * LANES] for c in range(value.shape[1] // LANES)]


def in_two(value):
    head = value.astype(BF16)
    tail = (value - head.astype(F32)).astype(BF16)
    return head, tail


def joined(p, devices, received, rows, lane, opposite):
    sides = {}
    detour = (p == 1) | (p == devices - 2)
    for distance in DISTANCES:
        even = received[distance, 0][rows, :]
        first = lax.rem(lax.div(p, distance), 2) == 0
        if (distance, 1) in received:
            odd = received[distance, 1][rows, :]
            if distance == 1:
                odd = jnp.where(detour, received[4, 1][rows, :], odd)
        else:
            odd = jnp.zeros_like(even)
        plus = jnp.where(p + distance < devices, jnp.where(first, even, odd), 0.0)
        minus = jnp.where(p - distance >= 0, jnp.where(first, odd, even), 0.0)
        sides[distance] = (minus, plus) if opposite else (plus, minus)
    tile0 = jnp.where(lane < 64, sides[1][0], sides[1][1])
    tile1 = jnp.where(
        lane < 48,
        sides[4][0],
        jnp.where(lane < 96, sides[4][1], jnp.where(lane < 112, sides[16][0], sides[16][1])),
    )
    return [tile0, tile1]


def send_mixed(p, devices, tile0, tile1):
    return jnp.where((p == 2) | (p == devices - 3), tile0, tile1)


def spread(tiles, place_ref, block):
    place = jnp.broadcast_to(place_ref[0:1, block * LANES : (block + 1) * LANES], (8, LANES))
    return [jnp.where(place >= 0, value, 0.0) for value in take_lanes(tiles, place)]


def boundary_values(chunks, bids_ref):
    return [take_lanes(chunks, row8(bids_ref, 0, t * LANES)) for t in range(2)]


def elements(chunks, conn_ref, high_ref, wide_ref, qw_ref, lame_ref, left_ref):
    elems = conn_ref.shape[1]
    work = jnp.zeros((8, LANES), F32)

    def wide(k, a, q, e0):
        return jnp.broadcast_to(wide_ref[k * 10 + a, q : q + 1, e0 : e0 + LANES], (8, LANES))

    for e0 in range(0, elems, LANES):
        nodal = [take_lanes(chunks, row8(conn_ref, a, e0)) for a in range(10)]
        forces = [[None] * 10 for _ in range(3)]
        lam = lame_ref[0:1, e0 : e0 + LANES]
        mu = lame_ref[1:2, e0 : e0 + LANES]
        for q in range(4):
            grad = [[None] * 3 for _ in range(3)]
            for k in range(3):
                for a in range(10):
                    g = wide(k, a, q, e0)
                    for i in range(3):
                        term = nodal[a][i] * g
                        grad[i][k] = term if a == 0 else grad[i][k] + term
            w = qw_ref[q : q + 1, e0 : e0 + LANES]
            wmu = jnp.broadcast_to(w * mu, (8, LANES))
            wlam = jnp.broadcast_to(w * lam, (8, LANES))
            swell = wlam * (grad[0][0] + grad[1][1] + grad[2][2])
            stress = [[None] * 3 for _ in range(3)]
            for i in range(3):
                stress[i][i] = wmu * (grad[i][i] + grad[i][i]) + swell
                for k in range(i):
                    stress[i][k] = wmu * (grad[i][k] + grad[k][i])
                    stress[k][i] = stress[i][k]
            for k in range(3):
                for a in range(10):
                    g = wide(k, a, q, e0)
                    for i in range(3):
                        term = stress[i][k] * g
                        forces[i][a] = term if q + k == 0 else forces[i][a] + term
        done = forces[0][0] * nodal[0][0]
        for a in range(10):
            for i in range(3):
                if a + i > 0:
                    done = done + forces[i][a] * nodal[a][i]
        work = work + jnp.where(row8(high_ref, 0, e0) >= 0, done, 0.0)
        for a in range(10):
            high = row8(high_ref, a, e0)
            parts = [in_two(forces[i][a]) for i in range(3)]
            for h in range(4):
                mask = high == h
                kept = [jnp.where(mask, parts[i][s].astype(F32), 0.0) for s in range(2) for i in range(3)]
                at = e0 * 10 + a * LANES
                left_ref[h * 48 : h * 48 + 48, at : at + LANES] = jnp.concatenate(kept, axis=0).astype(BF16)
    return work


def scatter(left_ref, hot_ref, first, last):
    out = lax.dot_general(
        left_ref[48 * first : 48 * last, :], hot_ref[...], (((1,), (0,)), ((), ())), preferred_element_type=F32
    )
    blocks = []
    for i in range(3):
        blocks.append([])
        for h in range(last - first):
            at = h * 48 + i * 8
            blocks[i] += split_lanes(out[at : at + 8] + out[at + 24 : at + 32])
    return blocks


def splat(value):
    return jnp.broadcast_to(value, (8, LANES))


def lane_sum(values):
    total = values[0]
    for value in values[1:]:
        total = total + value
    return jnp.sum(total, axis=1, keepdims=True)


def setup_kernel(
    count_ref, conn_ref, bids_ref, grads_ref, rhs_ref, d_ref, prec_ref, hot_ref, high_ref, wide_ref, place_ref, start_ref, size_ref
):
    elems = conn_ref.shape[1]
    element = lax.broadcasted_iota(jnp.int32, (10, elems), 1)
    is_live = element < count_ref[0]
    high_ref[...] = jnp.where(is_live, conn_ref[...] >> 8, -1)
    lows = lax.broadcasted_iota(jnp.int32, (LANES, 256), 1)
    padding = jnp.zeros((6, LANES), jnp.int32)
    for e0 in range(0, elems, LANES):
        index = jnp.concatenate([conn_ref[:, e0 : e0 + LANES] & 255, padding], axis=0).T
        for a in range(10):
            at = e0 * 10 + a * LANES
            hot_ref[at : at + LANES, :] = jnp.where(lows == index[:, a : a + 1], 1.0, 0.0).astype(BF16)
    for k in range(3):
        for a in range(10):
            wide_ref[k * 10 + a] = grads_ref[k, a].astype(F32)
    own, ghosts = rhs_ref.shape[1], bids_ref.shape[1]
    listed = jnp.broadcast_to(bids_ref[0:1, :], (8, ghosts)).T[:, 0:1]
    for first in range(0, own, LANES):
        node = first + lax.broadcasted_iota(jnp.int32, (ghosts, LANES), 1)
        entry = lax.broadcasted_iota(jnp.int32, (ghosts, LANES), 0)
        found = jnp.max(jnp.where(listed == node, entry, -1), axis=0, keepdims=True)
        place_ref[:, first : first + LANES] = found
    blocks = [slice(8 * i, 8 * i + 8) for i in range(3)]
    start_ref[...] = splat(lane_sum([p for b in blocks for p in split_lanes(rhs_ref[b, :] * d_ref[b, :])]))
    largest = jnp.abs(prec_ref[0])
    for i in range(1, 3):
        largest = jnp.maximum(largest, jnp.abs(prec_ref[i]))
    size_ref[...] = splat(jnp.max(jnp.max(largest, axis=1, keepdims=True), axis=0, keepdims=True))


def begin_kernel(devices, inputs, p_ref, *rest):
    hbm = rest[:inputs]
    held = rest[inputs : 2 * inputs]
    d_ref, t0_ref, t1_ref, mixed_ref, blocks_ref, sems = rest[2 * inputs :]
    copies = [pltpu.make_async_copy(hbm[k], held[k], sems.at[k]) for k in range(inputs)]
    for copy in copies:
        copy.start()
    for copy in copies[:3]:
        copy.wait()
    rhs_ref, prec_ref, bids_ref = held[:3]
    p = p_ref[0]
    blocks_ref[...] = jnp.zeros_like(blocks_ref)
    for i in range(3):
        d_ref[8 * i : 8 * i + 8, :] = (
            prec_ref[i, 0:1, :] * rhs_ref[0:8, :]
            + prec_ref[i, 1:2, :] * rhs_ref[8:16, :]
            + prec_ref[i, 2:3, :] * rhs_ref[16:24, :]
        )
        for j in range(3):
            blocks_ref[3 * i + j : 3 * i + j + 1, :] = prec_ref[i, j : j + 1, :]
    rows = [split_lanes(d_ref[8 * i : 8 * i + 8, :]) for i in range(3)]
    rows += [split_lanes(blocks_ref[8 * i : 8 * i + 8, :]) for i in range(2)]
    tiles = boundary_values(rows, bids_ref)
    for r in range(5):
        here = slice(8 * r, 8 * r + 8)
        t0_ref[here, :] = tiles[0][r]
        t1_ref[here, :] = tiles[1][r]
        mixed_ref[here, :] = send_mixed(p, devices, tiles[0][r], tiles[1][r])
    for copy in copies[3:]:
        copy.wait()


def first_kernel(
    keys, devices, p_ref, d_ref, bids_ref, size_ref, conn_ref, high_ref, wide_ref, qw_ref, lame_ref, hot_ref, mass_ref, *rest
):
    received = dict(zip(keys, rest[: len(keys)]))
    q_ref, s0_ref, s1_ref, mixed_ref, gprec_ref, scale_ref, dot_ref, left_ref = rest[len(keys) :]
    p = p_ref[0]
    lane = lax.broadcasted_iota(jnp.int32, (8, LANES), 1)
    chunks = []
    for i in range(3):
        ghost = joined(p, devices, received, slice(8 * i, 8 * i + 8), lane, False)
        chunks.append(split_lanes(d_ref[8 * i : 8 * i + 8, :]) + ghost)
    largest = size_ref[...]
    for r in range(2):
        tiles = joined(p, devices, received, slice(24 + 8 * r, 32 + 8 * r), lane, False)
        for t in range(2):
            gprec_ref[8 * r : 8 * r + 8, t * LANES : (t + 1) * LANES] = tiles[t]
            largest = jnp.maximum(largest, jnp.abs(tiles[t]))
    scale_ref[...] = splat(jnp.max(jnp.max(largest, axis=1, keepdims=True), axis=0, keepdims=True))
    work = elements(chunks, conn_ref, high_ref, wide_ref, qw_ref, lame_ref, left_ref)
    acc = scatter(left_ref, hot_ref, 0, 4)
    own_chunks = d_ref.shape[1] // LANES
    mass = mass_rows(mass_ref)
    dots = [work]
    partial = []
    for i in range(3):
        partial.append([])
        for c in range(own_chunks):
            heavy = mass[c] * chunks[i][c]
            partial[i].append(acc[i][c] + heavy)
            dots.append(heavy * chunks[i][c])
    tiles = boundary_values(partial, bids_ref)
    for i in range(3):
        send = [acc[i][own_chunks], acc[i][own_chunks + 1]], [tiles[0][i], tiles[1][i]]
        for part, (tile0, tile1) in enumerate(send):
            here = slice(24 * part + 8 * i, 24 * part + 8 * i + 8)
            s0_ref[here, :] = tile0
            s1_ref[here, :] = tile1
            mixed_ref[here, :] = send_mixed(p, devices, tile0, tile1)
        for c in range(own_chunks):
            q_ref[8 * i : 8 * i + 8, c * LANES : (c + 1) * LANES] = partial[i][c]
    dot_ref[...] = splat(lane_sum(dots))


def mass_rows(mass_ref):
    count = mass_ref.shape[0] // LANES
    return [jnp.broadcast_to(mass_ref[c * LANES : (c + 1) * LANES].reshape(1, LANES), (8, LANES)) for c in range(count)]


WINDOWS = ((1, 0, 64, 0), (4, 0, 48, 1), (16, 96, 112, 1))
WIDTHS = {1: 64, 4: 48, 16: 16}


def second_kernel(
    keys,
    devices,
    p_ref,
    qpart_ref,
    s0_ref,
    s1_ref,
    prec_ref,
    gprec_ref,
    scale_ref,
    start_ref,
    dot_ref,
    place_ref,
    conn_ref,
    high_ref,
    wide_ref,
    qw_ref,
    lame_ref,
    hot_ref,
    mass_ref,
    *rest,
):
    received = dict(zip(keys, rest[: len(keys)]))
    q_ref, s_ref, w_ref, out_ref, left_ref = rest[len(keys) :]
    p = p_ref[0]
    own_chunks = q_ref.shape[1] // LANES
    lane = lax.broadcasted_iota(jnp.int32, (8, LANES), 1)
    case = lax.broadcasted_iota(jnp.int32, (8, LANES), 0)
    back = [joined(p, devices, received, slice(8 * i, 8 * i + 8), lane, True) for i in range(3)]
    for c in range(own_chunks):
        for i, value in enumerate(spread(back, place_ref, c)):
            here = slice(8 * i, 8 * i + 8), slice(c * LANES, (c + 1) * LANES)
            q_ref[here] = qpart_ref[here] + value
    scale = scale_ref[...]
    inverse = (1.0 / scale)[0:1, 0:1]
    ghost_q = []
    for i in range(3):
        tiles = joined(p, devices, received, slice(24 + 8 * i, 32 + 8 * i), lane, False)
        ghost_q.append([s0_ref[8 * i : 8 * i + 8, :] + tiles[0], s1_ref[8 * i : 8 * i + 8, :] + tiles[1]])
    chunks = []
    for i in range(3):
        value = (
            (prec_ref[i, 0:1, :] * inverse) * q_ref[0:8, :]
            + (prec_ref[i, 1:2, :] * inverse) * q_ref[8:16, :]
            + (prec_ref[i, 2:3, :] * inverse) * q_ref[16:24, :]
        )
        s_ref[8 * i : 8 * i + 8, :] = value
        chunks.append(split_lanes(value))
        for t in range(2):
            total = None
            for j in range(3):
                term = (gprec_ref[3 * i + j : 3 * i + j + 1, t * LANES : (t + 1) * LANES] * inverse) * ghost_q[j][t]
                total = term if j == 0 else total + term
            chunks[i].append(total)
    work = elements(chunks, conn_ref, high_ref, wide_ref, qw_ref, lame_ref, left_ref)
    acc = scatter(left_ref, hot_ref, 0, 4)
    ghost = [acc[i][own_chunks:] for i in range(3)]
    mass = mass_rows(mass_ref)
    cross = []
    square = [work]
    for i in range(3):
        for c in range(own_chunks):
            here = slice(8 * i, 8 * i + 8), slice(c * LANES, (c + 1) * LANES)
            heavy = mass[c] * chunks[i][c]
            w_ref[here] = acc[i][c] + heavy
            cross.append(q_ref[here] * chunks[i][c])
            square.append(heavy * chunks[i][c])
    tail = jnp.zeros((8, LANES), F32)
    for k, value in enumerate((start_ref[...], dot_ref[...], splat(lane_sum(cross)), splat(lane_sum(square)))):
        tail = jnp.where(lane == 8 * k + case, value, tail)
    tail = jnp.where(lane[0:1] < 32, jnp.sum(tail, axis=0, keepdims=True), scale[0:1])

    def fill(j, unused):
        for k in range(8):
            out_ref[8 * j + k, 12, :, :] = tail
        return unused

    lax.fori_loop(0, devices // 8, fill, 0)
    for distance, shift_plus, shift_minus, tile in WINDOWS:
        for sign, shift in ((1, shift_plus), (-1, shift_minus)):
            moved = [ghost[i][tile] for i in range(3)]
            if shift:
                moved = [pltpu.roll(m, LANES - shift, 1) for m in moved]
            pair = jnp.where(lane < 64, moved[0], pltpu.roll(moved[1], 64, 1))
            rest = jnp.where(lane < 64, moved[2], pltpu.roll(pltpu.roll(moved[2], 4, 0), 64, 1))
            target = p + sign * distance

            @pl.when((target >= 0) & (target < devices))
            def _():
                out_ref[target, 0:8, 0, :] = pair
                out_ref[target, 8:12, 0, :] = rest[0:4]


def final_kernel(p_ref, in_ref, scale_ref, rhs_ref, d_ref, q_ref, s_ref, wpart_ref, place_ref, x_ref, r_ref):
    p = p_ref[0]
    devices = in_ref.shape[0]
    lane = lax.broadcasted_iota(jnp.int32, (8, LANES), 1)
    case = lax.broadcasted_iota(jnp.int32, (8, LANES), 0)
    mine = scale_ref[...]
    inv_mine = 1.0 / mine
    sums = None
    for j in range(0, devices, 8):
        rows = in_ref[j : j + 8, 12, 0, :]
        ratio = pltpu.roll(rows, LANES - 32, 1) * inv_mine
        rows = rows * jnp.where(lane < 16, 1.0, jnp.where(lane < 24, ratio, ratio * ratio))
        sums = rows if j == 0 else sums + rows
    sums = splat(jnp.sum(sums, axis=0, keepdims=True))
    e0, d0, cross, square = (
        splat(jnp.sum(jnp.where(lane == 8 * k + case, sums, 0.0), axis=1, keepdims=True)) for k in range(4)
    )
    step = e0 / d0
    scaled = step * mine
    fresh = scaled * (step * cross) - e0
    beta = fresh / e0
    more = 1.0 + beta
    bend = more * more * d0 - 2.0 * more * (scaled * cross) + scaled * (scaled * square)
    step1 = fresh / bend
    for_d = step + step1 * more
    for_s = step1 * scaled

    zero = jnp.zeros((8, LANES), F32)
    back = [[zero, zero] for _ in range(3)]
    for distance, shift_plus, shift_minus, tile in WINDOWS:
        for sign, shift in ((1, shift_plus), (-1, shift_minus)):
            source = p - sign * distance
            valid = (source >= 0) & (source < devices)
            source = jnp.clip(source, 0, devices - 1)
            pair = in_ref[source, 0:8, 0, :]
            rest = in_ref[source, 8:12, 0, :]
            rest = jnp.concatenate([rest, pltpu.roll(rest, 64, 1)], axis=0)
            ratio = splat(in_ref[source, 12, :, 32:33]) * inv_mine
            blocks = [pair, pltpu.roll(pair, 64, 1), rest]
            inside = (lane >= shift) & (lane < shift + WIDTHS[distance]) & valid
            for i in range(3):
                moved = blocks[i] if shift == 0 else pltpu.roll(blocks[i], shift, 1)
                back[i][tile] = jnp.where(inside, moved * ratio, back[i][tile])
    for c in range(rhs_ref.shape[1] // LANES):
        for i, value in enumerate(spread(back, place_ref, c)):
            here = slice(8 * i, 8 * i + 8), slice(c * LANES, (c + 1) * LANES)
            x_ref[here] = for_d * d_ref[here] - for_s * s_ref[here]
            r_ref[here] = rhs_ref[here] - for_d * q_ref[here] + for_s * (wpart_ref[here] + value)


def local(
    devices,
    right_side,
    mass_diag,
    precond_blocks,
    connectivity,
    shape_grads,
    quad_weight,
    lame_moduli,
    elem_count,
    boundary_ids,
):
    own = right_side.shape[2]
    elems = connectivity.shape[1]
    p = lax.axis_index(AXIS).astype(jnp.int32).reshape(1)
    rhs = right_side.reshape(24, own)
    bids = boundary_ids.reshape(1, boundary_ids.shape[0])
    grads = jnp.transpose(shape_grads, (1, 2, 0, 3))
    vmem = pl.BlockSpec(memory_space=pltpu.VMEM)
    smem = pl.BlockSpec(memory_space=pltpu.SMEM)
    hbm = pl.BlockSpec(memory_space=pltpu.HBM)
    moves = routes(devices)
    keys = list(moves)

    def shape(*dims, dtype=F32):
        return jax.ShapeDtypeStruct(dims, dtype)

    def call(kernel, out_shape, in_specs, scratch=(), cost=None):
        return pl.pallas_call(
            kernel,
            out_shape=out_shape,
            in_specs=in_specs,
            out_specs=[vmem] * len(out_shape),
            scratch_shapes=list(scratch),
            cost_estimate=cost,
            compiler_params=pltpu.CompilerParams(vmem_limit_bytes=24 << 20),
        )

    def exchange(tile0, tile1, mixed):
        tiles = {1: tile0, 4: tile1, 16: tile1}
        return [
            lax.ppermute(mixed if key == (4, 1) else tiles[key[0]], AXIS, sorted(moves[key].items())) for key in keys
        ]

    tile = shape(40, LANES)
    inputs = [
        pltpu.with_memory_space_constraint(value, pltpu.HBM)
        for value in (rhs, precond_blocks, bids, connectivity, grads, quad_weight, lame_moduli, mass_diag)
    ]
    *held, d, t0, t1, mixed = call(
        functools.partial(begin_kernel, devices, len(inputs)),
        [shape(*value.shape, dtype=value.dtype) for value in inputs] + [shape(24, own), tile, tile, tile],
        [smem] + [hbm] * len(inputs),
        [pltpu.VMEM((16, own), F32), pltpu.SemaphoreType.DMA((len(inputs),))],
    )(pltpu.with_memory_space_constraint(p, pltpu.SMEM), *inputs)
    rhs, precond_blocks, bids, connectivity, grads, quad_weight, lame_moduli, mass_diag = held
    got = exchange(t0, t1, mixed)
    row = shape(8, LANES)
    hot, high, wide, place, start, size = call(
        setup_kernel,
        [
            shape(10 * elems, 256, dtype=BF16),
            shape(10, elems, dtype=jnp.int32),
            shape(30, 4, elems),
            shape(1, own, dtype=jnp.int32),
            row,
            row,
        ],
        [smem] + [vmem] * 6,
        cost=pl.CostEstimate(flops=20_000_000, bytes_accessed=4_000_000, transcendentals=0),
    )(elem_count, connectivity, bids, grads, rhs, d, precond_blocks)
    mesh_args = (connectivity, high, wide, quad_weight, lame_moduli, hot, mass_diag)
    left = [pltpu.VMEM((192, 10 * elems), BF16)]
    tile = shape(48, LANES)
    qpart, s0, s1, mixed, gprec, scale, dot = call(
        functools.partial(first_kernel, keys, devices),
        [shape(24, own), tile, tile, tile, shape(16, 2 * LANES), row, row],
        [smem] + [vmem] * (10 + len(keys)),
        left,
    )(p, d, bids, size, *mesh_args, *got)
    got = exchange(s0, s1, mixed)
    q, s, wpart, message = call(
        functools.partial(second_kernel, keys, devices),
        [shape(24, own), shape(24, own), shape(24, own), shape(devices, 13, 1, LANES)],
        [smem] + [vmem] * (16 + len(keys)),
        left,
    )(p, qpart, s0, s1, precond_blocks, gprec, scale, start, dot, place, *mesh_args, *got)
    message = lax.all_to_all(message, AXIS, 0, 0, tiled=True)
    x, r = call(final_kernel, [shape(24, own), shape(24, own)], [smem] + [vmem] * 8)(
        p, message, scale, rhs, d, q, s, wpart, place
    )
    return x.reshape(3, CASES, own), r.reshape(3, CASES, own)


def solution(mesh):
    return jax.shard_map(
        functools.partial(local, mesh.shape[AXIS]),
        mesh=mesh,
        in_specs=(
            P(None, None, AXIS),
            P(AXIS),
            P(None, None, AXIS),
            P(None, AXIS),
            P(None, None, None, AXIS),
            P(None, AXIS),
            P(None, AXIS),
            P(AXIS),
            P(AXIS),
        ),
        out_specs=(P(None, None, AXIS), P(None, None, AXIS)),
        check_vma=False,
    )
```

```python
import functools

import jax
import jax.numpy as jnp
from jax import lax
from jax.experimental import pallas as pl
from jax.experimental.pallas import tpu as pltpu
from jax.sharding import PartitionSpec as P

F32 = jnp.float32
BF16 = jnp.bfloat16
AXIS = "dom"
CASES = 8
LANES = 128
DISTANCES = (1, 4, 16)


def routes(devices):
    listed = {}
    for distance in DISTANCES:
        for parity in (0, 1):
            route = {}
            for i in range(devices - distance):
                if (i // distance) % 2 == parity:
                    route[i], route[i + distance] = i + distance, i
            if route:
                for i in range(devices):
                    route.setdefault(i, i ^ 1)
                listed[distance, parity] = route
    last = devices - 1
    listed[1, 1].update({0: 1, 1: 2, 2: 0, last: last - 1, last - 1: last - 2, last - 2: last})
    listed[4, 1].update({2: 1, 1: 0, 0: 3, 3: 2})
    listed[4, 1].update({last - 2: last - 1, last - 1: last, last: last - 3, last - 3: last - 2})
    for route in listed.values():
        assert sorted(route.values()) == list(range(devices))
    return listed


def take_lanes(chunks, index):
    lane = index & (LANES - 1)
    which = index >> 7
    rows = len(chunks)
    picked = [None] * rows
    for c in range(len(chunks[0])):
        mask = which == c
        for r in range(rows):
            moved = jnp.take_along_axis(chunks[r][c], lane, axis=1)
            picked[r] = moved if c == 0 else jnp.where(mask, moved, picked[r])
    return picked


def row8(ref, row, start=0, width=LANES):
    return jnp.broadcast_to(ref[row : row + 1, start : start + width], (8, width))


def split_lanes(value):
    return [value[:, c * LANES : (c + 1) * LANES] for c in range(value.shape[1] // LANES)]


def in_two(value):
    head = value.astype(BF16)
    tail = (value - head.astype(F32)).astype(BF16)
    return head, tail


def joined(p, devices, received, rows, lane, opposite):
    sides = {}
    detour = (p == 1) | (p == devices - 2)
    for distance in DISTANCES:
        even = received[distance, 0][rows, :]
        first = lax.rem(lax.div(p, distance), 2) == 0
        if (distance, 1) in received:
            odd = received[distance, 1][rows, :]
            if distance == 1:
                odd = jnp.where(detour, received[4, 1][rows, :], odd)
        else:
            odd = jnp.zeros_like(even)
        plus = jnp.where(p + distance < devices, jnp.where(first, even, odd), 0.0)
        minus = jnp.where(p - distance >= 0, jnp.where(first, odd, even), 0.0)
        sides[distance] = (minus, plus) if opposite else (plus, minus)
    tile0 = jnp.where(lane < 64, sides[1][0], sides[1][1])
    tile1 = jnp.where(
        lane < 48,
        sides[4][0],
        jnp.where(lane < 96, sides[4][1], jnp.where(lane < 112, sides[16][0], sides[16][1])),
    )
    return [tile0, tile1]


def send_mixed(p, devices, tile0, tile1):
    return jnp.where((p == 2) | (p == devices - 3), tile0, tile1)


def spread(tiles, place_ref, block):
    place = jnp.broadcast_to(place_ref[0:1, block * LANES : (block + 1) * LANES], (8, LANES))
    return [jnp.where(place >= 0, value, 0.0) for value in take_lanes(tiles, place)]


def boundary_values(chunks, bids_ref):
    return [take_lanes(chunks, row8(bids_ref, 0, t * LANES)) for t in range(2)]


def elements(chunks, conn_ref, high_ref, wide_ref, qw_ref, lame_ref, left_ref):
    elems = conn_ref.shape[1]
    work = jnp.zeros((8, LANES), F32)

    def wide(k, a, q, e0):
        return jnp.broadcast_to(wide_ref[k * 10 + a, q : q + 1, e0 : e0 + LANES], (8, LANES))

    for e0 in range(0, elems, LANES):
        nodal = [take_lanes(chunks, row8(conn_ref, a, e0)) for a in range(10)]
        forces = [[None] * 10 for _ in range(3)]
        lam = lame_ref[0:1, e0 : e0 + LANES]
        mu = lame_ref[1:2, e0 : e0 + LANES]
        for q in range(4):
            grad = [[None] * 3 for _ in range(3)]
            for k in range(3):
                for a in range(10):
                    g = wide(k, a, q, e0)
                    for i in range(3):
                        term = nodal[a][i] * g
                        grad[i][k] = term if a == 0 else grad[i][k] + term
            w = qw_ref[q : q + 1, e0 : e0 + LANES]
            wmu = jnp.broadcast_to(w * mu, (8, LANES))
            wlam = jnp.broadcast_to(w * lam, (8, LANES))
            swell = wlam * (grad[0][0] + grad[1][1] + grad[2][2])
            stress = [[None] * 3 for _ in range(3)]
            for i in range(3):
                stress[i][i] = wmu * (grad[i][i] + grad[i][i]) + swell
                for k in range(i):
                    stress[i][k] = wmu * (grad[i][k] + grad[k][i])
                    stress[k][i] = stress[i][k]
            for k in range(3):
                for a in range(10):
                    g = wide(k, a, q, e0)
                    for i in range(3):
                        term = stress[i][k] * g
                        forces[i][a] = term if q + k == 0 else forces[i][a] + term
        done = forces[0][0] * nodal[0][0]
        for a in range(10):
            for i in range(3):
                if a + i > 0:
                    done = done + forces[i][a] * nodal[a][i]
        work = work + jnp.where(row8(high_ref, 0, e0) >= 0, done, 0.0)
        for a in range(10):
            high = row8(high_ref, a, e0)
            parts = [in_two(forces[i][a]) for i in range(3)]
            for h in range(4):
                mask = high == h
                kept = [jnp.where(mask, parts[i][s].astype(F32), 0.0) for s in range(2) for i in range(3)]
                at = e0 * 10 + a * LANES
                left_ref[h * 48 : h * 48 + 48, at : at + LANES] = jnp.concatenate(kept, axis=0).astype(BF16)
    return work


def scatter(left_ref, hot_ref, first, last):
    out = lax.dot_general(
        left_ref[48 * first : 48 * last, :], hot_ref[...], (((1,), (0,)), ((), ())), preferred_element_type=F32
    )
    blocks = []
    for i in range(3):
        blocks.append([])
        for h in range(last - first):
            at = h * 48 + i * 8
            blocks[i] += split_lanes(out[at : at + 8] + out[at + 24 : at + 32])
    return blocks


def splat(value):
    return jnp.broadcast_to(value, (8, LANES))


def lane_sum(values):
    total = values[0]
    for value in values[1:]:
        total = total + value
    return jnp.sum(total, axis=1, keepdims=True)


def setup_kernel(
    count_ref, conn_ref, bids_ref, grads_ref, rhs_ref, d_ref, prec_ref, hot_ref, high_ref, wide_ref, place_ref, start_ref, size_ref
):
    elems = conn_ref.shape[1]
    element = lax.broadcasted_iota(jnp.int32, (10, elems), 1)
    is_live = element < count_ref[0]
    high_ref[...] = jnp.where(is_live, conn_ref[...] >> 8, -1)
    lows = lax.broadcasted_iota(jnp.int32, (LANES, 256), 1)
    padding = jnp.zeros((6, LANES), jnp.int32)
    for e0 in range(0, elems, LANES):
        index = jnp.concatenate([conn_ref[:, e0 : e0 + LANES] & 255, padding], axis=0).T
        for a in range(10):
            at = e0 * 10 + a * LANES
            hot_ref[at : at + LANES, :] = jnp.where(lows == index[:, a : a + 1], 1.0, 0.0).astype(BF16)
    for k in range(3):
        for a in range(10):
            wide_ref[k * 10 + a] = grads_ref[k, a].astype(F32)
    own, ghosts = rhs_ref.shape[1], bids_ref.shape[1]
    listed = jnp.broadcast_to(bids_ref[0:1, :], (8, ghosts)).T[:, 0:1]
    for first in range(0, own, LANES):
        node = first + lax.broadcasted_iota(jnp.int32, (ghosts, LANES), 1)
        entry = lax.broadcasted_iota(jnp.int32, (ghosts, LANES), 0)
        found = jnp.max(jnp.where(listed == node, entry, -1), axis=0, keepdims=True)
        place_ref[:, first : first + LANES] = found
    blocks = [slice(8 * i, 8 * i + 8) for i in range(3)]
    start_ref[...] = splat(lane_sum([p for b in blocks for p in split_lanes(rhs_ref[b, :] * d_ref[b, :])]))
    largest = jnp.abs(prec_ref[0])
    for i in range(1, 3):
        largest = jnp.maximum(largest, jnp.abs(prec_ref[i]))
    size_ref[...] = splat(jnp.max(jnp.max(largest, axis=1, keepdims=True), axis=0, keepdims=True))


def begin_kernel(devices, inputs, p_ref, *rest):
    hbm = rest[:inputs]
    held = rest[inputs : 2 * inputs]
    d_ref, t0_ref, t1_ref, mixed_ref, blocks_ref, sems = rest[2 * inputs :]
    copies = [pltpu.make_async_copy(hbm[k], held[k], sems.at[k]) for k in range(inputs)]
    for copy in copies:
        copy.start()
    for copy in copies[:3]:
        copy.wait()
    rhs_ref, prec_ref, bids_ref = held[:3]
    p = p_ref[0]
    blocks_ref[...] = jnp.zeros_like(blocks_ref)
    for i in range(3):
        d_ref[8 * i : 8 * i + 8, :] = (
            prec_ref[i, 0:1, :] * rhs_ref[0:8, :]
            + prec_ref[i, 1:2, :] * rhs_ref[8:16, :]
            + prec_ref[i, 2:3, :] * rhs_ref[16:24, :]
        )
        for j in range(3):
            blocks_ref[3 * i + j : 3 * i + j + 1, :] = prec_ref[i, j : j + 1, :]
    rows = [split_lanes(d_ref[8 * i : 8 * i + 8, :]) for i in range(3)]
    rows += [split_lanes(blocks_ref[8 * i : 8 * i + 8, :]) for i in range(2)]
    tiles = boundary_values(rows, bids_ref)
    for r in range(5):
        here = slice(8 * r, 8 * r + 8)
        t0_ref[here, :] = tiles[0][r]
        t1_ref[here, :] = tiles[1][r]
        mixed_ref[here, :] = send_mixed(p, devices, tiles[0][r], tiles[1][r])
    for copy in copies[3:]:
        copy.wait()


def first_kernel(
    keys, devices, p_ref, d_ref, bids_ref, size_ref, conn_ref, high_ref, wide_ref, qw_ref, lame_ref, hot_ref, mass_ref, *rest
):
    received = dict(zip(keys, rest[: len(keys)]))
    q_ref, s0_ref, s1_ref, mixed_ref, gprec_ref, scale_ref, dot_ref, left_ref = rest[len(keys) :]
    p = p_ref[0]
    lane = lax.broadcasted_iota(jnp.int32, (8, LANES), 1)
    chunks = []
    for i in range(3):
        ghost = joined(p, devices, received, slice(8 * i, 8 * i + 8), lane, False)
        chunks.append(split_lanes(d_ref[8 * i : 8 * i + 8, :]) + ghost)
    largest = size_ref[...]
    for r in range(2):
        tiles = joined(p, devices, received, slice(24 + 8 * r, 32 + 8 * r), lane, False)
        for t in range(2):
            gprec_ref[8 * r : 8 * r + 8, t * LANES : (t + 1) * LANES] = tiles[t]
            largest = jnp.maximum(largest, jnp.abs(tiles[t]))
    scale_ref[...] = splat(jnp.max(jnp.max(largest, axis=1, keepdims=True), axis=0, keepdims=True))
    work = elements(chunks, conn_ref, high_ref, wide_ref, qw_ref, lame_ref, left_ref)
    acc = scatter(left_ref, hot_ref, 0, 4)
    own_chunks = d_ref.shape[1] // LANES
    mass = mass_rows(mass_ref)
    dots = [work]
    partial = []
    for i in range(3):
        partial.append([])
        for c in range(own_chunks):
            heavy = mass[c] * chunks[i][c]
            partial[i].append(acc[i][c] + heavy)
            dots.append(heavy * chunks[i][c])
    tiles = boundary_values(partial, bids_ref)
    for i in range(3):
        send = [acc[i][own_chunks], acc[i][own_chunks + 1]], [tiles[0][i], tiles[1][i]]
        for part, (tile0, tile1) in enumerate(send):
            here = slice(24 * part + 8 * i, 24 * part + 8 * i + 8)
            s0_ref[here, :] = tile0
            s1_ref[here, :] = tile1
            mixed_ref[here, :] = send_mixed(p, devices, tile0, tile1)
        for c in range(own_chunks):
            q_ref[8 * i : 8 * i + 8, c * LANES : (c + 1) * LANES] = partial[i][c]
    dot_ref[...] = splat(lane_sum(dots))


def mass_rows(mass_ref):
    count = mass_ref.shape[0] // LANES
    return [jnp.broadcast_to(mass_ref[c * LANES : (c + 1) * LANES].reshape(1, LANES), (8, LANES)) for c in range(count)]


WINDOWS = (
    (1, 1, 0, 0, 64),
    (1, -1, 0, 64, 64),
    (4, 1, 1, 0, 48),
    (4, -1, 1, 48, 48),
    (16, 1, 1, 96, 16),
    (16, -1, 1, 112, 16),
)


def second_kernel(
    keys,
    devices,
    p_ref,
    qpart_ref,
    s0_ref,
    s1_ref,
    prec_ref,
    gprec_ref,
    scale_ref,
    start_ref,
    dot_ref,
    place_ref,
    conn_ref,
    high_ref,
    wide_ref,
    qw_ref,
    lame_ref,
    hot_ref,
    mass_ref,
    *rest,
):
    received = dict(zip(keys, rest[: len(keys)]))
    q_ref, s_ref, w_ref, out_ref, left_ref = rest[len(keys) :]
    p = p_ref[0]
    own_chunks = q_ref.shape[1] // LANES
    lane = lax.broadcasted_iota(jnp.int32, (8, LANES), 1)
    back = [joined(p, devices, received, slice(8 * i, 8 * i + 8), lane, True) for i in range(3)]
    for c in range(own_chunks):
        for i, value in enumerate(spread(back, place_ref, c)):
            here = slice(8 * i, 8 * i + 8), slice(c * LANES, (c + 1) * LANES)
            q_ref[here] = qpart_ref[here] + value
    scale = scale_ref[...]
    inverse = (1.0 / scale)[0:1, 0:1]
    ghost_q = []
    for i in range(3):
        tiles = joined(p, devices, received, slice(24 + 8 * i, 32 + 8 * i), lane, False)
        ghost_q.append([s0_ref[8 * i : 8 * i + 8, :] + tiles[0], s1_ref[8 * i : 8 * i + 8, :] + tiles[1]])
    chunks = []
    for i in range(3):
        value = (
            (prec_ref[i, 0:1, :] * inverse) * q_ref[0:8, :]
            + (prec_ref[i, 1:2, :] * inverse) * q_ref[8:16, :]
            + (prec_ref[i, 2:3, :] * inverse) * q_ref[16:24, :]
        )
        s_ref[8 * i : 8 * i + 8, :] = value
        chunks.append(split_lanes(value))
        for t in range(2):
            total = None
            for j in range(3):
                term = (gprec_ref[3 * i + j : 3 * i + j + 1, t * LANES : (t + 1) * LANES] * inverse) * ghost_q[j][t]
                total = term if j == 0 else total + term
            chunks[i].append(total)
    work = elements(chunks, conn_ref, high_ref, wide_ref, qw_ref, lame_ref, left_ref)
    acc = scatter(left_ref, hot_ref, 0, 4)
    ghost = [acc[i][own_chunks:] for i in range(3)]
    mass = mass_rows(mass_ref)
    cross = []
    square = [work]
    for i in range(3):
        for c in range(own_chunks):
            here = slice(8 * i, 8 * i + 8), slice(c * LANES, (c + 1) * LANES)
            heavy = mass[c] * chunks[i][c]
            w_ref[here] = acc[i][c] + heavy
            cross.append(q_ref[here] * chunks[i][c])
            square.append(heavy * chunks[i][c])
    tail = jnp.where(lane < 120, 0.0, scale)
    for k, value in enumerate((start_ref[...], dot_ref[...], splat(lane_sum(cross)), splat(lane_sum(square)))):
        tail = jnp.where(lane == 120 + k, value, tail)

    def fill(j, unused):
        for k in range(8):
            out_ref[8 * j + k] = tail
        return unused

    lax.fori_loop(0, devices // 8, fill, 0)

    def pack(tile, column):
        packed = tail
        for i in range(3):
            shift = (40 * i - column) % LANES
            moved = pltpu.roll(ghost[i][tile], shift, 1) if shift else ghost[i][tile]
            packed = jnp.where((lane >= 40 * i) & (lane < 40 * i + 40), moved, packed)
        return packed

    for distance, sign, tile, column, width in WINDOWS:
        target = p + sign * distance
        direct = pack(tile, column)
        beyond = pack(tile, column + 40) if width > 40 else None

        @pl.when((target >= 0) & (target < devices))
        def _():
            out_ref[target] = direct
            if beyond is not None:
                out_ref[jnp.bitwise_xor(target, 1)] = beyond


def unpacked(in_ref, owner, devices, lane, inverse, direct):
    back = [[jnp.zeros((8, LANES), F32) for _ in range(2)] for _ in range(3)]
    for distance, sign, tile, column, width in WINDOWS:
        first, size = (column, min(width, 40)) if direct else (column + 40, width - 40)
        if size <= 0:
            continue
        source = owner - sign * distance
        valid = (source >= 0) & (source < devices)
        block = in_ref[jnp.clip(source, 0, devices - 1)]
        ratio = splat(block[:, 124:125]) * inverse
        inside = (lane >= first) & (lane < first + size) & valid
        for i in range(3):
            shift = (first - 40 * i) % LANES
            moved = pltpu.roll(block, shift, 1) if shift else block
            back[i][tile] = jnp.where(inside, moved * ratio, back[i][tile])
    return [back[i][t] for t in range(2) for i in range(3)]


def relay_kernel(p_ref, in_ref, out_ref):
    devices = in_ref.shape[0]
    lane = lax.broadcasted_iota(jnp.int32, (8, LANES), 1)
    owner = jnp.bitwise_xor(p_ref[0], 1)
    inverse = 1.0 / splat(in_ref[owner][:, 124:125])
    for k, block in enumerate(unpacked(in_ref, owner, devices, lane, inverse, False)):
        out_ref[8 * k : 8 * k + 8, :] = block


def scalar_kernel(p_ref, in_ref, scale_ref, out_ref):
    devices = in_ref.shape[0]
    lane = lax.broadcasted_iota(jnp.int32, (8, LANES), 1)
    mine = scale_ref[...]
    inv_mine = 1.0 / mine
    for k, block in enumerate(unpacked(in_ref, p_ref[0], devices, lane, inv_mine, True)):
        out_ref[8 * k : 8 * k + 8, :] = block

    def term(j):
        tile = in_ref[j]
        ratio = pltpu.roll(tile, LANES - 4, 1) * inv_mine
        return tile * jnp.where(lane == 122, ratio, jnp.where(lane == 123, ratio * ratio, 1.0))

    def add_up(j, sums):
        values = [term(8 * j + k) for k in range(8)]
        while len(values) > 1:
            values = [a + b for a, b in zip(values[::2], values[1::2])]
        return sums + values[0]

    sums = lax.fori_loop(0, devices // 8, add_up, jnp.zeros((8, LANES), F32), unroll=devices <= 64)
    e0, d0, cross, square = (splat(sums[:, k : k + 1]) for k in range(120, 124))
    step = e0 / d0
    scaled = step * mine
    fresh = scaled * (step * cross) - e0
    beta = fresh / e0
    more = 1.0 + beta
    bend = more * more * d0 - 2.0 * more * (scaled * cross) + scaled * (scaled * square)
    step1 = fresh / bend
    out_ref[48:56, :] = step + step1 * more
    out_ref[56:64, :] = step1 * scaled


def final_kernel(direct_ref, relayed_ref, rhs_ref, d_ref, q_ref, s_ref, wpart_ref, place_ref, x_ref, r_ref):
    lane = lax.broadcasted_iota(jnp.int32, (8, LANES), 1)
    for_d = direct_ref[48:56, :]
    for_s = direct_ref[56:64, :]
    back = [[None, None] for _ in range(3)]
    for t in range(2):
        far = lane < 0
        for _, _, tile, column, width in WINDOWS:
            if tile == t:
                far = far | ((lane >= column + 40) & (lane < column + width))
        for i in range(3):
            here = slice(24 * t + 8 * i, 24 * t + 8 * i + 8)
            back[i][t] = jnp.where(far, relayed_ref[here, :], direct_ref[here, :])
    for c in range(rhs_ref.shape[1] // LANES):
        for i, value in enumerate(spread(back, place_ref, c)):
            here = slice(8 * i, 8 * i + 8), slice(c * LANES, (c + 1) * LANES)
            x_ref[here] = for_d * d_ref[here] - for_s * s_ref[here]
            r_ref[here] = rhs_ref[here] - for_d * q_ref[here] + for_s * (wpart_ref[here] + value)


def local(
    devices,
    right_side,
    mass_diag,
    precond_blocks,
    connectivity,
    shape_grads,
    quad_weight,
    lame_moduli,
    elem_count,
    boundary_ids,
):
    own = right_side.shape[2]
    elems = connectivity.shape[1]
    p = lax.axis_index(AXIS).astype(jnp.int32).reshape(1)
    rhs = right_side.reshape(24, own)
    bids = boundary_ids.reshape(1, boundary_ids.shape[0])
    grads = jnp.transpose(shape_grads, (1, 2, 0, 3))
    vmem = pl.BlockSpec(memory_space=pltpu.VMEM)
    smem = pl.BlockSpec(memory_space=pltpu.SMEM)
    hbm = pl.BlockSpec(memory_space=pltpu.HBM)
    moves = routes(devices)
    keys = list(moves)

    def shape(*dims, dtype=F32):
        return jax.ShapeDtypeStruct(dims, dtype)

    def call(kernel, out_shape, in_specs, scratch=(), cost=None):
        return pl.pallas_call(
            kernel,
            out_shape=out_shape,
            in_specs=in_specs,
            out_specs=[vmem] * len(out_shape),
            scratch_shapes=list(scratch),
            cost_estimate=cost,
            compiler_params=pltpu.CompilerParams(vmem_limit_bytes=24 << 20),
        )

    def exchange(tile0, tile1, mixed):
        tiles = {1: tile0, 4: tile1, 16: tile1}
        return [
            lax.ppermute(mixed if key == (4, 1) else tiles[key[0]], AXIS, sorted(moves[key].items())) for key in keys
        ]

    tile = shape(40, LANES)
    inputs = [
        pltpu.with_memory_space_constraint(value, pltpu.HBM)
        for value in (rhs, precond_blocks, bids, connectivity, grads, quad_weight, lame_moduli, mass_diag)
    ]
    *held, d, t0, t1, mixed = call(
        functools.partial(begin_kernel, devices, len(inputs)),
        [shape(*value.shape, dtype=value.dtype) for value in inputs] + [shape(24, own), tile, tile, tile],
        [smem] + [hbm] * len(inputs),
        [pltpu.VMEM((16, own), F32), pltpu.SemaphoreType.DMA((len(inputs),))],
    )(pltpu.with_memory_space_constraint(p, pltpu.SMEM), *inputs)
    rhs, precond_blocks, bids, connectivity, grads, quad_weight, lame_moduli, mass_diag = held
    got = exchange(t0, t1, mixed)
    row = shape(8, LANES)
    hot, high, wide, place, start, size = call(
        setup_kernel,
        [
            shape(10 * elems, 256, dtype=BF16),
            shape(10, elems, dtype=jnp.int32),
            shape(30, 4, elems),
            shape(1, own, dtype=jnp.int32),
            row,
            row,
        ],
        [smem] + [vmem] * 6,
        cost=pl.CostEstimate(flops=20_000_000, bytes_accessed=4_000_000, transcendentals=0),
    )(elem_count, connectivity, bids, grads, rhs, d, precond_blocks)
    mesh_args = (connectivity, high, wide, quad_weight, lame_moduli, hot, mass_diag)
    left = [pltpu.VMEM((192, 10 * elems), BF16)]
    tile = shape(48, LANES)
    qpart, s0, s1, mixed, gprec, scale, dot = call(
        functools.partial(first_kernel, keys, devices),
        [shape(24, own), tile, tile, tile, shape(16, 2 * LANES), row, row],
        [smem] + [vmem] * (10 + len(keys)),
        left,
    )(p, d, bids, size, *mesh_args, *got)
    got = exchange(s0, s1, mixed)
    q, s, wpart, message = call(
        functools.partial(second_kernel, keys, devices),
        [shape(24, own), shape(24, own), shape(24, own), shape(devices, 8, LANES)],
        [smem] + [vmem] * (16 + len(keys)),
        left,
    )(p, qpart, s0, s1, precond_blocks, gprec, scale, start, dot, place, *mesh_args, *got)
    message = lax.all_to_all(message, AXIS, 0, 0, tiled=True)
    (relay,) = call(relay_kernel, [tile], [smem, vmem])(p, message)
    relayed = lax.ppermute(relay, AXIS, [(i, i ^ 1) for i in range(devices)])
    (direct,) = call(
        scalar_kernel,
        [shape(64, LANES)],
        [smem] + [vmem] * 2,
        cost=pl.CostEstimate(flops=20_000_000, bytes_accessed=2_000_000, transcendentals=0),
    )(p, message, scale)
    x, r = call(final_kernel, [shape(24, own), shape(24, own)], [vmem] * 8)(
        direct, relayed, rhs, d, q, s, wpart, place
    )
    return x.reshape(3, CASES, own), r.reshape(3, CASES, own)


def solution(mesh):
    return jax.shard_map(
        functools.partial(local, mesh.shape[AXIS]),
        mesh=mesh,
        in_specs=(
            P(None, None, AXIS),
            P(AXIS),
            P(None, None, AXIS),
            P(None, AXIS),
            P(None, None, None, AXIS),
            P(None, AXIS),
            P(None, AXIS),
            P(AXIS),
            P(AXIS),
        ),
        out_specs=(P(None, None, AXIS), P(None, None, AXIS)),
        check_vma=False,
    )
```

```python
import functools

import jax
import jax.numpy as jnp
from jax import lax
from jax.experimental import pallas as pl
from jax.experimental.pallas import tpu as pltpu
from jax.sharding import PartitionSpec as P

F32 = jnp.float32
BF16 = jnp.bfloat16
AXIS = "dom"
CASES = 8
LANES = 128
DISTANCES = (1, 4, 16)


def routes(devices):
    listed = {}
    for distance in DISTANCES:
        for parity in (0, 1):
            route = {}
            for i in range(devices - distance):
                if (i // distance) % 2 == parity:
                    route[i], route[i + distance] = i + distance, i
            if route:
                for i in range(devices):
                    route.setdefault(i, i ^ 1)
                listed[distance, parity] = route
    last = devices - 1
    listed[1, 1].update({0: 1, 1: 2, 2: 0, last: last - 1, last - 1: last - 2, last - 2: last})
    listed[4, 1].update({2: 1, 1: 0, 0: 3, 3: 2})
    listed[4, 1].update({last - 2: last - 1, last - 1: last, last: last - 3, last - 3: last - 2})
    for route in listed.values():
        assert sorted(route.values()) == list(range(devices))
    return listed


def take_lanes(chunks, index):
    lane = index & (LANES - 1)
    which = index >> 7
    rows = len(chunks)
    picked = [None] * rows
    for c in range(len(chunks[0])):
        mask = which == c
        for r in range(rows):
            moved = jnp.take_along_axis(chunks[r][c], lane, axis=1)
            picked[r] = moved if c == 0 else jnp.where(mask, moved, picked[r])
    return picked


def row8(ref, row, start=0, width=LANES):
    return jnp.broadcast_to(ref[row : row + 1, start : start + width], (8, width))


def split_lanes(value):
    return [value[:, c * LANES : (c + 1) * LANES] for c in range(value.shape[1] // LANES)]


def in_two(value):
    head = value.astype(BF16)
    tail = (value - head.astype(F32)).astype(BF16)
    return head, tail


def plus_lanes(lane):
    return [lane < 64, (lane < 48) | ((lane >= 96) & (lane < 112))]


def pack_far(blocks, lane):
    packed = jnp.zeros((8, LANES), F32)
    for r, block in enumerate(blocks):
        moved = pltpu.roll(block, (32 * r - 96) % LANES, 1)
        packed = jnp.where((lane >= 32 * r) & (lane < 32 * r + 32), moved, packed)
    return packed


def joined(p, devices, received, block, lane):
    def arrived(key):
        if key[0] == 16:
            shift = (96 - 32 * block) % LANES
            return pltpu.roll(received[key][0:8, :], shift, 1) if shift else received[key][0:8, :]
        return received[key][8 * block : 8 * block + 8, :]

    sides = {}
    detour = (p == 1) | (p == devices - 2)
    for distance in DISTANCES:
        even = arrived((distance, 0))
        first = lax.rem(lax.div(p, distance), 2) == 0
        if (distance, 1) in received:
            odd = arrived((distance, 1))
            if distance == 1:
                odd = jnp.where(detour, arrived((4, 1)), odd)
        else:
            odd = jnp.zeros_like(even)
        plus = jnp.where(p + distance < devices, jnp.where(first, even, odd), 0.0)
        minus = jnp.where(p - distance >= 0, jnp.where(first, odd, even), 0.0)
        sides[distance] = plus, minus
    tiles = []
    for a, b in ((0, 1), (1, 0)):
        tile1 = jnp.where(
            lane < 48,
            sides[4][a],
            jnp.where(lane < 96, sides[4][b], jnp.where(lane < 112, sides[16][a], sides[16][b])),
        )
        tiles.append([jnp.where(lane < 64, sides[1][a], sides[1][b]), tile1])
    return tiles


def send_mixed(p, devices, tile0, tile1):
    return jnp.where((p == 2) | (p == devices - 3), tile0, tile1)


def spread(tiles, place_ref, block):
    place = jnp.broadcast_to(place_ref[0:1, block * LANES : (block + 1) * LANES], (8, LANES))
    return [jnp.where(place >= 0, value, 0.0) for value in take_lanes(tiles, place)]


def boundary_values(chunks, bids_ref):
    return [take_lanes(chunks, row8(bids_ref, 0, t * LANES)) for t in range(2)]


def elements(chunks, count, conn_ref, high_ref, wide_ref, qw_ref, lame_ref, hot_ref, held_ref, left_ref, sum_ref, work_ref):
    elems = conn_ref.shape[1]
    for i in range(3):
        for c, value in enumerate(chunks[i]):
            held_ref[8 * i : 8 * i + 8, c * LANES : (c + 1) * LANES] = value

    def wide(k, a, q, e0):
        return jnp.broadcast_to(wide_ref[k * 10 + a, q : q + 1, e0 : e0 + LANES], (8, LANES))

    def block(e0):
        held = [split_lanes(held_ref[8 * i : 8 * i + 8, :]) for i in range(3)] if e0 else chunks
        nodal = [take_lanes(held, row8(conn_ref, a, e0)) for a in range(10)]
        forces = [[None] * 10 for _ in range(3)]
        lam = lame_ref[0:1, e0 : e0 + LANES]
        mu = lame_ref[1:2, e0 : e0 + LANES]
        for q in range(4):
            grad = [[None] * 3 for _ in range(3)]
            for k in range(3):
                for a in range(10):
                    g = wide(k, a, q, e0)
                    for i in range(3):
                        term = nodal[a][i] * g
                        grad[i][k] = term if a == 0 else grad[i][k] + term
            w = qw_ref[q : q + 1, e0 : e0 + LANES]
            wmu = jnp.broadcast_to(w * mu, (8, LANES))
            wlam = jnp.broadcast_to(w * lam, (8, LANES))
            swell = wlam * (grad[0][0] + grad[1][1] + grad[2][2])
            stress = [[None] * 3 for _ in range(3)]
            for i in range(3):
                stress[i][i] = wmu * (grad[i][i] + grad[i][i]) + swell
                for k in range(i):
                    stress[i][k] = wmu * (grad[i][k] + grad[k][i])
                    stress[k][i] = stress[i][k]
            for k in range(3):
                for a in range(10):
                    g = wide(k, a, q, e0)
                    for i in range(3):
                        term = stress[i][k] * g
                        forces[i][a] = term if q + k == 0 else forces[i][a] + term
        done = forces[0][0] * nodal[0][0]
        for a in range(10):
            for i in range(3):
                if a + i > 0:
                    done = done + forces[i][a] * nodal[a][i]
        done = jnp.where(row8(high_ref, 0, e0) >= 0, done, 0.0)
        for a in range(10):
            high = row8(high_ref, a, e0)
            parts = [in_two(forces[i][a]) for i in range(3)]
            for h in range(4):
                mask = high == h
                kept = [jnp.where(mask, parts[i][s].astype(F32), 0.0) for s in range(2) for i in range(3)]
                left_ref[h * 48 : h * 48 + 48, a * LANES : (a + 1) * LANES] = jnp.concatenate(kept, axis=0).astype(
                    BF16
                )
        added = lax.dot_general(
            left_ref[...],
            hot_ref[e0 * 10 : (e0 + LANES) * 10, :],
            (((1,), (0,)), ((), ())),
            preferred_element_type=F32,
        )
        sum_ref[...] = sum_ref[...] + added if e0 else added
        work_ref[...] = work_ref[...] + done if e0 else done

    block(0)
    for e0 in range(LANES, elems, LANES):
        pl.when(e0 < count)(functools.partial(block, e0))


def node_sums(sum_ref):
    out = sum_ref[...]
    blocks = []
    for i in range(3):
        blocks.append([])
        for h in range(4):
            at = h * 48 + i * 8
            blocks[i] += split_lanes(out[at : at + 8] + out[at + 24 : at + 32])
    return blocks


def splat(value):
    return jnp.broadcast_to(value, (8, LANES))


def lane_sum(values):
    total = values[0]
    for value in values[1:]:
        total = total + value
    return jnp.sum(total, axis=1, keepdims=True)


def setup_kernel(
    count_ref, conn_ref, bids_ref, grads_ref, rhs_ref, d_ref, prec_ref, hot_ref, high_ref, wide_ref, place_ref, start_ref, size_ref
):
    elems = conn_ref.shape[1]
    element = lax.broadcasted_iota(jnp.int32, (10, elems), 1)
    is_live = element < count_ref[0]
    high_ref[...] = jnp.where(is_live, conn_ref[...] >> 8, -1)
    lows = lax.broadcasted_iota(jnp.int32, (LANES, 256), 1)
    padding = jnp.zeros((6, LANES), jnp.int32)
    for e0 in range(0, elems, LANES):
        index = jnp.concatenate([conn_ref[:, e0 : e0 + LANES] & 255, padding], axis=0).T
        for a in range(10):
            at = e0 * 10 + a * LANES
            hot_ref[at : at + LANES, :] = jnp.where(lows == index[:, a : a + 1], 1.0, 0.0).astype(BF16)
    for k in range(3):
        for a in range(10):
            wide_ref[k * 10 + a] = grads_ref[k, a].astype(F32)
    own, ghosts = rhs_ref.shape[1], bids_ref.shape[1]
    listed = jnp.broadcast_to(bids_ref[0:1, :], (8, ghosts)).T[:, 0:1]
    for first in range(0, own, LANES):
        node = first + lax.broadcasted_iota(jnp.int32, (ghosts, LANES), 1)
        entry = lax.broadcasted_iota(jnp.int32, (ghosts, LANES), 0)
        found = jnp.max(jnp.where(listed == node, entry, -1), axis=0, keepdims=True)
        place_ref[:, first : first + LANES] = found
    blocks = [slice(8 * i, 8 * i + 8) for i in range(3)]
    start_ref[...] = splat(lane_sum([p for b in blocks for p in split_lanes(rhs_ref[b, :] * d_ref[b, :])]))
    largest = jnp.abs(prec_ref[0])
    for i in range(1, 3):
        largest = jnp.maximum(largest, jnp.abs(prec_ref[i]))
    size_ref[...] = splat(jnp.max(jnp.max(largest, axis=1, keepdims=True), axis=0, keepdims=True))


def entry(i, j):
    return (0, 1, 2, 1, 3, 4, 2, 4, 5)[3 * i + j]


def begin_kernel(devices, inputs, p_ref, *rest):
    hbm = rest[:inputs]
    held = rest[inputs : 2 * inputs]
    d_ref, t0_ref, t1_ref, mixed_ref, far_ref, blocks_ref, sems = rest[2 * inputs :]
    copies = [pltpu.make_async_copy(hbm[k], held[k], sems.at[k]) for k in range(inputs)]
    for copy in copies:
        copy.start()
    for copy in copies[:3]:
        copy.wait()
    rhs_ref, prec_ref, bids_ref = held[:3]
    p = p_ref[0]
    blocks_ref[...] = jnp.zeros_like(blocks_ref)
    for i in range(3):
        d_ref[8 * i : 8 * i + 8, :] = (
            prec_ref[i, 0:1, :] * rhs_ref[0:8, :]
            + prec_ref[i, 1:2, :] * rhs_ref[8:16, :]
            + prec_ref[i, 2:3, :] * rhs_ref[16:24, :]
        )
        for j in range(i, 3):
            k = entry(i, j)
            blocks_ref[k : k + 1, :] = prec_ref[i, j : j + 1, :]
    rows = [split_lanes(d_ref[8 * i : 8 * i + 8, :]) for i in range(3)]
    rows.append(split_lanes(blocks_ref[...]))
    tiles = boundary_values(rows, bids_ref)
    far_ref[...] = jnp.zeros_like(far_ref)
    far_ref[0:8, :] = pack_far(tiles[1], lax.broadcasted_iota(jnp.int32, (8, LANES), 1))
    for r in range(4):
        here = slice(8 * r, 8 * r + 8)
        t0_ref[here, :] = tiles[0][r]
        t1_ref[here, :] = tiles[1][r]
        mixed_ref[here, :] = send_mixed(p, devices, tiles[0][r], tiles[1][r])
    for copy in copies[3:]:
        copy.wait()


def first_kernel(
    keys, devices, p_ref, count_ref, d_ref, bids_ref, size_ref, conn_ref, high_ref, wide_ref, qw_ref, lame_ref, hot_ref, mass_ref, *rest
):
    received = dict(zip(keys, rest[: len(keys)]))
    q_ref, ghost_ref, gprec_ref, scale_ref, dot_ref, *send = rest[len(keys) : -4]
    scratch = rest[-4:]
    send = dict(zip(keys, send))
    p = p_ref[0]
    lane = lax.broadcasted_iota(jnp.int32, (8, LANES), 1)
    chunks = []
    for i in range(3):
        chunks.append(split_lanes(d_ref[8 * i : 8 * i + 8, :]) + joined(p, devices, received, i, lane)[0])
    largest = size_ref[...]
    for t, tile in enumerate(joined(p, devices, received, 3, lane)[0]):
        gprec_ref[:, t * LANES : (t + 1) * LANES] = tile
        largest = jnp.maximum(largest, jnp.abs(tile))
    scale_ref[...] = splat(jnp.max(jnp.max(largest, axis=1, keepdims=True), axis=0, keepdims=True))
    elements(chunks, count_ref[0], conn_ref, high_ref, wide_ref, qw_ref, lame_ref, hot_ref, *scratch)
    acc = node_sums(scratch[2])
    work = scratch[3][...]
    own_chunks = d_ref.shape[1] // LANES
    mass = mass_rows(mass_ref)
    dots = [work]
    partial = []
    for i in range(3):
        partial.append([])
        for c in range(own_chunks):
            heavy = mass[c] * chunks[i][c]
            partial[i].append(acc[i][c] + heavy)
            dots.append(heavy * chunks[i][c])
    tiles = boundary_values(partial, bids_ref)
    higher = plus_lanes(lane)
    message = {}
    for key in keys:
        distance, parity = key
        t = 0 if distance == 1 else 1
        first = lax.rem(lax.div(p, distance), 2) == parity
        message[key] = []
        for i in range(3):
            mine, theirs = acc[i][own_chunks + t], tiles[t][i]
            upward = jnp.where(higher[t], mine, theirs)
            downward = jnp.where(higher[t], theirs, mine)
            message[key].append(jnp.where(first, upward, downward))
    message[4, 1] = [send_mixed(p, devices, a, b) for a, b in zip(message[1, 1], message[4, 1])]
    for key in keys:
        if key[0] == 16:
            send[key][...] = jnp.zeros_like(send[key])
            send[key][0:8, :] = pack_far(message[key], lane)
            continue
        for i in range(3):
            send[key][8 * i : 8 * i + 8, :] = message[key][i]
    for i in range(3):
        for t in range(2):
            here = slice(24 * t + 8 * i, 24 * t + 8 * i + 8)
            ghost_ref[here, :] = acc[i][own_chunks + t]
        for c in range(own_chunks):
            q_ref[8 * i : 8 * i + 8, c * LANES : (c + 1) * LANES] = partial[i][c]
    dot_ref[...] = splat(lane_sum(dots))


def mass_rows(mass_ref):
    count = mass_ref.shape[0] // LANES
    return [jnp.broadcast_to(mass_ref[c * LANES : (c + 1) * LANES].reshape(1, LANES), (8, LANES)) for c in range(count)]


WINDOWS = (
    (1, 1, 0, 0, 64),
    (1, -1, 0, 64, 64),
    (4, 1, 1, 0, 48),
    (4, -1, 1, 48, 48),
    (16, 1, 1, 96, 16),
    (16, -1, 1, 112, 16),
)


def second_kernel(
    keys,
    devices,
    p_ref,
    count_ref,
    qpart_ref,
    ghost_ref,
    prec_ref,
    gprec_ref,
    scale_ref,
    start_ref,
    dot_ref,
    place_ref,
    conn_ref,
    high_ref,
    wide_ref,
    qw_ref,
    lame_ref,
    hot_ref,
    mass_ref,
    *rest,
):
    received = dict(zip(keys, rest[: len(keys)]))
    q_ref, s_ref, w_ref, out_ref, *scratch = rest[len(keys) :]
    p = p_ref[0]
    own_chunks = q_ref.shape[1] // LANES
    lane = lax.broadcasted_iota(jnp.int32, (8, LANES), 1)
    swapped = [joined(p, devices, received, i, lane) for i in range(3)]
    back = [both[1] for both in swapped]
    for c in range(own_chunks):
        for i, value in enumerate(spread(back, place_ref, c)):
            here = slice(8 * i, 8 * i + 8), slice(c * LANES, (c + 1) * LANES)
            q_ref[here] = qpart_ref[here] + value
    scale = scale_ref[...]
    inverse = (1.0 / scale)[0:1, 0:1]
    ghost_q = []
    for i in range(3):
        ghost_q.append(
            [ghost_ref[24 * t + 8 * i : 24 * t + 8 * i + 8, :] + swapped[i][0][t] for t in range(2)]
        )
    chunks = []
    for i in range(3):
        value = (
            (prec_ref[i, 0:1, :] * inverse) * q_ref[0:8, :]
            + (prec_ref[i, 1:2, :] * inverse) * q_ref[8:16, :]
            + (prec_ref[i, 2:3, :] * inverse) * q_ref[16:24, :]
        )
        s_ref[8 * i : 8 * i + 8, :] = value
        chunks.append(split_lanes(value))
        for t in range(2):
            total = None
            for j in range(3):
                k = entry(i, j)
                term = (gprec_ref[k : k + 1, t * LANES : (t + 1) * LANES] * inverse) * ghost_q[j][t]
                total = term if j == 0 else total + term
            chunks[i].append(total)
    elements(chunks, count_ref[0], conn_ref, high_ref, wide_ref, qw_ref, lame_ref, hot_ref, *scratch)
    acc = node_sums(scratch[2])
    work = scratch[3][...]
    ghost = [acc[i][own_chunks:] for i in range(3)]
    mass = mass_rows(mass_ref)
    cross = []
    square = [work]
    for i in range(3):
        for c in range(own_chunks):
            here = slice(8 * i, 8 * i + 8), slice(c * LANES, (c + 1) * LANES)
            heavy = mass[c] * chunks[i][c]
            w_ref[here] = acc[i][c] + heavy
            cross.append(q_ref[here] * chunks[i][c])
            square.append(heavy * chunks[i][c])
    tail = jnp.where(lane < 120, 0.0, scale)
    for k, value in enumerate((start_ref[...], dot_ref[...], splat(lane_sum(cross)), splat(lane_sum(square)))):
        tail = jnp.where(lane == 120 + k, value, tail)

    def fill(j, unused):
        for k in range(8):
            out_ref[8 * j + k] = tail
        return unused

    lax.fori_loop(0, devices // 8, fill, 0)

    def pack(tile, column):
        packed = tail
        for i in range(3):
            shift = (40 * i - column) % LANES
            moved = pltpu.roll(ghost[i][tile], shift, 1) if shift else ghost[i][tile]
            packed = jnp.where((lane >= 40 * i) & (lane < 40 * i + 40), moved, packed)
        return packed

    for distance, sign, tile, column, width in WINDOWS:
        target = p + sign * distance
        direct = pack(tile, column)
        beyond = pack(tile, column + 40) if width > 40 else None

        @pl.when((target >= 0) & (target < devices))
        def _():
            out_ref[target] = direct
            if beyond is not None:
                out_ref[jnp.bitwise_xor(target, 1)] = beyond


def unpacked(in_ref, owner, devices, lane, inverse, direct):
    back = [[jnp.zeros((8, LANES), F32) for _ in range(2)] for _ in range(3)]
    for distance, sign, tile, column, width in WINDOWS:
        first, size = (column, min(width, 40)) if direct else (column + 40, width - 40)
        if size <= 0:
            continue
        source = owner - sign * distance
        valid = (source >= 0) & (source < devices)
        block = in_ref[jnp.clip(source, 0, devices - 1)]
        ratio = splat(block[:, 124:125]) * inverse
        inside = (lane >= first) & (lane < first + size) & valid
        for i in range(3):
            shift = (first - 40 * i) % LANES
            moved = pltpu.roll(block, shift, 1) if shift else block
            back[i][tile] = jnp.where(inside, moved * ratio, back[i][tile])
    return [back[i][t] for t in range(2) for i in range(3)]


def relay_kernel(p_ref, in_ref, out_ref):
    devices = in_ref.shape[0]
    lane = lax.broadcasted_iota(jnp.int32, (8, LANES), 1)
    owner = jnp.bitwise_xor(p_ref[0], 1)
    inverse = 1.0 / splat(in_ref[owner][:, 124:125])
    for k, block in enumerate(unpacked(in_ref, owner, devices, lane, inverse, False)):
        out_ref[8 * k : 8 * k + 8, :] = block


def scalar_kernel(p_ref, in_ref, scale_ref, out_ref):
    devices = in_ref.shape[0]
    lane = lax.broadcasted_iota(jnp.int32, (8, LANES), 1)
    mine = scale_ref[...]
    inv_mine = 1.0 / mine
    for k, block in enumerate(unpacked(in_ref, p_ref[0], devices, lane, inv_mine, True)):
        out_ref[8 * k : 8 * k + 8, :] = block

    def term(j):
        tile = in_ref[j]
        ratio = pltpu.roll(tile, LANES - 4, 1) * inv_mine
        return tile * jnp.where(lane == 122, ratio, jnp.where(lane == 123, ratio * ratio, 1.0))

    def add_up(j, sums):
        values = [term(8 * j + k) for k in range(8)]
        while len(values) > 1:
            values = [a + b for a, b in zip(values[::2], values[1::2])]
        return sums + values[0]

    sums = lax.fori_loop(0, devices // 8, add_up, jnp.zeros((8, LANES), F32), unroll=devices <= 64)
    e0, d0, cross, square = (splat(sums[:, k : k + 1]) for k in range(120, 124))
    step = e0 / d0
    scaled = step * mine
    fresh = scaled * (step * cross) - e0
    beta = fresh / e0
    more = 1.0 + beta
    bend = more * more * d0 - 2.0 * more * (scaled * cross) + scaled * (scaled * square)
    step1 = fresh / bend
    out_ref[48:56, :] = step + step1 * more
    out_ref[56:64, :] = step1 * scaled


def final_kernel(direct_ref, relayed_ref, rhs_ref, d_ref, q_ref, s_ref, wpart_ref, place_ref, x_ref, r_ref):
    lane = lax.broadcasted_iota(jnp.int32, (8, LANES), 1)
    for_d = direct_ref[48:56, :]
    for_s = direct_ref[56:64, :]
    back = [[None, None] for _ in range(3)]
    for t in range(2):
        far = lane < 0
        for _, _, tile, column, width in WINDOWS:
            if tile == t:
                far = far | ((lane >= column + 40) & (lane < column + width))
        for i in range(3):
            here = slice(24 * t + 8 * i, 24 * t + 8 * i + 8)
            back[i][t] = jnp.where(far, relayed_ref[here, :], direct_ref[here, :])
    for c in range(rhs_ref.shape[1] // LANES):
        for i, value in enumerate(spread(back, place_ref, c)):
            here = slice(8 * i, 8 * i + 8), slice(c * LANES, (c + 1) * LANES)
            x_ref[here] = for_d * d_ref[here] - for_s * s_ref[here]
            r_ref[here] = rhs_ref[here] - for_d * q_ref[here] + for_s * (wpart_ref[here] + value)


def local(
    devices,
    right_side,
    mass_diag,
    precond_blocks,
    connectivity,
    shape_grads,
    quad_weight,
    lame_moduli,
    elem_count,
    boundary_ids,
):
    own = right_side.shape[2]
    elems = connectivity.shape[1]
    p = lax.axis_index(AXIS).astype(jnp.int32).reshape(1)
    rhs = right_side.reshape(24, own)
    bids = boundary_ids.reshape(1, boundary_ids.shape[0])
    grads = jnp.transpose(shape_grads, (1, 2, 0, 3))
    vmem = pl.BlockSpec(memory_space=pltpu.VMEM)
    smem = pl.BlockSpec(memory_space=pltpu.SMEM)
    hbm = pl.BlockSpec(memory_space=pltpu.HBM)
    moves = routes(devices)
    keys = list(moves)

    def shape(*dims, dtype=F32):
        return jax.ShapeDtypeStruct(dims, dtype)

    def call(kernel, out_shape, in_specs, scratch=(), cost=None):
        return pl.pallas_call(
            kernel,
            out_shape=out_shape,
            in_specs=in_specs,
            out_specs=[vmem] * len(out_shape),
            scratch_shapes=list(scratch),
            cost_estimate=cost,
            compiler_params=pltpu.CompilerParams(vmem_limit_bytes=24 << 20),
        )

    def exchange(tiles):
        return [lax.ppermute(tiles[key], AXIS, sorted(moves[key].items())) for key in keys]

    tile = shape(32, LANES)
    row = shape(8, LANES)
    inputs = [
        pltpu.with_memory_space_constraint(value, pltpu.HBM)
        for value in (rhs, precond_blocks, bids, connectivity, grads, quad_weight, lame_moduli, mass_diag)
    ]
    *held, d, t0, t1, mixed, far = call(
        functools.partial(begin_kernel, devices, len(inputs)),
        [shape(*value.shape, dtype=value.dtype) for value in inputs] + [shape(24, own), tile, tile, tile, shape(32, LANES)],
        [smem] + [hbm] * len(inputs),
        [pltpu.VMEM((8, own), F32), pltpu.SemaphoreType.DMA((len(inputs),))],
    )(pltpu.with_memory_space_constraint(p, pltpu.SMEM), *inputs)
    rhs, precond_blocks, bids, connectivity, grads, quad_weight, lame_moduli, mass_diag = held
    kind = {1: t0, 4: t1, 16: far}
    got = exchange({key: mixed if key == (4, 1) else kind[key[0]] for key in keys})
    hot, high, wide, place, start, size = call(
        setup_kernel,
        [
            shape(10 * elems, 256, dtype=BF16),
            shape(10, elems, dtype=jnp.int32),
            shape(30, 4, elems),
            shape(1, own, dtype=jnp.int32),
            row,
            row,
        ],
        [smem] + [vmem] * 6,
        cost=pl.CostEstimate(flops=20_000_000, bytes_accessed=4_000_000, transcendentals=0),
    )(elem_count, connectivity, bids, grads, rhs, d, precond_blocks)
    mesh_args = (connectivity, high, wide, quad_weight, lame_moduli, hot, mass_diag)
    left = [
        pltpu.VMEM((24, own + boundary_ids.shape[0]), F32),
        pltpu.VMEM((192, 10 * LANES), BF16),
        pltpu.VMEM((192, 256), F32),
        pltpu.VMEM((8, LANES), F32),
    ]
    tile = shape(48, LANES)
    qpart, ghost, gprec, scale, dot, *send = call(
        functools.partial(first_kernel, keys, devices),
        [shape(24, own), tile, shape(8, 2 * LANES), row, row]
        + [shape(8 if key[0] == 16 else 24, LANES) for key in keys],
        [smem, smem] + [vmem] * (10 + len(keys)),
        left,
    )(p, elem_count, d, bids, size, *mesh_args, *got)
    got = exchange(dict(zip(keys, send)))
    q, s, wpart, message = call(
        functools.partial(second_kernel, keys, devices),
        [shape(24, own), shape(24, own), shape(24, own), shape(devices, 8, LANES)],
        [smem, smem] + [vmem] * (15 + len(keys)),
        left,
    )(p, elem_count, qpart, ghost, precond_blocks, gprec, scale, start, dot, place, *mesh_args, *got)
    message = lax.all_to_all(message, AXIS, 0, 0, tiled=True)
    (relay,) = call(relay_kernel, [tile], [smem, vmem])(p, message)
    relayed = lax.ppermute(relay, AXIS, [(i, i ^ 1) for i in range(devices)])
    (direct,) = call(
        scalar_kernel,
        [shape(64, LANES)],
        [smem] + [vmem] * 2,
        cost=pl.CostEstimate(flops=20_000_000, bytes_accessed=2_000_000, transcendentals=0),
    )(p, message, scale)
    x, r = call(final_kernel, [shape(24, own), shape(24, own)], [vmem] * 8)(
        direct, relayed, rhs, d, q, s, wpart, place
    )
    return x.reshape(3, CASES, own), r.reshape(3, CASES, own)


def solution(mesh):
    return jax.shard_map(
        functools.partial(local, mesh.shape[AXIS]),
        mesh=mesh,
        in_specs=(
            P(None, None, AXIS),
            P(AXIS),
            P(None, None, AXIS),
            P(None, AXIS),
            P(None, None, None, AXIS),
            P(None, AXIS),
            P(None, AXIS),
            P(AXIS),
            P(AXIS),
        ),
        out_specs=(P(None, None, AXIS), P(None, None, AXIS)),
        check_vma=False,
    )
```

```python
import functools

import jax
import jax.numpy as jnp
from jax import lax
from jax.experimental import pallas as pl
from jax.experimental.pallas import tpu as pltpu
from jax.sharding import PartitionSpec as P

F32 = jnp.float32
BF16 = jnp.bfloat16
AXIS = "dom"
CASES = 8
LANES = 128
DISTANCES = (1, 4, 16)


def routes(devices):
    listed = {}
    for distance in DISTANCES:
        for parity in (0, 1):
            route = {}
            for i in range(devices - distance):
                if (i // distance) % 2 == parity:
                    route[i], route[i + distance] = i + distance, i
            if route:
                for i in range(devices):
                    route.setdefault(i, i ^ 1)
                listed[distance, parity] = route
    last = devices - 1
    listed[1, 1].update({0: 1, 1: 2, 2: 0, last: last - 1, last - 1: last - 2, last - 2: last})
    listed[4, 1].update({2: 1, 1: 0, 0: 3, 3: 2})
    listed[4, 1].update({last - 2: last - 1, last - 1: last, last: last - 3, last - 3: last - 2})
    for route in listed.values():
        assert sorted(route.values()) == list(range(devices))
    return listed


def take_lanes(chunks, index):
    lane = index & (LANES - 1)
    which = index >> 7
    rows = len(chunks)
    picked = [None] * rows
    for c in range(len(chunks[0])):
        mask = which == c
        for r in range(rows):
            moved = jnp.take_along_axis(chunks[r][c], lane, axis=1)
            picked[r] = moved if c == 0 else jnp.where(mask, moved, picked[r])
    return picked


def row8(ref, row, start=0, width=LANES):
    return jnp.broadcast_to(ref[row : row + 1, start : start + width], (8, width))


def split_lanes(value):
    return [value[:, c * LANES : (c + 1) * LANES] for c in range(value.shape[1] // LANES)]


def in_two(value):
    head = value.astype(BF16)
    tail = (value - head.astype(F32)).astype(BF16)
    return head, tail


def plus_lanes(lane):
    return [lane < 64, (lane < 48) | ((lane >= 96) & (lane < 112))]


def pack_far(blocks, lane):
    packed = jnp.zeros((8, LANES), F32)
    for r, block in enumerate(blocks):
        moved = pltpu.roll(block, (32 * r - 96) % LANES, 1)
        packed = jnp.where((lane >= 32 * r) & (lane < 32 * r + 32), moved, packed)
    return packed


def joined(p, devices, received, block, lane):
    def arrived(key):
        if key[0] == 16:
            shift = (96 - 32 * block) % LANES
            return pltpu.roll(received[key][0:8, :], shift, 1) if shift else received[key][0:8, :]
        return received[key][8 * block : 8 * block + 8, :]

    sides = {}
    detour = (p == 1) | (p == devices - 2)
    for distance in DISTANCES:
        even = arrived((distance, 0))
        first = lax.rem(lax.div(p, distance), 2) == 0
        if (distance, 1) in received:
            odd = arrived((distance, 1))
            if distance == 1:
                odd = jnp.where(detour, arrived((4, 1)), odd)
        else:
            odd = jnp.zeros_like(even)
        plus = jnp.where(p + distance < devices, jnp.where(first, even, odd), 0.0)
        minus = jnp.where(p - distance >= 0, jnp.where(first, odd, even), 0.0)
        sides[distance] = plus, minus
    tiles = []
    for a, b in ((0, 1), (1, 0)):
        tile1 = jnp.where(
            lane < 48,
            sides[4][a],
            jnp.where(lane < 96, sides[4][b], jnp.where(lane < 112, sides[16][a], sides[16][b])),
        )
        tiles.append([jnp.where(lane < 64, sides[1][a], sides[1][b]), tile1])
    return tiles


def send_mixed(p, devices, tile0, tile1):
    return jnp.where((p == 2) | (p == devices - 3), tile0, tile1)


def spread(tiles, place_ref, block):
    place = jnp.broadcast_to(place_ref[0:1, block * LANES : (block + 1) * LANES], (8, LANES))
    return [jnp.where(place >= 0, value, 0.0) for value in take_lanes(tiles, place)]


def boundary_values(chunks, bids_ref):
    return [take_lanes(chunks, row8(bids_ref, 0, t * LANES)) for t in range(2)]


def elements(chunks, count, conn_ref, high_ref, wide_ref, qw_ref, lame_ref, hot_ref, held_ref, left_ref, sum_ref, work_ref):
    elems = conn_ref.shape[1]
    for i in range(3):
        for c, value in enumerate(chunks[i]):
            held_ref[8 * i : 8 * i + 8, c * LANES : (c + 1) * LANES] = value

    def wide(k, a, q, e0):
        return jnp.broadcast_to(wide_ref[k * 10 + a, q : q + 1, e0 : e0 + LANES], (8, LANES))

    def block(e0):
        held = [split_lanes(held_ref[8 * i : 8 * i + 8, :]) for i in range(3)] if e0 else chunks
        nodal = [take_lanes(held, row8(conn_ref, a, e0)) for a in range(10)]
        forces = [[None] * 10 for _ in range(3)]
        lam = lame_ref[0:1, e0 : e0 + LANES]
        mu = lame_ref[1:2, e0 : e0 + LANES]
        for q in range(4):
            grad = [[None] * 3 for _ in range(3)]
            for k in range(3):
                for a in range(10):
                    g = wide(k, a, q, e0)
                    for i in range(3):
                        term = nodal[a][i] * g
                        grad[i][k] = term if a == 0 else grad[i][k] + term
            w = qw_ref[q : q + 1, e0 : e0 + LANES]
            wmu = jnp.broadcast_to(w * mu, (8, LANES))
            wlam = jnp.broadcast_to(w * lam, (8, LANES))
            swell = wlam * (grad[0][0] + grad[1][1] + grad[2][2])
            stress = [[None] * 3 for _ in range(3)]
            for i in range(3):
                stress[i][i] = wmu * (grad[i][i] + grad[i][i]) + swell
                for k in range(i):
                    stress[i][k] = wmu * (grad[i][k] + grad[k][i])
                    stress[k][i] = stress[i][k]
            for k in range(3):
                for a in range(10):
                    g = wide(k, a, q, e0)
                    for i in range(3):
                        term = stress[i][k] * g
                        forces[i][a] = term if q + k == 0 else forces[i][a] + term
        done = forces[0][0] * nodal[0][0]
        for a in range(10):
            for i in range(3):
                if a + i > 0:
                    done = done + forces[i][a] * nodal[a][i]
        done = jnp.where(row8(high_ref, 0, e0) >= 0, done, 0.0)
        for a in range(10):
            high = row8(high_ref, a, e0)
            parts = [in_two(forces[i][a]) for i in range(3)]
            for h in range(4):
                mask = high == h
                kept = [jnp.where(mask, parts[i][s].astype(F32), 0.0) for s in range(2) for i in range(3)]
                left_ref[h * 48 : h * 48 + 48, a * LANES : (a + 1) * LANES] = jnp.concatenate(kept, axis=0).astype(
                    BF16
                )
        added = lax.dot_general(
            left_ref[...],
            hot_ref[e0 * 10 : (e0 + LANES) * 10, :],
            (((1,), (0,)), ((), ())),
            preferred_element_type=F32,
        )
        sum_ref[...] = sum_ref[...] + added if e0 else added
        work_ref[...] = work_ref[...] + done if e0 else done

    block(0)
    for e0 in range(LANES, elems, LANES):
        pl.when(e0 < count)(functools.partial(block, e0))


def node_sums(sum_ref):
    out = sum_ref[...]
    blocks = []
    for i in range(3):
        blocks.append([])
        for h in range(4):
            at = h * 48 + i * 8
            blocks[i] += split_lanes(out[at : at + 8] + out[at + 24 : at + 32])
    return blocks


def splat(value):
    return jnp.broadcast_to(value, (8, LANES))


def lane_sum(values):
    total = values[0]
    for value in values[1:]:
        total = total + value
    return jnp.sum(total, axis=1, keepdims=True)


def setup_kernel(
    count_ref, conn_ref, bids_ref, grads_ref, rhs_ref, d_ref, prec_ref, hot_ref, high_ref, wide_ref, place_ref, start_ref, size_ref
):
    elems = conn_ref.shape[1]
    element = lax.broadcasted_iota(jnp.int32, (10, elems), 1)
    is_live = element < count_ref[0]
    high_ref[...] = jnp.where(is_live, conn_ref[...] >> 8, -1)
    lows = lax.broadcasted_iota(jnp.int32, (LANES, 256), 1)
    padding = jnp.zeros((6, LANES), jnp.int32)
    for e0 in range(0, elems, LANES):
        index = jnp.concatenate([conn_ref[:, e0 : e0 + LANES] & 255, padding], axis=0).T
        for a in range(10):
            at = e0 * 10 + a * LANES
            hot_ref[at : at + LANES, :] = jnp.where(lows == index[:, a : a + 1], 1.0, 0.0).astype(BF16)
    for k in range(3):
        for a in range(10):
            wide_ref[k * 10 + a] = grads_ref[k, a].astype(F32)
    own, ghosts = rhs_ref.shape[1], bids_ref.shape[1]
    listed = jnp.broadcast_to(bids_ref[0:1, :], (8, ghosts)).T[:, 0:1]
    for first in range(0, own, LANES):
        node = first + lax.broadcasted_iota(jnp.int32, (ghosts, LANES), 1)
        entry = lax.broadcasted_iota(jnp.int32, (ghosts, LANES), 0)
        found = jnp.max(jnp.where(listed == node, entry, -1), axis=0, keepdims=True)
        place_ref[:, first : first + LANES] = found
    blocks = [slice(8 * i, 8 * i + 8) for i in range(3)]
    start_ref[...] = splat(lane_sum([p for b in blocks for p in split_lanes(rhs_ref[b, :] * d_ref[b, :])]))
    largest = jnp.abs(prec_ref[0])
    for i in range(1, 3):
        largest = jnp.maximum(largest, jnp.abs(prec_ref[i]))
    size_ref[...] = splat(jnp.max(jnp.max(largest, axis=1, keepdims=True), axis=0, keepdims=True))


def entry(i, j):
    return (0, 1, 2, 1, 3, 4, 2, 4, 5)[3 * i + j]


def begin_kernel(devices, inputs, p_ref, *rest):
    hbm = rest[:inputs]
    held = rest[inputs : 2 * inputs]
    d_ref, t0_ref, t1_ref, mixed_ref, far_ref, blocks_ref, sems = rest[2 * inputs :]
    copies = [pltpu.make_async_copy(hbm[k], held[k], sems.at[k]) for k in range(inputs)]
    for copy in copies:
        copy.start()
    for copy in copies[:3]:
        copy.wait()
    rhs_ref, prec_ref, bids_ref = held[:3]
    p = p_ref[0]
    blocks_ref[...] = jnp.zeros_like(blocks_ref)
    for i in range(3):
        d_ref[8 * i : 8 * i + 8, :] = (
            prec_ref[i, 0:1, :] * rhs_ref[0:8, :]
            + prec_ref[i, 1:2, :] * rhs_ref[8:16, :]
            + prec_ref[i, 2:3, :] * rhs_ref[16:24, :]
        )
        for j in range(i, 3):
            k = entry(i, j)
            blocks_ref[k : k + 1, :] = prec_ref[i, j : j + 1, :]
    rows = [split_lanes(d_ref[8 * i : 8 * i + 8, :]) for i in range(3)]
    rows.append(split_lanes(blocks_ref[...]))
    tiles = boundary_values(rows, bids_ref)
    far_ref[...] = jnp.zeros_like(far_ref)
    far_ref[0:8, :] = pack_far(tiles[1], lax.broadcasted_iota(jnp.int32, (8, LANES), 1))
    for r in range(4):
        here = slice(8 * r, 8 * r + 8)
        t0_ref[here, :] = tiles[0][r]
        t1_ref[here, :] = tiles[1][r]
        mixed_ref[here, :] = send_mixed(p, devices, tiles[0][r], tiles[1][r])
    for copy in copies[3:]:
        copy.wait()


def first_kernel(
    keys, devices, p_ref, count_ref, d_ref, bids_ref, size_ref, conn_ref, high_ref, wide_ref, qw_ref, lame_ref, hot_ref, mass_ref, *rest
):
    received = dict(zip(keys, rest[: len(keys)]))
    q_ref, ghost_ref, gprec_ref, scale_ref, dot_ref, *send = rest[len(keys) : -4]
    scratch = rest[-4:]
    send = dict(zip(keys, send))
    p = p_ref[0]
    lane = lax.broadcasted_iota(jnp.int32, (8, LANES), 1)
    chunks = []
    for i in range(3):
        chunks.append(split_lanes(d_ref[8 * i : 8 * i + 8, :]) + joined(p, devices, received, i, lane)[0])
    largest = size_ref[...]
    for t, tile in enumerate(joined(p, devices, received, 3, lane)[0]):
        gprec_ref[:, t * LANES : (t + 1) * LANES] = tile
        largest = jnp.maximum(largest, jnp.abs(tile))
    scale_ref[...] = splat(jnp.max(jnp.max(largest, axis=1, keepdims=True), axis=0, keepdims=True))
    elements(chunks, count_ref[0], conn_ref, high_ref, wide_ref, qw_ref, lame_ref, hot_ref, *scratch)
    acc = node_sums(scratch[2])
    work = scratch[3][...]
    own_chunks = d_ref.shape[1] // LANES
    mass = mass_rows(mass_ref)
    dots = [work]
    partial = []
    for i in range(3):
        partial.append([])
        for c in range(own_chunks):
            heavy = mass[c] * chunks[i][c]
            partial[i].append(acc[i][c] + heavy)
            dots.append(heavy * chunks[i][c])
    tiles = boundary_values(partial, bids_ref)
    higher = plus_lanes(lane)
    message = {}
    for key in keys:
        distance, parity = key
        t = 0 if distance == 1 else 1
        first = lax.rem(lax.div(p, distance), 2) == parity
        message[key] = []
        for i in range(3):
            mine, theirs = acc[i][own_chunks + t], tiles[t][i]
            upward = jnp.where(higher[t], mine, theirs)
            downward = jnp.where(higher[t], theirs, mine)
            message[key].append(jnp.where(first, upward, downward))
    message[4, 1] = [send_mixed(p, devices, a, b) for a, b in zip(message[1, 1], message[4, 1])]
    for key in keys:
        if key[0] == 16:
            send[key][...] = jnp.zeros_like(send[key])
            send[key][0:8, :] = pack_far(message[key], lane)
            continue
        for i in range(3):
            send[key][8 * i : 8 * i + 8, :] = message[key][i]
    for i in range(3):
        for t in range(2):
            here = slice(24 * t + 8 * i, 24 * t + 8 * i + 8)
            ghost_ref[here, :] = acc[i][own_chunks + t]
        for c in range(own_chunks):
            q_ref[8 * i : 8 * i + 8, c * LANES : (c + 1) * LANES] = partial[i][c]
    dot_ref[...] = splat(lane_sum(dots))


def mass_rows(mass_ref):
    count = mass_ref.shape[0] // LANES
    return [jnp.broadcast_to(mass_ref[c * LANES : (c + 1) * LANES].reshape(1, LANES), (8, LANES)) for c in range(count)]


WINDOWS = (
    (1, 1, 0, 0, 64),
    (1, -1, 0, 64, 64),
    (4, 1, 1, 0, 48),
    (4, -1, 1, 48, 48),
    (16, 1, 1, 96, 16),
    (16, -1, 1, 112, 16),
)


def second_kernel(
    keys,
    devices,
    p_ref,
    count_ref,
    qpart_ref,
    ghost_ref,
    prec_ref,
    gprec_ref,
    scale_ref,
    start_ref,
    dot_ref,
    place_ref,
    conn_ref,
    high_ref,
    wide_ref,
    qw_ref,
    lame_ref,
    hot_ref,
    mass_ref,
    *rest,
):
    received = dict(zip(keys, rest[: len(keys)]))
    q_ref, s_ref, w_ref, out_ref, *scratch = rest[len(keys) :]
    p = p_ref[0]
    own_chunks = q_ref.shape[1] // LANES
    lane = lax.broadcasted_iota(jnp.int32, (8, LANES), 1)
    swapped = [joined(p, devices, received, i, lane) for i in range(3)]
    back = [both[1] for both in swapped]
    for c in range(own_chunks):
        for i, value in enumerate(spread(back, place_ref, c)):
            here = slice(8 * i, 8 * i + 8), slice(c * LANES, (c + 1) * LANES)
            q_ref[here] = qpart_ref[here] + value
    scale = scale_ref[...]
    inverse = (1.0 / scale)[0:1, 0:1]
    ghost_q = []
    for i in range(3):
        ghost_q.append(
            [ghost_ref[24 * t + 8 * i : 24 * t + 8 * i + 8, :] + swapped[i][0][t] for t in range(2)]
        )
    chunks = []
    for i in range(3):
        value = (
            (prec_ref[i, 0:1, :] * inverse) * q_ref[0:8, :]
            + (prec_ref[i, 1:2, :] * inverse) * q_ref[8:16, :]
            + (prec_ref[i, 2:3, :] * inverse) * q_ref[16:24, :]
        )
        s_ref[8 * i : 8 * i + 8, :] = value
        chunks.append(split_lanes(value))
        for t in range(2):
            total = None
            for j in range(3):
                k = entry(i, j)
                term = (gprec_ref[k : k + 1, t * LANES : (t + 1) * LANES] * inverse) * ghost_q[j][t]
                total = term if j == 0 else total + term
            chunks[i].append(total)
    elements(chunks, count_ref[0], conn_ref, high_ref, wide_ref, qw_ref, lame_ref, hot_ref, *scratch)
    acc = node_sums(scratch[2])
    work = scratch[3][...]
    ghost = [acc[i][own_chunks:] for i in range(3)]
    mass = mass_rows(mass_ref)
    cross = []
    square = [work]
    for i in range(3):
        for c in range(own_chunks):
            here = slice(8 * i, 8 * i + 8), slice(c * LANES, (c + 1) * LANES)
            heavy = mass[c] * chunks[i][c]
            w_ref[here] = acc[i][c] + heavy
            cross.append(q_ref[here] * chunks[i][c])
            square.append(heavy * chunks[i][c])
    tail = jnp.where(lane < 120, 0.0, scale)
    for k, value in enumerate((start_ref[...], dot_ref[...], splat(lane_sum(cross)), splat(lane_sum(square)))):
        tail = jnp.where(lane == 120 + k, value, tail)

    def fill(j, unused):
        for k in range(8):
            out_ref[8 * j + k] = tail
        return unused

    lax.fori_loop(0, devices // 8, fill, 0)

    def pack(tile, column):
        packed = tail
        for i in range(3):
            shift = (40 * i - column) % LANES
            moved = pltpu.roll(ghost[i][tile], shift, 1) if shift else ghost[i][tile]
            packed = jnp.where((lane >= 40 * i) & (lane < 40 * i + 40), moved, packed)
        return packed

    for distance, sign, tile, column, width in WINDOWS:
        target = p + sign * distance
        direct = pack(tile, column)
        beyond = pack(tile, column + 40) if width > 40 else None

        @pl.when((target >= 0) & (target < devices))
        def _():
            out_ref[target] = direct
            if beyond is not None:
                out_ref[jnp.bitwise_xor(target, 1)] = beyond


def unpacked(in_ref, owner, devices, lane, inverse, direct):
    back = [[jnp.zeros((8, LANES), F32) for _ in range(2)] for _ in range(3)]
    for distance, sign, tile, column, width in WINDOWS:
        first, size = (column, min(width, 40)) if direct else (column + 40, width - 40)
        if size <= 0:
            continue
        source = owner - sign * distance
        valid = (source >= 0) & (source < devices)
        block = in_ref[jnp.clip(source, 0, devices - 1)]
        ratio = splat(block[:, 124:125]) * inverse
        inside = (lane >= first) & (lane < first + size) & valid
        for i in range(3):
            shift = (first - 40 * i) % LANES
            moved = pltpu.roll(block, shift, 1) if shift else block
            back[i][tile] = jnp.where(inside, moved * ratio, back[i][tile])
    return [back[i][t] for t in range(2) for i in range(3)]


def relay_kernel(p_ref, in_ref, out_ref):
    devices = in_ref.shape[0]
    lane = lax.broadcasted_iota(jnp.int32, (8, LANES), 1)
    owner = jnp.bitwise_xor(p_ref[0], 1)
    inverse = 1.0 / splat(in_ref[owner][:, 124:125])
    for k, block in enumerate(unpacked(in_ref, owner, devices, lane, inverse, False)):
        out_ref[8 * k : 8 * k + 8, :] = block


def scalar_kernel(p_ref, in_ref, scale_ref, out_ref):
    devices = in_ref.shape[0]
    lane = lax.broadcasted_iota(jnp.int32, (8, LANES), 1)
    mine = scale_ref[...]
    inv_mine = 1.0 / mine
    for k, block in enumerate(unpacked(in_ref, p_ref[0], devices, lane, inv_mine, True)):
        out_ref[8 * k : 8 * k + 8, :] = block

    def term(j):
        tile = in_ref[j]
        ratio = pltpu.roll(tile, LANES - 4, 1) * inv_mine
        return tile * jnp.where(lane == 122, ratio, jnp.where(lane == 123, ratio * ratio, 1.0))

    def add_up(j, sums):
        values = [term(8 * j + k) for k in range(8)]
        while len(values) > 1:
            values = [a + b for a, b in zip(values[::2], values[1::2])]
        return sums + values[0]

    sums = lax.fori_loop(0, devices // 8, add_up, jnp.zeros((8, LANES), F32), unroll=devices <= 64)
    e0, d0, cross, square = (splat(sums[:, k : k + 1]) for k in range(120, 124))
    step = e0 / d0
    scaled = step * mine
    fresh = scaled * (step * cross) - e0
    beta = fresh / e0
    more = 1.0 + beta
    bend = more * more * d0 - 2.0 * more * (scaled * cross) + scaled * (scaled * square)
    step1 = fresh / bend
    out_ref[48:56, :] = step + step1 * more
    out_ref[56:64, :] = step1 * scaled


def final_kernel(direct_ref, relayed_ref, rhs_ref, d_ref, q_ref, s_ref, wpart_ref, place_ref, x_ref, r_ref):
    lane = lax.broadcasted_iota(jnp.int32, (8, LANES), 1)
    for_d = direct_ref[48:56, :]
    for_s = direct_ref[56:64, :]
    back = [[None, None] for _ in range(3)]
    for t in range(2):
        far = lane < 0
        for _, _, tile, column, width in WINDOWS:
            if tile == t:
                far = far | ((lane >= column + 40) & (lane < column + width))
        for i in range(3):
            here = slice(24 * t + 8 * i, 24 * t + 8 * i + 8)
            back[i][t] = jnp.where(far, relayed_ref[here, :], direct_ref[here, :])
    for c in range(rhs_ref.shape[1] // LANES):
        for i, value in enumerate(spread(back, place_ref, c)):
            here = slice(8 * i, 8 * i + 8), slice(c * LANES, (c + 1) * LANES)
            x_ref[here] = for_d * d_ref[here] - for_s * s_ref[here]
            r_ref[here] = rhs_ref[here] - for_d * q_ref[here] + for_s * (wpart_ref[here] + value)


def local(
    devices,
    right_side,
    mass_diag,
    precond_blocks,
    connectivity,
    shape_grads,
    quad_weight,
    lame_moduli,
    elem_count,
    boundary_ids,
):
    own = right_side.shape[2]
    elems = connectivity.shape[1]
    p = lax.axis_index(AXIS).astype(jnp.int32).reshape(1)
    rhs = right_side.reshape(24, own)
    bids = boundary_ids.reshape(1, boundary_ids.shape[0])
    grads = jnp.transpose(shape_grads, (1, 2, 0, 3))
    vmem = pl.BlockSpec(memory_space=pltpu.VMEM)
    smem = pl.BlockSpec(memory_space=pltpu.SMEM)
    hbm = pl.BlockSpec(memory_space=pltpu.HBM)
    moves = routes(devices)
    keys = list(moves)

    def shape(*dims, dtype=F32):
        return jax.ShapeDtypeStruct(dims, dtype)

    def call(kernel, out_shape, in_specs, scratch=(), cost=None):
        return pl.pallas_call(
            kernel,
            out_shape=out_shape,
            in_specs=in_specs,
            out_specs=[vmem] * len(out_shape),
            scratch_shapes=list(scratch),
            cost_estimate=cost,
            compiler_params=pltpu.CompilerParams(vmem_limit_bytes=24 << 20),
        )

    def exchange(tiles):
        return [lax.ppermute(tiles[key], AXIS, sorted(moves[key].items())) for key in keys]

    tile = shape(32, LANES)
    row = shape(8, LANES)
    inputs = [
        pltpu.with_memory_space_constraint(value, pltpu.HBM)
        for value in (rhs, precond_blocks, bids, connectivity, grads, quad_weight, lame_moduli, mass_diag)
    ]
    *held, d, t0, t1, mixed, far = call(
        functools.partial(begin_kernel, devices, len(inputs)),
        [shape(*value.shape, dtype=value.dtype) for value in inputs] + [shape(24, own), tile, tile, tile, shape(32, LANES)],
        [smem] + [hbm] * len(inputs),
        [pltpu.VMEM((8, own), F32), pltpu.SemaphoreType.DMA((len(inputs),))],
    )(pltpu.with_memory_space_constraint(p, pltpu.SMEM), *inputs)
    rhs, precond_blocks, bids, connectivity, grads, quad_weight, lame_moduli, mass_diag = held
    kind = {1: t0, 4: t1, 16: far}
    got = exchange({key: mixed if key == (4, 1) else kind[key[0]] for key in keys})
    hot, high, wide, place, start, size = call(
        setup_kernel,
        [
            shape(10 * elems, 256, dtype=BF16),
            shape(10, elems, dtype=jnp.int32),
            shape(30, 4, elems),
            shape(1, own, dtype=jnp.int32),
            row,
            row,
        ],
        [smem] + [vmem] * 6,
        cost=pl.CostEstimate(flops=20_000_000, bytes_accessed=4_000_000, transcendentals=0),
    )(elem_count, connectivity, bids, grads, rhs, d, precond_blocks)
    mesh_args = (connectivity, high, wide, quad_weight, lame_moduli, hot, mass_diag)
    left = [
        pltpu.VMEM((24, own + boundary_ids.shape[0]), F32),
        pltpu.VMEM((192, 10 * LANES), BF16),
        pltpu.VMEM((192, 256), F32),
        pltpu.VMEM((8, LANES), F32),
    ]
    tile = shape(48, LANES)
    qpart, ghost, gprec, scale, dot, *send = call(
        functools.partial(first_kernel, keys, devices),
        [shape(24, own), tile, shape(8, 2 * LANES), row, row]
        + [shape(32 if key[0] == 16 else 24, LANES) for key in keys],
        [smem, smem] + [vmem] * (10 + len(keys)),
        left,
    )(p, elem_count, d, bids, size, *mesh_args, *got)
    got = exchange(dict(zip(keys, send)))
    q, s, wpart, message = call(
        functools.partial(second_kernel, keys, devices),
        [shape(24, own), shape(24, own), shape(24, own), shape(devices, 8, LANES)],
        [smem, smem] + [vmem] * (15 + len(keys)),
        left,
    )(p, elem_count, qpart, ghost, precond_blocks, gprec, scale, start, dot, place, *mesh_args, *got)
    message = lax.all_to_all(message, AXIS, 0, 0, tiled=True)
    (relay,) = call(relay_kernel, [tile], [smem, vmem])(p, message)
    relayed = lax.ppermute(relay, AXIS, [(i, i ^ 1) for i in range(devices)])
    (direct,) = call(
        scalar_kernel,
        [shape(64, LANES)],
        [smem] + [vmem] * 2,
        cost=pl.CostEstimate(flops=20_000_000, bytes_accessed=2_000_000, transcendentals=0),
    )(p, message, scale)
    x, r = call(final_kernel, [shape(24, own), shape(24, own)], [vmem] * 8)(
        direct, relayed, rhs, d, q, s, wpart, place
    )
    return x.reshape(3, CASES, own), r.reshape(3, CASES, own)


def solution(mesh):
    return jax.shard_map(
        functools.partial(local, mesh.shape[AXIS]),
        mesh=mesh,
        in_specs=(
            P(None, None, AXIS),
            P(AXIS),
            P(None, None, AXIS),
            P(None, AXIS),
            P(None, None, None, AXIS),
            P(None, AXIS),
            P(None, AXIS),
            P(AXIS),
            P(AXIS),
        ),
        out_specs=(P(None, None, AXIS), P(None, None, AXIS)),
        check_vma=False,
    )
```

```python
import functools

import jax
import jax.numpy as jnp
from jax import lax
from jax.experimental import pallas as pl
from jax.experimental.pallas import tpu as pltpu
from jax.sharding import PartitionSpec as P

F32 = jnp.float32
BF16 = jnp.bfloat16
AXIS = "dom"
CASES = 8
LANES = 128
DISTANCES = (1, 4, 16)


def routes(devices):
    listed = {}
    for distance in DISTANCES:
        for parity in (0, 1):
            route = {}
            for i in range(devices - distance):
                if (i // distance) % 2 == parity:
                    route[i], route[i + distance] = i + distance, i
            if route:
                for i in range(devices):
                    route.setdefault(i, i ^ 1)
                listed[distance, parity] = route
    last = devices - 1
    listed[1, 1].update({0: 1, 1: 2, 2: 0, last: last - 1, last - 1: last - 2, last - 2: last})
    listed[4, 1].update({2: 1, 1: 0, 0: 3, 3: 2})
    listed[4, 1].update({last - 2: last - 1, last - 1: last, last: last - 3, last - 3: last - 2})
    for route in listed.values():
        assert sorted(route.values()) == list(range(devices))
    return listed


def take_lanes(chunks, index):
    lane = index & (LANES - 1)
    which = index >> 7
    rows = len(chunks)
    picked = [None] * rows
    for c in range(len(chunks[0])):
        mask = which == c
        for r in range(rows):
            moved = jnp.take_along_axis(chunks[r][c], lane, axis=1)
            picked[r] = moved if c == 0 else jnp.where(mask, moved, picked[r])
    return picked


def row8(ref, row, start=0, width=LANES):
    return jnp.broadcast_to(ref[row : row + 1, start : start + width], (8, width))


def split_lanes(value):
    return [value[:, c * LANES : (c + 1) * LANES] for c in range(value.shape[1] // LANES)]


def in_two(value):
    head = value.astype(BF16)
    tail = (value - head.astype(F32)).astype(BF16)
    return head, tail


def plus_lanes(lane):
    return [lane < 64, (lane < 48) | ((lane >= 96) & (lane < 112))]


def pack_far(blocks, lane):
    packed = jnp.zeros((8, LANES), F32)
    for r, block in enumerate(blocks):
        moved = pltpu.roll(block, (32 * r - 96) % LANES, 1)
        packed = jnp.where((lane >= 32 * r) & (lane < 32 * r + 32), moved, packed)
    return packed


def joined(p, devices, received, block, lane):
    def arrived(key):
        if key[0] == 16:
            shift = (96 - 32 * block) % LANES
            return pltpu.roll(received[key][0:8, :], shift, 1) if shift else received[key][0:8, :]
        return received[key][8 * block : 8 * block + 8, :]

    sides = {}
    detour = (p == 1) | (p == devices - 2)
    for distance in DISTANCES:
        even = arrived((distance, 0))
        first = lax.rem(lax.div(p, distance), 2) == 0
        if (distance, 1) in received:
            odd = arrived((distance, 1))
            if distance == 1:
                odd = jnp.where(detour, arrived((4, 1)), odd)
        else:
            odd = jnp.zeros_like(even)
        plus = jnp.where(p + distance < devices, jnp.where(first, even, odd), 0.0)
        minus = jnp.where(p - distance >= 0, jnp.where(first, odd, even), 0.0)
        sides[distance] = plus, minus
    tiles = []
    for a, b in ((0, 1), (1, 0)):
        tile1 = jnp.where(
            lane < 48,
            sides[4][a],
            jnp.where(lane < 96, sides[4][b], jnp.where(lane < 112, sides[16][a], sides[16][b])),
        )
        tiles.append([jnp.where(lane < 64, sides[1][a], sides[1][b]), tile1])
    return tiles


def send_mixed(p, devices, tile0, tile1):
    return jnp.where((p == 2) | (p == devices - 3), tile0, tile1)


def spread(tiles, place_ref, block):
    place = jnp.broadcast_to(place_ref[0:1, block * LANES : (block + 1) * LANES], (8, LANES))
    return [jnp.where(place >= 0, value, 0.0) for value in take_lanes(tiles, place)]


def boundary_values(chunks, bids_ref):
    return [take_lanes(chunks, row8(bids_ref, 0, t * LANES)) for t in range(2)]


def elements(chunks, count, conn_ref, high_ref, wide_ref, qw_ref, lame_ref, hot_ref, held_ref, left_ref, sum_ref, work_ref):
    elems = conn_ref.shape[1]
    for i in range(3):
        for c, value in enumerate(chunks[i]):
            held_ref[8 * i : 8 * i + 8, c * LANES : (c + 1) * LANES] = value

    def wide(k, a, q, e0):
        return jnp.broadcast_to(wide_ref[k * 10 + a, q : q + 1, e0 : e0 + LANES], (8, LANES))

    def block(e0):
        held = [split_lanes(held_ref[8 * i : 8 * i + 8, :]) for i in range(3)] if e0 else chunks
        nodal = [take_lanes(held, row8(conn_ref, a, e0)) for a in range(10)]
        forces = [[None] * 10 for _ in range(3)]
        lam = lame_ref[0:1, e0 : e0 + LANES]
        mu = lame_ref[1:2, e0 : e0 + LANES]
        for q in range(4):
            grad = [[None] * 3 for _ in range(3)]
            for k in range(3):
                for a in range(10):
                    g = wide(k, a, q, e0)
                    for i in range(3):
                        term = nodal[a][i] * g
                        grad[i][k] = term if a == 0 else grad[i][k] + term
            w = qw_ref[q : q + 1, e0 : e0 + LANES]
            wmu = jnp.broadcast_to(w * mu, (8, LANES))
            wlam = jnp.broadcast_to(w * lam, (8, LANES))
            swell = wlam * (grad[0][0] + grad[1][1] + grad[2][2])
            stress = [[None] * 3 for _ in range(3)]
            for i in range(3):
                stress[i][i] = wmu * (grad[i][i] + grad[i][i]) + swell
                for k in range(i):
                    stress[i][k] = wmu * (grad[i][k] + grad[k][i])
                    stress[k][i] = stress[i][k]
            for k in range(3):
                for a in range(10):
                    g = wide(k, a, q, e0)
                    for i in range(3):
                        term = stress[i][k] * g
                        forces[i][a] = term if q + k == 0 else forces[i][a] + term
        done = forces[0][0] * nodal[0][0]
        for a in range(10):
            for i in range(3):
                if a + i > 0:
                    done = done + forces[i][a] * nodal[a][i]
        done = jnp.where(row8(high_ref, 0, e0) >= 0, done, 0.0)
        for a in range(10):
            high = row8(high_ref, a, e0)
            parts = [in_two(forces[i][a]) for i in range(3)]
            for h in range(4):
                mask = high == h
                kept = [jnp.where(mask, parts[i][s].astype(F32), 0.0) for s in range(2) for i in range(3)]
                left_ref[h * 48 : h * 48 + 48, a * LANES : (a + 1) * LANES] = jnp.concatenate(kept, axis=0).astype(
                    BF16
                )
        added = lax.dot_general(
            left_ref[...],
            hot_ref[e0 * 10 : (e0 + LANES) * 10, :],
            (((1,), (0,)), ((), ())),
            preferred_element_type=F32,
        )
        sum_ref[...] = sum_ref[...] + added if e0 else added
        work_ref[...] = work_ref[...] + done if e0 else done

    block(0)
    for e0 in range(LANES, elems, LANES):
        pl.when(e0 < count)(functools.partial(block, e0))


def node_sums(sum_ref):
    out = sum_ref[...]
    blocks = []
    for i in range(3):
        blocks.append([])
        for h in range(4):
            at = h * 48 + i * 8
            blocks[i] += split_lanes(out[at : at + 8] + out[at + 24 : at + 32])
    return blocks


def splat(value):
    return jnp.broadcast_to(value, (8, LANES))


def lane_sum(values):
    total = values[0]
    for value in values[1:]:
        total = total + value
    return jnp.sum(total, axis=1, keepdims=True)


def setup_kernel(
    count_ref, conn_ref, bids_ref, grads_ref, rhs_ref, d_ref, prec_ref, hot_ref, high_ref, wide_ref, place_ref, start_ref, size_ref
):
    elems = conn_ref.shape[1]
    element = lax.broadcasted_iota(jnp.int32, (10, elems), 1)
    is_live = element < count_ref[0]
    high_ref[...] = jnp.where(is_live, conn_ref[...] >> 8, -1)
    lows = lax.broadcasted_iota(jnp.int32, (LANES, 256), 1)
    padding = jnp.zeros((6, LANES), jnp.int32)

    def one_hot(e0):
        index = jnp.concatenate([conn_ref[:, e0 : e0 + LANES] & 255, padding], axis=0).T
        for a in range(10):
            at = e0 * 10 + a * LANES
            hot_ref[at : at + LANES, :] = jnp.where(lows == index[:, a : a + 1], 1.0, 0.0).astype(BF16)

    one_hot(0)
    for e0 in range(LANES, elems, LANES):
        pl.when(e0 < count_ref[0])(functools.partial(one_hot, e0))
    for k in range(3):
        for a in range(10):
            wide_ref[k * 10 + a] = grads_ref[k, a].astype(F32)
    own, ghosts = rhs_ref.shape[1], bids_ref.shape[1]
    listed = jnp.broadcast_to(bids_ref[0:1, :], (8, ghosts)).T[:, 0:1]
    for first in range(0, own, LANES):
        node = first + lax.broadcasted_iota(jnp.int32, (ghosts, LANES), 1)
        entry = lax.broadcasted_iota(jnp.int32, (ghosts, LANES), 0)
        found = jnp.max(jnp.where(listed == node, entry, -1), axis=0, keepdims=True)
        place_ref[:, first : first + LANES] = found
    blocks = [slice(8 * i, 8 * i + 8) for i in range(3)]
    start_ref[...] = splat(lane_sum([p for b in blocks for p in split_lanes(rhs_ref[b, :] * d_ref[b, :])]))
    largest = jnp.abs(prec_ref[0])
    for i in range(1, 3):
        largest = jnp.maximum(largest, jnp.abs(prec_ref[i]))
    size_ref[...] = splat(jnp.max(jnp.max(largest, axis=1, keepdims=True), axis=0, keepdims=True))


def entry(i, j):
    return (0, 1, 2, 1, 3, 4, 2, 4, 5)[3 * i + j]


def begin_kernel(devices, inputs, p_ref, *rest):
    hbm = rest[:inputs]
    held = rest[inputs : 2 * inputs]
    d_ref, t0_ref, t1_ref, mixed_ref, far_ref, blocks_ref, sems = rest[2 * inputs :]
    copies = [pltpu.make_async_copy(hbm[k], held[k], sems.at[k]) for k in range(inputs)]
    for copy in copies:
        copy.start()
    for copy in copies[:3]:
        copy.wait()
    rhs_ref, prec_ref, bids_ref = held[:3]
    p = p_ref[0]
    blocks_ref[...] = jnp.zeros_like(blocks_ref)
    for i in range(3):
        d_ref[8 * i : 8 * i + 8, :] = (
            prec_ref[i, 0:1, :] * rhs_ref[0:8, :]
            + prec_ref[i, 1:2, :] * rhs_ref[8:16, :]
            + prec_ref[i, 2:3, :] * rhs_ref[16:24, :]
        )
        for j in range(i, 3):
            k = entry(i, j)
            blocks_ref[k : k + 1, :] = prec_ref[i, j : j + 1, :]
    rows = [split_lanes(d_ref[8 * i : 8 * i + 8, :]) for i in range(3)]
    rows.append(split_lanes(blocks_ref[...]))
    tiles = boundary_values(rows, bids_ref)
    far_ref[...] = jnp.zeros_like(far_ref)
    far_ref[0:8, :] = pack_far(tiles[1], lax.broadcasted_iota(jnp.int32, (8, LANES), 1))
    for r in range(4):
        here = slice(8 * r, 8 * r + 8)
        t0_ref[here, :] = tiles[0][r]
        t1_ref[here, :] = tiles[1][r]
        mixed_ref[here, :] = send_mixed(p, devices, tiles[0][r], tiles[1][r])
    for copy in copies[3:]:
        copy.wait()


def first_kernel(
    keys, devices, p_ref, count_ref, d_ref, bids_ref, size_ref, conn_ref, high_ref, wide_ref, qw_ref, lame_ref, hot_ref, mass_ref, *rest
):
    received = dict(zip(keys, rest[: len(keys)]))
    q_ref, ghost_ref, gprec_ref, scale_ref, dot_ref, *send = rest[len(keys) : -4]
    scratch = rest[-4:]
    send = dict(zip(keys, send))
    p = p_ref[0]
    lane = lax.broadcasted_iota(jnp.int32, (8, LANES), 1)
    chunks = []
    for i in range(3):
        chunks.append(split_lanes(d_ref[8 * i : 8 * i + 8, :]) + joined(p, devices, received, i, lane)[0])
    largest = size_ref[...]
    for t, tile in enumerate(joined(p, devices, received, 3, lane)[0]):
        gprec_ref[:, t * LANES : (t + 1) * LANES] = tile
        largest = jnp.maximum(largest, jnp.abs(tile))
    scale_ref[...] = splat(jnp.max(jnp.max(largest, axis=1, keepdims=True), axis=0, keepdims=True))
    elements(chunks, count_ref[0], conn_ref, high_ref, wide_ref, qw_ref, lame_ref, hot_ref, *scratch)
    acc = node_sums(scratch[2])
    work = scratch[3][...]
    own_chunks = d_ref.shape[1] // LANES
    mass = mass_rows(mass_ref)
    dots = [work]
    partial = []
    for i in range(3):
        partial.append([])
        for c in range(own_chunks):
            heavy = mass[c] * chunks[i][c]
            partial[i].append(acc[i][c] + heavy)
            dots.append(heavy * chunks[i][c])
    tiles = boundary_values(partial, bids_ref)
    higher = plus_lanes(lane)
    message = {}
    for key in keys:
        distance, parity = key
        t = 0 if distance == 1 else 1
        first = lax.rem(lax.div(p, distance), 2) == parity
        message[key] = []
        for i in range(3):
            mine, theirs = acc[i][own_chunks + t], tiles[t][i]
            upward = jnp.where(higher[t], mine, theirs)
            downward = jnp.where(higher[t], theirs, mine)
            message[key].append(jnp.where(first, upward, downward))
    message[4, 1] = [send_mixed(p, devices, a, b) for a, b in zip(message[1, 1], message[4, 1])]
    for key in keys:
        if key[0] == 16:
            send[key][...] = jnp.zeros_like(send[key])
            send[key][0:8, :] = pack_far(message[key], lane)
            continue
        for i in range(3):
            send[key][8 * i : 8 * i + 8, :] = message[key][i]
    for i in range(3):
        for t in range(2):
            here = slice(24 * t + 8 * i, 24 * t + 8 * i + 8)
            ghost_ref[here, :] = acc[i][own_chunks + t]
        for c in range(own_chunks):
            q_ref[8 * i : 8 * i + 8, c * LANES : (c + 1) * LANES] = partial[i][c]
    dot_ref[...] = splat(lane_sum(dots))


def mass_rows(mass_ref):
    count = mass_ref.shape[0] // LANES
    return [jnp.broadcast_to(mass_ref[c * LANES : (c + 1) * LANES].reshape(1, LANES), (8, LANES)) for c in range(count)]


WINDOWS = (
    (1, 1, 0, 0, 64),
    (1, -1, 0, 64, 64),
    (4, 1, 1, 0, 48),
    (4, -1, 1, 48, 48),
    (16, 1, 1, 96, 16),
    (16, -1, 1, 112, 16),
)


def second_kernel(
    keys,
    devices,
    p_ref,
    count_ref,
    qpart_ref,
    ghost_ref,
    prec_ref,
    gprec_ref,
    scale_ref,
    start_ref,
    dot_ref,
    place_ref,
    conn_ref,
    high_ref,
    wide_ref,
    qw_ref,
    lame_ref,
    hot_ref,
    mass_ref,
    *rest,
):
    received = dict(zip(keys, rest[: len(keys)]))
    q_ref, s_ref, w_ref, out_ref, *scratch = rest[len(keys) :]
    p = p_ref[0]
    own_chunks = q_ref.shape[1] // LANES
    lane = lax.broadcasted_iota(jnp.int32, (8, LANES), 1)
    swapped = [joined(p, devices, received, i, lane) for i in range(3)]
    back = [both[1] for both in swapped]
    for c in range(own_chunks):
        for i, value in enumerate(spread(back, place_ref, c)):
            here = slice(8 * i, 8 * i + 8), slice(c * LANES, (c + 1) * LANES)
            q_ref[here] = qpart_ref[here] + value
    scale = scale_ref[...]
    inverse = (1.0 / scale)[0:1, 0:1]
    ghost_q = []
    for i in range(3):
        ghost_q.append(
            [ghost_ref[24 * t + 8 * i : 24 * t + 8 * i + 8, :] + swapped[i][0][t] for t in range(2)]
        )
    chunks = []
    for i in range(3):
        value = (
            (prec_ref[i, 0:1, :] * inverse) * q_ref[0:8, :]
            + (prec_ref[i, 1:2, :] * inverse) * q_ref[8:16, :]
            + (prec_ref[i, 2:3, :] * inverse) * q_ref[16:24, :]
        )
        s_ref[8 * i : 8 * i + 8, :] = value
        chunks.append(split_lanes(value))
        for t in range(2):
            total = None
            for j in range(3):
                k = entry(i, j)
                term = (gprec_ref[k : k + 1, t * LANES : (t + 1) * LANES] * inverse) * ghost_q[j][t]
                total = term if j == 0 else total + term
            chunks[i].append(total)
    elements(chunks, count_ref[0], conn_ref, high_ref, wide_ref, qw_ref, lame_ref, hot_ref, *scratch)
    acc = node_sums(scratch[2])
    work = scratch[3][...]
    ghost = [acc[i][own_chunks:] for i in range(3)]
    mass = mass_rows(mass_ref)
    cross = []
    square = [work]
    for i in range(3):
        for c in range(own_chunks):
            here = slice(8 * i, 8 * i + 8), slice(c * LANES, (c + 1) * LANES)
            heavy = mass[c] * chunks[i][c]
            w_ref[here] = acc[i][c] + heavy
            cross.append(q_ref[here] * chunks[i][c])
            square.append(heavy * chunks[i][c])
    tail = jnp.where(lane < 120, 0.0, scale)
    for k, value in enumerate((start_ref[...], dot_ref[...], splat(lane_sum(cross)), splat(lane_sum(square)))):
        tail = jnp.where(lane == 120 + k, value, tail)

    def fill(j, unused):
        for k in range(8):
            out_ref[8 * j + k] = tail
        return unused

    lax.fori_loop(0, devices // 8, fill, 0)

    def pack(tile, column):
        packed = tail
        for i in range(3):
            shift = (40 * i - column) % LANES
            moved = pltpu.roll(ghost[i][tile], shift, 1) if shift else ghost[i][tile]
            packed = jnp.where((lane >= 40 * i) & (lane < 40 * i + 40), moved, packed)
        return packed

    for distance, sign, tile, column, width in WINDOWS:
        target = p + sign * distance
        direct = pack(tile, column)
        beyond = pack(tile, column + 40) if width > 40 else None

        @pl.when((target >= 0) & (target < devices))
        def _():
            out_ref[target] = direct
            if beyond is not None:
                out_ref[jnp.bitwise_xor(target, 1)] = beyond


def unpacked(in_ref, owner, devices, lane, inverse, direct):
    back = [[jnp.zeros((8, LANES), F32) for _ in range(2)] for _ in range(3)]
    for distance, sign, tile, column, width in WINDOWS:
        first, size = (column, min(width, 40)) if direct else (column + 40, width - 40)
        if size <= 0:
            continue
        source = owner - sign * distance
        valid = (source >= 0) & (source < devices)
        block = in_ref[jnp.clip(source, 0, devices - 1)]
        ratio = splat(block[:, 124:125]) * inverse
        inside = (lane >= first) & (lane < first + size) & valid
        for i in range(3):
            shift = (first - 40 * i) % LANES
            moved = pltpu.roll(block, shift, 1) if shift else block
            back[i][tile] = jnp.where(inside, moved * ratio, back[i][tile])
    return [back[i][t] for t in range(2) for i in range(3)]


def relay_kernel(p_ref, in_ref, out_ref):
    devices = in_ref.shape[0]
    lane = lax.broadcasted_iota(jnp.int32, (8, LANES), 1)
    owner = jnp.bitwise_xor(p_ref[0], 1)
    inverse = 1.0 / splat(in_ref[owner][:, 124:125])
    for k, block in enumerate(unpacked(in_ref, owner, devices, lane, inverse, False)):
        out_ref[8 * k : 8 * k + 8, :] = block


def scalar_kernel(p_ref, in_ref, scale_ref, out_ref):
    devices = in_ref.shape[0]
    lane = lax.broadcasted_iota(jnp.int32, (8, LANES), 1)
    mine = scale_ref[...]
    inv_mine = 1.0 / mine
    for k, block in enumerate(unpacked(in_ref, p_ref[0], devices, lane, inv_mine, True)):
        out_ref[8 * k : 8 * k + 8, :] = block

    def term(j):
        tile = in_ref[j]
        ratio = pltpu.roll(tile, LANES - 4, 1) * inv_mine
        return tile * jnp.where(lane == 122, ratio, jnp.where(lane == 123, ratio * ratio, 1.0))

    def add_up(j, sums):
        values = [term(8 * j + k) for k in range(8)]
        while len(values) > 1:
            values = [a + b for a, b in zip(values[::2], values[1::2])]
        return sums + values[0]

    sums = lax.fori_loop(0, devices // 8, add_up, jnp.zeros((8, LANES), F32), unroll=devices <= 64)
    e0, d0, cross, square = (splat(sums[:, k : k + 1]) for k in range(120, 124))
    step = e0 / d0
    scaled = step * mine
    fresh = scaled * (step * cross) - e0
    beta = fresh / e0
    more = 1.0 + beta
    bend = more * more * d0 - 2.0 * more * (scaled * cross) + scaled * (scaled * square)
    step1 = fresh / bend
    out_ref[48:56, :] = step + step1 * more
    out_ref[56:64, :] = step1 * scaled


def final_kernel(direct_ref, relayed_ref, rhs_ref, d_ref, q_ref, s_ref, wpart_ref, place_ref, x_ref, r_ref):
    lane = lax.broadcasted_iota(jnp.int32, (8, LANES), 1)
    for_d = direct_ref[48:56, :]
    for_s = direct_ref[56:64, :]
    back = [[None, None] for _ in range(3)]
    for t in range(2):
        far = lane < 0
        for _, _, tile, column, width in WINDOWS:
            if tile == t:
                far = far | ((lane >= column + 40) & (lane < column + width))
        for i in range(3):
            here = slice(24 * t + 8 * i, 24 * t + 8 * i + 8)
            back[i][t] = jnp.where(far, relayed_ref[here, :], direct_ref[here, :])
    for c in range(rhs_ref.shape[1] // LANES):
        for i, value in enumerate(spread(back, place_ref, c)):
            here = slice(8 * i, 8 * i + 8), slice(c * LANES, (c + 1) * LANES)
            x_ref[here] = for_d * d_ref[here] - for_s * s_ref[here]
            r_ref[here] = rhs_ref[here] - for_d * q_ref[here] + for_s * (wpart_ref[here] + value)


def local(
    devices,
    right_side,
    mass_diag,
    precond_blocks,
    connectivity,
    shape_grads,
    quad_weight,
    lame_moduli,
    elem_count,
    boundary_ids,
):
    own = right_side.shape[2]
    elems = connectivity.shape[1]
    p = lax.axis_index(AXIS).astype(jnp.int32).reshape(1)
    rhs = right_side.reshape(24, own)
    bids = boundary_ids.reshape(1, boundary_ids.shape[0])
    grads = jnp.transpose(shape_grads, (1, 2, 0, 3))
    vmem = pl.BlockSpec(memory_space=pltpu.VMEM)
    smem = pl.BlockSpec(memory_space=pltpu.SMEM)
    hbm = pl.BlockSpec(memory_space=pltpu.HBM)
    moves = routes(devices)
    keys = list(moves)

    def shape(*dims, dtype=F32):
        return jax.ShapeDtypeStruct(dims, dtype)

    def call(kernel, out_shape, in_specs, scratch=(), cost=None):
        return pl.pallas_call(
            kernel,
            out_shape=out_shape,
            in_specs=in_specs,
            out_specs=[vmem] * len(out_shape),
            scratch_shapes=list(scratch),
            cost_estimate=cost,
            compiler_params=pltpu.CompilerParams(vmem_limit_bytes=24 << 20),
        )

    def exchange(tiles):
        return [lax.ppermute(tiles[key], AXIS, sorted(moves[key].items())) for key in keys]

    tile = shape(32, LANES)
    row = shape(8, LANES)
    inputs = [
        pltpu.with_memory_space_constraint(value, pltpu.HBM)
        for value in (rhs, precond_blocks, bids, connectivity, grads, quad_weight, lame_moduli, mass_diag)
    ]
    *held, d, t0, t1, mixed, far = call(
        functools.partial(begin_kernel, devices, len(inputs)),
        [shape(*value.shape, dtype=value.dtype) for value in inputs] + [shape(24, own), tile, tile, tile, shape(32, LANES)],
        [smem] + [hbm] * len(inputs),
        [pltpu.VMEM((8, own), F32), pltpu.SemaphoreType.DMA((len(inputs),))],
    )(pltpu.with_memory_space_constraint(p, pltpu.SMEM), *inputs)
    rhs, precond_blocks, bids, connectivity, grads, quad_weight, lame_moduli, mass_diag = held
    kind = {1: t0, 4: t1, 16: far}
    got = exchange({key: mixed if key == (4, 1) else kind[key[0]] for key in keys})
    hot, high, wide, place, start, size = call(
        setup_kernel,
        [
            shape(10 * elems, 256, dtype=BF16),
            shape(10, elems, dtype=jnp.int32),
            shape(30, 4, elems),
            shape(1, own, dtype=jnp.int32),
            row,
            row,
        ],
        [smem] + [vmem] * 6,
        cost=pl.CostEstimate(flops=20_000_000, bytes_accessed=4_000_000, transcendentals=0),
    )(elem_count, connectivity, bids, grads, rhs, d, precond_blocks)
    mesh_args = (connectivity, high, wide, quad_weight, lame_moduli, hot, mass_diag)
    left = [
        pltpu.VMEM((24, own + boundary_ids.shape[0]), F32),
        pltpu.VMEM((192, 10 * LANES), BF16),
        pltpu.VMEM((192, 256), F32),
        pltpu.VMEM((8, LANES), F32),
    ]
    tile = shape(48, LANES)
    qpart, ghost, gprec, scale, dot, *send = call(
        functools.partial(first_kernel, keys, devices),
        [shape(24, own), tile, shape(8, 2 * LANES), row, row]
        + [shape(8 if key[0] == 16 else 24, LANES) for key in keys],
        [smem, smem] + [vmem] * (10 + len(keys)),
        left,
    )(p, elem_count, d, bids, size, *mesh_args, *got)
    got = exchange(dict(zip(keys, send)))
    q, s, wpart, message = call(
        functools.partial(second_kernel, keys, devices),
        [shape(24, own), shape(24, own), shape(24, own), shape(devices, 8, LANES)],
        [smem, smem] + [vmem] * (15 + len(keys)),
        left,
    )(p, elem_count, qpart, ghost, precond_blocks, gprec, scale, start, dot, place, *mesh_args, *got)
    message = lax.all_to_all(message, AXIS, 0, 0, tiled=True)
    (relay,) = call(relay_kernel, [tile], [smem, vmem])(p, message)
    relayed = lax.ppermute(relay, AXIS, [(i, i ^ 1) for i in range(devices)])
    (direct,) = call(
        scalar_kernel,
        [shape(64, LANES)],
        [smem] + [vmem] * 2,
        cost=pl.CostEstimate(flops=20_000_000, bytes_accessed=2_000_000, transcendentals=0),
    )(p, message, scale)
    x, r = call(final_kernel, [shape(24, own), shape(24, own)], [vmem] * 8)(
        direct, relayed, rhs, d, q, s, wpart, place
    )
    return x.reshape(3, CASES, own), r.reshape(3, CASES, own)


def solution(mesh):
    return jax.shard_map(
        functools.partial(local, mesh.shape[AXIS]),
        mesh=mesh,
        in_specs=(
            P(None, None, AXIS),
            P(AXIS),
            P(None, None, AXIS),
            P(None, AXIS),
            P(None, None, None, AXIS),
            P(None, AXIS),
            P(None, AXIS),
            P(AXIS),
            P(AXIS),
        ),
        out_specs=(P(None, None, AXIS), P(None, None, AXIS)),
        check_vma=False,
    )
```
